32 devices in a mesh: node: 32 (over z, y, x, core).
Axes of the slice: x: 2, y: 2, z: 4, core: 2. Of those that a mesh axis runs over, the one named last changes fastest.
Arguments:
- event_node: int32 [16384], P('node'), may hold values from 0 to 8191, as said below
- neighbours: int32 [16384, 10], P('node'), may hold values from 0 to 8191, as said below
- event_bucket: int32 [16384], P('node'), may hold values from 0 to 127
- neighbour_bucket: int32 [16384, 10], P('node'), may hold values from 0 to 127
- edge_features: bfloat16 [16384, 128], P('node'), may hold values from -6 to 6
- affinity: float32 [16384, 10], P('node'), may hold values from -320 to 320
- upstream: bfloat16 [16384, 512], P('node'), may hold values from -6 to 6
- node_memory: bfloat16 [8192, 512], P('node'), may hold values from -4 to 4
- edge_weight: bfloat16 [128, 512], replicated, may hold values from -0.5 to 0.5
- time_message: float32 [128, 512], replicated, may hold values from -6 to 6
- input_weight: bfloat16 [512, 1536], replicated, may hold values from -0.25 to 0.25
- hidden_weight: bfloat16 [512, 1536], replicated, may hold values from -0.25 to 0.25
- gate_bias: float32 [1536], replicated, may hold values from -6 to 6
- time_key: float32 [128, 512], replicated, may hold values from -6 to 6
- query_weight: bfloat16 [512, 512], replicated, may hold values from -0.25 to 0.25
- key_weight: bfloat16 [512, 512], replicated, may hold values from -0.25 to 0.25
- value_weight: bfloat16 [512, 512], replicated, may hold values from -0.25 to 0.25
- out_weight: bfloat16 [512, 512], replicated, may hold values from -0.25 to 0.25
Outputs:
- embedding: bfloat16 [16384, 512], P('node')
- new_memory: bfloat16 [8192, 512], P('node')
- grad_query: float32 [512, 512], replicated
- grad_key: float32 [512, 512], replicated
- grad_value: float32 [512, 512], replicated
- grad_out: float32 [512, 512], replicated
The draws below stay inside these ranges and needn't reach their ends.
Inputs may be any that keep to these rules, and one draw needn't show every extreme that they name: `event_node`: node i belongs to index i // 256 of node. Of the 512 rows of one device, at most 48 name nodes of one index; in every draw one index receives exactly 48 of them from every device. `neighbours`: node i belongs to index i // 256 of node. Of the 5120 entries of one device's rows, at most 320 name nodes of one index, and these name at most 64 distinct nodes; in every draw one index receives exactly 320 entries naming exactly 64 distinct nodes from every device.
All inputs are finite; a program needn't handle non-finite values.
Results may differ from the reference program's by a relative error of at most 0.012.
Values may be sent and summed in bfloat16 or wider, within the bound.
A program may use at most 192 MiB of HBM per device.

```python
import math
import jax
import jax.numpy as jnp
from jax import lax

MEM = 512
MSG = 512
EDGE = 128
HEADS = 2
NEIGH = 10
TBUCK = 128
CAPU = 64
EV_DEV = 512
NODE_DEV = 256
EVENTS = 16384
NODES = 8192
CAPM = 48
CAPN = 320
N_NODE = 32


def packed_owners(device_key, amount, capacity, hottest):
    slots_all = N_NODE * capacity
    slot_ids = jnp.arange(slots_all, dtype=jnp.int32)
    owners = slot_ids // capacity
    within = slot_ids % capacity
    priority = jax.random.permutation(jax.random.fold_in(device_key, 1), slots_all).astype(jnp.int32) + 1
    priority = jnp.where(owners == hottest, 0, priority)
    ordered = jnp.argsort(priority, stable=True)[:amount]
    shuffled = ordered[jax.random.permutation(jax.random.fold_in(device_key, 2), amount)]
    return (owners[shuffled], within[shuffled])


def draw_event_node(key, part):
    hottest = jax.random.randint(jax.random.fold_in(key, 11), (), 0, N_NODE)

    def device(number):
        device_key = jax.random.fold_in(jax.random.fold_in(key, 12), number)
        owners, within = packed_owners(device_key, EV_DEV, CAPM, hottest)
        local_rows = jax.random.randint(jax.random.fold_in(device_key, 3), (EV_DEV,), 0, NODE_DEV)
        return owners * NODE_DEV + local_rows
    return jax.vmap(device)(jnp.arange(N_NODE, dtype=jnp.int32)).reshape(-1).astype(jnp.int32)


def draw_neighbours(key, part):
    hottest = jax.random.randint(jax.random.fold_in(key, 21), (), 0, N_NODE)

    def device(number):
        device_key = jax.random.fold_in(jax.random.fold_in(key, 22), number)
        owners, within = packed_owners(device_key, EV_DEV * NEIGH, CAPN, hottest)

        def pool_of(owner_id):
            return jax.random.permutation(jax.random.fold_in(device_key, 1000 + owner_id), NODE_DEV)[:CAPU]
        pools = jax.vmap(pool_of)(jnp.arange(N_NODE, dtype=jnp.int32))
        local_rows = pools[owners, within % CAPU]
        return (owners * NODE_DEV + local_rows).reshape(EV_DEV, NEIGH)
    whole = jax.vmap(device)(jnp.arange(N_NODE, dtype=jnp.int32))
    return whole.reshape(EV_DEV * N_NODE, NEIGH).astype(jnp.int32)


def draw_affinity(key, part):
    rows_all = EV_DEV * N_NODE
    return jax.random.normal(jax.random.fold_in(key, 1), (rows_all, NEIGH), jnp.float32)


def touch_ends(entries, stream_key, smallest, high):
    spot = [jax.random.randint(jax.random.fold_in(stream_key, axis), (), 0, length) for axis, length in enumerate(entries.shape)]
    longest = entries.shape.index(max(entries.shape))
    beside = spot[:longest] + [(spot[longest] + 1) % entries.shape[longest]] + spot[longest + 1:]
    return entries.at[tuple(spot)].set(smallest).at[tuple(beside)].set(high)


def block_scale(rng, shape, split, least, high):
    level, own = 1.0, jax.random.fold_in(rng, 6)
    for dim, shards_of in split:
        draws = jnp.exp(jax.random.uniform(jax.random.fold_in(own, dim), (shards_of,), jnp.float32, least / len(split), high / len(split)))
        level = level * jnp.repeat(draws, shape[dim] // shards_of).reshape([-1 if axis == dim else 1 for axis in range(len(shape))])
    return level


def scatter_about(rng, extent, width, reach, shards=(), kind=jnp.bfloat16):
    drawn = jax.random.normal(rng, extent, jnp.float32) * width
    if len(shards) > 0:
        drawn = block_scale(rng, extent, shards, -0.22, 0.18) * drawn
    return jnp.clip(drawn, min=-reach, max=reach).astype(kind)


def setup_inputs(seed: int = 0) -> dict:
    seeds = jax.random.split(jax.random.key(seed), 19)
    event_node = draw_event_node(jax.random.fold_in(seeds[18], 71), 0)
    neighbours = draw_neighbours(jax.random.fold_in(seeds[18], 71), 0)
    event_bucket = touch_ends(jax.random.randint(seeds[2], (EVENTS,), 0, TBUCK), jax.random.fold_in(seeds[2], 1), 0, TBUCK - 1).astype(jnp.int32)
    neighbour_bucket = touch_ends(jax.random.randint(seeds[3], (EVENTS, NEIGH), 0, TBUCK), jax.random.fold_in(seeds[3], 1), 0, TBUCK - 1).astype(jnp.int32)
    edge_features = scatter_about(seeds[4], (EVENTS, EDGE), 1.0, 6.0, ((0, 32),))
    affinity = draw_affinity(jax.random.fold_in(seeds[18], 71), 0)
    upstream = scatter_about(seeds[6], (EVENTS, MEM), 1.0, 6.0, ((0, 32),))
    node_memory = scatter_about(seeds[7], (NODES, MEM), 1.0, 4.0, ((0, 32),))
    edge_weight = scatter_about(seeds[8], (EDGE, MSG), EDGE ** -0.5, 0.5)
    time_message = scatter_about(seeds[9], (TBUCK, MSG), 1.0, 6.0, (), jnp.float32)
    input_weight = scatter_about(seeds[10], (MSG, 3 * MEM), MSG ** -0.5, 0.25)
    hidden_weight = scatter_about(seeds[11], (MEM, 3 * MEM), MEM ** -0.5, 0.25)
    gate_bias = scatter_about(seeds[12], (3 * MEM,), 1.0, 6.0, (), jnp.float32)
    time_key = scatter_about(seeds[13], (TBUCK, MEM), 1.0, 6.0, (), jnp.float32)
    query_weight = scatter_about(seeds[14], (MEM, MEM), MEM ** -0.5, 0.25)
    key_weight = scatter_about(seeds[15], (MEM, MEM), MEM ** -0.5, 0.25)
    value_weight = scatter_about(seeds[16], (MEM, MEM), MEM ** -0.5, 0.25)
    out_weight = scatter_about(seeds[17], (MEM, MEM), MEM ** -0.5, 0.25)
    return {"event_node": event_node, "neighbours": neighbours, "event_bucket": event_bucket, "neighbour_bucket": neighbour_bucket, "edge_features": edge_features, "affinity": affinity, "upstream": upstream, "node_memory": node_memory, "edge_weight": edge_weight, "time_message": time_message, "input_weight": input_weight, "hidden_weight": hidden_weight, "gate_bias": gate_bias, "time_key": time_key, "query_weight": query_weight, "key_weight": key_weight, "value_weight": value_weight, "out_weight": out_weight}


def make_message(edge_rows, buckets, edge_weight, time_message):
    before = jnp.dot(edge_rows, edge_weight, preferred_element_type=jnp.float32) + jnp.take(time_message, buckets, axis=0)
    return jax.nn.silu(before).astype(jnp.bfloat16)

def gru_rows(aggregate, previous, input_weight, hidden_weight, gate_bias):
    columns = previous.shape[1]
    inputs = jnp.dot(aggregate, input_weight, preferred_element_type=jnp.float32) + gate_bias
    hidden = jnp.dot(previous, hidden_weight, preferred_element_type=jnp.float32)
    update = jax.nn.sigmoid(inputs[:, :columns] + hidden[:, :columns])
    resets = jax.nn.sigmoid(inputs[:, columns:2 * columns] + hidden[:, columns:2 * columns])
    candidate = jnp.tanh(inputs[:, 2 * columns:] + resets * hidden[:, 2 * columns:])
    return (1.0 - update) * candidate + update * previous.astype(jnp.float32)

def attend(target, neighbour_rows, neighbour_bucket, affinity, time_key, query_weight, key_weight, value_weight, out_weight):
    events, fanout, columns = neighbour_rows.shape
    head_size = columns // HEADS
    query = jnp.dot(target, query_weight, preferred_element_type=jnp.float32).astype(jnp.bfloat16).reshape(events, HEADS, head_size)
    flat_rows = neighbour_rows.reshape(events * fanout, columns)
    key_rows = jnp.dot(flat_rows, key_weight, preferred_element_type=jnp.float32) + jnp.take(time_key, neighbour_bucket.reshape(-1), axis=0)
    key_rows = key_rows.astype(jnp.bfloat16).reshape(events, fanout, HEADS, head_size)
    value_rows = jnp.dot(flat_rows, value_weight, preferred_element_type=jnp.float32).astype(jnp.bfloat16).reshape(events, fanout, HEADS, head_size)
    scores = jnp.einsum('ehd,enhd->ehn', query.astype(jnp.float32), key_rows.astype(jnp.float32)) / math.sqrt(head_size)
    scores = scores + affinity[:, None, :]
    probs = jax.nn.softmax(scores, axis=-1).astype(jnp.bfloat16)
    mixed = jnp.einsum('ehn,enhd->ehd', probs.astype(jnp.float32), value_rows.astype(jnp.float32))
    mixed = mixed.astype(jnp.bfloat16).reshape(events, columns)
    return (jnp.dot(mixed, out_weight, preferred_element_type=jnp.float32) + target.astype(jnp.float32)).astype(jnp.bfloat16)

def reference(event_node, neighbours, event_bucket, neighbour_bucket, edge_features, affinity, upstream, node_memory, edge_weight, time_message, input_weight, hidden_weight, gate_bias, time_key, query_weight, key_weight, value_weight, out_weight):
    messages = make_message(edge_features, event_bucket, edge_weight, time_message)
    totals = jax.ops.segment_sum(messages.astype(jnp.float32), event_node, num_segments=NODES)
    counts = jax.ops.segment_sum(jnp.ones(event_node.shape, jnp.float32), event_node, num_segments=NODES)
    aggregate = (totals / jnp.maximum(counts, 1.0)[:, None]).astype(jnp.bfloat16)
    updated = gru_rows(aggregate, node_memory, input_weight, hidden_weight, gate_bias)
    new_memory = jnp.where(counts[:, None] > 0, updated, node_memory.astype(jnp.float32)).astype(jnp.bfloat16)

    def block(carry, number):
        start = number * EV_DEV
        targets = lax.dynamic_slice_in_dim(event_node, start, EV_DEV)
        nearby = lax.dynamic_slice_in_dim(neighbours, start, EV_DEV)
        buckets = lax.dynamic_slice_in_dim(neighbour_bucket, start, EV_DEV)
        logits = lax.dynamic_slice_in_dim(affinity, start, EV_DEV)
        tangent = lax.dynamic_slice_in_dim(upstream, start, EV_DEV)
        target_rows = jnp.take(new_memory, targets, axis=0)
        nearby_rows = jnp.take(new_memory, nearby.reshape(-1), axis=0).reshape(EV_DEV, NEIGH, MEM)

        def forward(weight_q, weight_k, weight_v, weight_o):
            return attend(target_rows, nearby_rows, buckets, logits, time_key, weight_q, weight_k, weight_v, weight_o)
        result, pullback = jax.vjp(forward, query_weight, key_weight, value_weight, out_weight)
        grads = pullback(tangent)
        carry = tuple((total + grad.astype(jnp.float32) for total, grad in zip(carry, grads)))
        return (carry, result)
    zeros_start = tuple((jnp.zeros((MEM, MEM), jnp.float32) for _ in range(4)))
    summed, blocks = lax.scan(block, zeros_start, jnp.arange(N_NODE, dtype=jnp.int32))
    embedding = blocks.reshape(EVENTS, MEM)
    factor = 1.0 / math.sqrt(EVENTS)
    return (embedding, new_memory, summed[0] * factor, summed[1] * factor, summed[2] * factor, summed[3] * factor)
```

```python
import functools
import math

import jax
import jax.numpy as jnp
from jax import lax
from jax.experimental import pallas as pl
from jax.experimental.pallas import tpu as pltpu
from jax.sharding import PartitionSpec as P

HEADS = 2
LANES = 128
GROUP = 32
BF = jnp.bfloat16
F32 = jnp.float32
VMEM_LIMIT = 60 * 1024 * 1024
RESIDENT_LIMIT = 20 * 1024 * 1024
NT = (((1,), (1,)), ((), ()))
TN = (((0,), (0,)), ((), ()))


def mm(a, b):
    return jnp.dot(a, b, preferred_element_type=F32)


def mm_nt(a, b):
    return lax.dot_general(a, b, NT, preferred_element_type=F32)


def mm_tn(a, b):
    return lax.dot_general(a, b, TN, preferred_element_type=F32)


def halves(table):
    high = table.astype(BF)
    low = (table - high.astype(F32)).astype(BF)
    return high, low


def pack_kernel(devices, slots, feats, meta, owners, outgoing, sel):
    events = feats.shape[0]
    ids = lax.broadcasted_iota(jnp.int32, (devices, events), 0)
    theirs = ids == owners[...]
    before = lax.broadcasted_iota(jnp.int32, (events, events), 0) < lax.broadcasted_iota(
        jnp.int32, (events, events), 1
    )
    rank = mm(theirs.astype(F32).astype(BF), before.astype(F32).astype(BF))
    sel[...] = jnp.where(theirs, rank, -1.0)
    slot_ids = lax.broadcasted_iota(jnp.int32, (slots, events), 0).astype(F32)
    lane_ids = lax.broadcasted_iota(jnp.int32, (LANES, events), 0).astype(F32)

    def pick(step, carry):
        for part in range(4):
            device = step * 4 + part
            row = sel[pl.ds(device, 1), :]
            hits = (slot_ids == row).astype(F32).astype(BF)
            outgoing[device, :slots, :] = mm(hits, feats[...]).astype(BF)
            turned = (lane_ids == row).astype(F32).astype(BF)
            outgoing[device, slots:, :] = mm_nt(meta[...], turned).astype(BF)
        return carry

    lax.fori_loop(0, devices // 4, pick, 0)


def exchange_kernel(devices, outgoing, inbox, send_sems, recv_sems, own_sem):
    me = lax.axis_index("node")
    barrier = pltpu.get_barrier_semaphore()

    def greet(step, carry):
        pl.semaphore_signal(
            barrier,
            inc=1,
            device_id=(lax.rem(me + step, devices),),
            device_id_type=pl.DeviceIdType.MESH,
        )
        return carry

    lax.fori_loop(1, devices, greet, 0)
    pl.semaphore_wait(barrier, devices - 1)

    def send(step):
        peer = lax.rem(me + step, devices)
        return pltpu.make_async_remote_copy(
            src_ref=outgoing.at[peer],
            dst_ref=inbox.at[me],
            send_sem=send_sems.at[peer],
            recv_sem=recv_sems.at[me],
            device_id=(peer,),
            device_id_type=pl.DeviceIdType.MESH,
        )

    def receive(step):
        peer = lax.rem(me + step, devices)
        return pltpu.make_async_remote_copy(
            src_ref=outgoing.at[peer],
            dst_ref=inbox.at[peer],
            send_sem=send_sems.at[peer],
            recv_sem=recv_sems.at[peer],
            device_id=(peer,),
            device_id_type=pl.DeviceIdType.MESH,
        )

    def start(step, carry):
        send(step).start()
        return carry

    def finish(step, carry):
        receive(step).wait_recv()
        send(step).wait_send()
        return carry

    lax.fori_loop(1, devices, start, 0)
    own = pltpu.make_async_copy(outgoing.at[me], inbox.at[me], own_sem)
    own.start()
    own.wait()
    lax.fori_loop(1, devices, finish, 0)


def reduce_kernel(
    line,
    side,
    strands,
    factor,
    grads,
    result,
    near,
    pair,
    first_land,
    first_sum,
    second_land,
    second_sum,
    line_land,
    pair_send,
    pair_recv,
    first_send,
    first_recv,
    second_send,
    second_recv,
    line_send,
    line_recv,
    line_back_send,
    line_back_recv,
    second_back_send,
    second_back_recv,
    first_back_send,
    first_back_recv,
    hop_send,
    hop_recv,
):
    me = lax.axis_index("node")
    core = lax.rem(me, 2)
    chip = me // 2
    partner = me + 1 - 2 * core
    low, mid, far = lax.rem(chip, side), lax.rem(chip // side, side), chip // (side * side)
    first = (1 - core) * low + core * mid
    second = (1 - core) * mid + core * low
    first_stride = 2 * (1 + core * (side - 1))
    second_stride = 2 * (side - core * (side - 1))
    half = grads.shape[0] // 2
    rows = half // strands
    rows_a = rows // side
    rows_b = rows_a // side
    rows_z = rows_b // line
    mesh_id = pl.DeviceIdType.MESH

    firsts = [lax.rem(first + step, side) for step in range(1, side)]
    seconds = [lax.rem(second + step, side) for step in range(1, side)]
    fars = [lax.rem(far + step, line) for step in range(1, line)]

    def first_device(place):
        return me + (place - first) * first_stride

    def second_device(place):
        return me + (place - second) * second_stride

    def far_device(place):
        return me + (place - far) * (2 * side * side)

    everyone = (
        [partner]
        + [first_device(place) for place in firsts]
        + [second_device(place) for place in seconds]
        + [far_device(place) for place in fars]
    )
    barrier = pltpu.get_barrier_semaphore()
    for device in everyone:
        pl.semaphore_signal(barrier, inc=1, device_id=(device,), device_id_type=mesh_id)
    pl.semaphore_wait(barrier, len(everyone))

    def span(start, size):
        return pl.ds(pl.multiple_of(start, 16), size)

    def remote(src, dst, send, recv, device):
        return pltpu.make_async_remote_copy(
            src_ref=src,
            dst_ref=dst,
            send_sem=send,
            recv_sem=recv,
            device_id=(device,),
            device_id_type=mesh_id,
        )

    def swap(s):
        return remote(
            grads.at[span((1 - core) * half + s * rows, rows)],
            near.at[span(s * rows, rows)],
            pair_send.at[s],
            pair_recv.at[s],
            partner,
        )

    def to_first(s, place, source):
        return remote(
            pair.at[span(s * rows + place * rows_a, rows_a)],
            first_land.at[span(s * rows + source * rows_a, rows_a)],
            first_send.at[s, place],
            first_recv.at[s, source],
            first_device(place),
        )

    def to_second(s, place, source):
        return remote(
            first_sum.at[span(s * rows_a + place * rows_b, rows_b)],
            second_land.at[span(s * rows_a + source * rows_b, rows_b)],
            second_send.at[s, place],
            second_recv.at[s, source],
            second_device(place),
        )

    def to_far(s, place, source):
        return remote(
            second_sum.at[span(s * rows_b + place * rows_z, rows_z)],
            line_land.at[span(s * rows_b + source * rows_z, rows_z)],
            line_send.at[s, place],
            line_recv.at[s, source],
            far_device(place),
        )

    def place_of(which, s, a, b=0, f=0):
        return which * half + s * rows + a * rows_a + b * rows_b + f * rows_z

    def spread(at, send, recv, device):
        return remote(result.at[at], result.at[at], send, recv, device)

    def back_far(s, place, source):
        at = span(place_of(core, s, first, second, source), rows_z)
        return spread(at, line_back_send.at[s, place], line_back_recv.at[s, source], far_device(place))

    def back_second(s, place, source):
        at = span(place_of(core, s, first, source), rows_b)
        return spread(
            at, second_back_send.at[s, place], second_back_recv.at[s, source], second_device(place)
        )

    def back_first(s, place, source):
        at = span(place_of(core, s, source), rows_a)
        return spread(
            at, first_back_send.at[s, place], first_back_recv.at[s, source], first_device(place)
        )

    def hop(s, source, which):
        at = span(place_of(which, s, source), rows_a)
        return spread(at, hop_send.at[s, source], hop_recv.at[s, source], partner)

    started = []

    def start(made):
        made.start()
        started.append(made)

    def stage_pair(s):
        swap(s).wait_recv()
        at = span(s * rows, rows)
        own = grads[span(core * half + s * rows, rows), :]
        pair[at, :] = (own.astype(F32) + near[at, :].astype(F32)).astype(BF)
        for place in firsts:
            start(to_first(s, place, first))

    def stage_first(s):
        total = pair[span(s * rows + first * rows_a, rows_a), :].astype(F32)
        for place in firsts:
            to_first(s, place, place).wait_recv()
            total += first_land[span(s * rows + place * rows_a, rows_a), :].astype(F32)
        first_sum[span(s * rows_a, rows_a), :] = total.astype(BF)
        for place in seconds:
            start(to_second(s, place, second))

    def stage_second(s):
        total = first_sum[span(s * rows_a + second * rows_b, rows_b), :].astype(F32)
        for place in seconds:
            to_second(s, place, place).wait_recv()
            total += second_land[span(s * rows_a + place * rows_b, rows_b), :].astype(F32)
        second_sum[span(s * rows_b, rows_b), :] = total.astype(BF)
        for place in fars:
            start(to_far(s, place, far))

    def stage_line(s):
        total = second_sum[span(s * rows_b + far * rows_z, rows_z), :].astype(F32)
        for place in fars:
            to_far(s, place, place).wait_recv()
            total += line_land[span(s * rows_b + place * rows_z, rows_z), :].astype(F32)
        result[span(place_of(core, s, first, second, far), rows_z), :] = (total * factor).astype(BF)
        for place in fars:
            start(back_far(s, place, far))

    def stage_back_line(s):
        for place in fars:
            back_far(s, place, place).wait_recv()
        for place in seconds:
            start(back_second(s, place, second))

    def stage_back_second(s):
        for place in seconds:
            back_second(s, place, place).wait_recv()
        for place in firsts:
            start(back_first(s, place, first))
        start(hop(s, first, core))

    def stage_back_first(s):
        for place in firsts:
            back_first(s, place, place).wait_recv()
            start(hop(s, place, core))

    for s in range(strands):
        start(swap(s))
    for s in range(strands):
        stage_pair(s)
    stages = [
        stage_first,
        stage_second,
        stage_line,
        stage_back_line,
        stage_back_second,
        stage_back_first,
    ]
    for step in range(strands + len(stages) - 1):
        for number, stage in enumerate(stages):
            if 0 <= step - number < strands:
                stage(step - number)
    for s in range(strands):
        for place in [first] + firsts:
            hop(s, place, 1 - core).wait_recv()
    for made in started:
        made.wait_send()


def memory_kernel(
    devices,
    slots,
    chunk,
    inbox,
    memory,
    edge_weight,
    time_message,
    input_weight,
    hidden_weight,
    gate_bias,
    out_memory,
    out_table,
    picked,
    picked_meta,
    totals,
    counts,
    wide,
):
    rows = memory.shape[0]
    columns = memory.shape[1]
    stride = columns // LANES
    turn = (
        lax.broadcasted_iota(jnp.int32, (slots, LANES), 0)
        == lax.broadcasted_iota(jnp.int32, (slots, LANES), 1)
    ).astype(F32).astype(BF)

    def pick(step, carry):
        for part in range(4):
            source = step * 4 + part
            at = pl.ds(pl.multiple_of(source * slots, slots), slots)
            picked[at, :] = inbox[source, :slots, :]
            picked_meta[at, :] = mm_nt(turn, inbox[source, slots:, :])
        return carry

    lax.fori_loop(0, devices // 4, pick, 0)
    totals[...] = jnp.zeros_like(totals)
    counts[...] = jnp.zeros_like(counts)
    high, low = halves(time_message[...])
    weight = edge_weight[...]

    def add(step, carry):
        at = pl.ds(pl.multiple_of(step * chunk, chunk), chunk)
        info = picked_meta[at, :]
        node, bucket, valid = info[:, 0:1], info[:, 1:2], info[:, 2:3]
        lanes = lax.broadcasted_iota(jnp.int32, (chunk, high.shape[0]), 1).astype(F32)
        picks = (lanes == bucket).astype(F32).astype(BF)
        pre = mm(picked[at, :], weight) + mm(picks, high) + mm(picks, low)
        message = (pre / (1.0 + jnp.exp(-pre))).astype(BF)
        ids = lax.broadcasted_iota(jnp.int32, (chunk, rows), 1).astype(F32)
        hot = jnp.where(ids == node, valid, 0.0).astype(BF)
        totals[...] += mm_tn(hot, message)
        counts[...] += mm_tn(hot, jnp.ones((chunk, LANES), BF))
        return carry

    lax.fori_loop(0, devices * slots // chunk, add, 0)
    count = counts[:, 0:1]
    aggregate = (totals[...] / jnp.maximum(count, 1.0)).astype(BF)
    previous = memory[...]

    def gate(which):
        cut = slice(which * columns, (which + 1) * columns)
        return (
            mm(aggregate, input_weight[:, cut]) + gate_bias[:, cut],
            mm(previous, hidden_weight[:, cut]),
        )

    from_input, from_hidden = gate(0)
    update = jax.nn.sigmoid(from_input + from_hidden)
    from_input, from_hidden = gate(1)
    resets = jax.nn.sigmoid(from_input + from_hidden)
    from_input, from_hidden = gate(2)
    candidate = jnp.tanh(from_input + resets * from_hidden)
    old = previous.astype(F32)
    fresh = (1.0 - update) * candidate + update * old
    fresh = jnp.where(count > 0, fresh, old)
    out_memory[...] = fresh.astype(BF)
    for part in range(stride):
        wide[pl.ds(part, rows, stride=stride), :] = fresh[:, part * LANES : (part + 1) * LANES]
    out_table[...] = wide[...].astype(BF)


def gather_kernel(
    line,
    side,
    subs,
    own,
    whole,
    recv,
    hop_recv,
    line_send,
    first_send,
    second_send,
    hop_send,
    own_sem,
):
    me = lax.axis_index("node")
    core = lax.rem(me, 2)
    chip = me // 2
    partner = me + 1 - 2 * core
    low, mid, far = lax.rem(chip, side), lax.rem(chip // side, side), chip // (side * side)
    first = (1 - core) * low + core * mid
    second = (1 - core) * mid + core * low
    first_stride = 1 + core * (side - 1)
    second_stride = side - core * (side - 1)
    rows = own.shape[0]
    size = rows // subs
    mesh_id = pl.DeviceIdType.MESH

    def chip_of(along, over, across):
        return (
            lax.rem(far + line - along, line) * side * side
            + lax.rem(first + side - over, side) * first_stride
            + lax.rem(second + side - across, side) * second_stride
        )

    peers = [2 * chip_of(line - step, 0, 0) + core for step in range(1, line)]
    first_peers = [2 * chip_of(0, side - step, 0) + core for step in range(1, side)]
    second_peers = [2 * chip_of(0, 0, side - step) + core for step in range(1, side)]
    everyone = peers + first_peers + second_peers + [partner]
    barrier = pltpu.get_barrier_semaphore()
    for device in everyone:
        pl.semaphore_signal(barrier, inc=1, device_id=(device,), device_id_type=mesh_id)
    pl.semaphore_wait(barrier, len(everyone))

    def at(source, part, kind):
        return pl.ds(pl.multiple_of((2 * source + kind) * rows + part * size, 16), size)

    def copy(source, part, mine, send_sem, device):
        src = own.at[pl.ds(part * size, size)] if mine else whole.at[at(source, part, core)]
        return pltpu.make_async_remote_copy(
            src_ref=src,
            dst_ref=whole.at[at(source, part, core)],
            send_sem=send_sem,
            recv_sem=recv.at[source * subs + part],
            device_id=(device,),
            device_id_type=mesh_id,
        )

    def hop(source, part, mine, kind):
        src = own.at[pl.ds(part * size, size)] if mine else whole.at[at(source, part, kind)]
        return pltpu.make_async_remote_copy(
            src_ref=src,
            dst_ref=whole.at[at(source, part, kind)],
            send_sem=hop_send.at[source * subs + part],
            recv_sem=hop_recv.at[source * subs + part],
            device_id=(partner,),
            device_id_type=mesh_id,
        )

    started = []

    def start(made):
        made.start()
        started.append(made)

    def landed(source, part):
        copy(source, part, False, hop_send.at[0], partner).wait_recv()

    stay = pltpu.make_async_copy(own, whole.at[pl.ds(pl.multiple_of(me * rows, 16), rows)], own_sem)
    stay.start()
    steps = line * subs
    for step in range(steps + 2):
        if step < steps:
            along, part = divmod(step, subs)
            source = chip_of(along, 0, 0)
            mine = along == 0
            if not mine:
                landed(source, part)
            for to, device in enumerate(first_peers):
                start(copy(source, part, mine, first_send.at[step, to], device))
            if mine:
                for to, device in enumerate(peers):
                    start(copy(source, part, mine, line_send.at[part, to], device))
            for to, device in enumerate(second_peers):
                start(copy(source, part, mine, second_send.at[step, 0, to], device))
            start(hop(source, part, mine, core))
        if 0 <= step - 1 < steps:
            along, part = divmod(step - 1, subs)
            for over in range(1, side):
                source = chip_of(along, over, 0)
                landed(source, part)
                for to, device in enumerate(second_peers):
                    start(copy(source, part, False, second_send.at[step - 1, over, to], device))
                start(hop(source, part, False, core))
        if 0 <= step - 2 < steps:
            along, part = divmod(step - 2, subs)
            for across in range(1, side):
                for over in range(side):
                    source = chip_of(along, over, across)
                    landed(source, part)
                    start(hop(source, part, False, core))
    stay.wait()
    for made in started:
        made.wait_send()

    def drain(source, carry):
        for part in range(subs):
            hop(source, part, False, 1 - core).wait_recv()
        return carry

    lax.fori_loop(0, line * side * side, drain, 0)


def event_kernel(
    resident,
    events,
    fanout,
    ids,
    source,
    buckets,
    affinity,
    upstream,
    time_key,
    query_weight,
    key_weight,
    value_weight,
    out_weight,
    embedding,
    grads,
    *scratch,
):
    columns = upstream.shape[1]
    head = columns // HEADS
    stride = columns // LANES
    if resident:
        landing, table, near, sems, *scratch = scratch
        parts = sems.shape[0]
        size = landing.shape[0] // parts
        copies = []
        for part in range(parts):
            at = pl.ds(part * size, size)
            copies.append(pltpu.make_async_copy(source.at[at], landing.at[at], sems.at[part]))
            copies[-1].start()
    else:
        near, sem, *scratch = scratch
        picks = (fanout + 1) * events

        def request(row, carry):
            pltpu.make_async_copy(
                source.at[pl.ds(pl.multiple_of(ids[row], stride), stride)],
                near.at[pl.ds(pl.multiple_of(row * stride, stride), stride)],
                sem,
            ).start()
            return carry

        lax.fori_loop(0, picks, request, 0)
    target, query, back, pull, mix, hits, tq = scratch
    heads = [slice(h * head, (h + 1) * head) for h in range(HEADS)]
    high, low = halves(time_key[...])

    back[...] = mm_nt(upstream[...], out_weight[...]).astype(BF)
    for h, cut in enumerate(heads):
        pull[HEADS + h] = mm_nt(back[:, cut], value_weight[:, cut])

    if resident:
        step_rows = 256
        for part in range(parts):
            copies[part].wait()

            def widen(step, carry, part=part):
                at = pl.ds(pl.multiple_of(part * size + step * step_rows, step_rows), step_rows)
                table[at, :] = landing[at, :].astype(F32)
                return carry

            lax.fori_loop(0, size // step_rows, widen, 0)

        unroll = 16

        def fetch(step, carry):
            for lane in range(unroll):
                row = step * unroll + lane
                start = pl.multiple_of(ids[row], stride)
                near[pl.ds(pl.multiple_of(row * stride, stride), stride), :] = table[
                    pl.ds(start, stride), :
                ]
            return carry

        lax.fori_loop(0, (fanout + 1) * events // unroll, fetch, 0)
    else:
        pltpu.make_async_copy(source.at[pl.ds(0, picks * stride)], near, sem).wait()

    for part in range(stride):
        target[:, part * LANES : (part + 1) * LANES] = near[
            pl.ds(fanout * events * stride + part, events, stride=stride), :
        ].astype(BF)
    query[...] = mm(target[...], query_weight[...]).astype(BF)
    for h, cut in enumerate(heads):
        pull[h] = mm_nt(query[:, cut], key_weight[:, cut])
        tq[h] = mm_nt(query[:, cut], high[:, cut]) + mm_nt(query[:, cut], low[:, cut])

    size = 32
    scale = 1.0 / math.sqrt(head)
    lane = lax.broadcasted_iota(jnp.int32, (size, LANES), 1)
    masks = [(lane >= h * GROUP) & (lane < h * GROUP + fanout) for h in range(HEADS)]

    def per_head(values, op, fill):
        out = jnp.zeros((size, LANES), F32)
        for mask in masks:
            out = jnp.where(
                mask, op(jnp.where(mask, values, fill), axis=1, keepdims=True), out
            )
        return out

    def block(step, carry):
        first = pl.multiple_of(step * size, size)
        at = pl.ds(first, size)
        names = buckets[at, :]

        def rows_of(j, part):
            return near[pl.ds((j * events + first) * stride + part, size, stride=stride), :]

        raw = jnp.zeros((size, LANES), F32)
        for j in range(fanout):
            same = lane == names[:, j : j + 1]
            nearby = [rows_of(j, part) for part in range(stride)]
            for k in range(2 * HEADS):
                total = nearby[0] * pull[k, at, 0:LANES]
                for part in range(1, stride):
                    total += nearby[part] * pull[k, at, part * LANES : (part + 1) * LANES]
                if k < HEADS:
                    total += jnp.where(same, tq[k, at, :], 0.0)
                raw = jnp.where(
                    lane == k * GROUP + j, jnp.sum(total, axis=1, keepdims=True), raw
                )
        scores = raw * scale + affinity[at, :]
        active = masks[0]
        for mask in masks[1:]:
            active = active | mask
        top = per_head(scores, jnp.max, -3.0e38)
        raised = jnp.where(active, jnp.exp(jnp.where(active, scores - top, 0.0)), 0.0)
        below = per_head(raised, jnp.sum, 0.0)
        probs = jnp.where(active, raised / jnp.where(active, below, 1.0), 0.0)
        turned = pltpu.roll(raw, HEADS * GROUP, axis=1).astype(BF).astype(F32)
        slopes = jnp.where(active, turned, 0.0)
        inner = per_head(probs * slopes, jnp.sum, 0.0)
        slopes = probs * (slopes - inner) * scale
        blend = jnp.where(
            active, probs.astype(BF).astype(F32), pltpu.roll(slopes, HEADS * GROUP, axis=1)
        )
        spread = [
            [
                jnp.broadcast_to(blend[:, k * GROUP + j : k * GROUP + j + 1], (size, LANES))
                for j in range(fanout)
            ]
            for k in range(2 * HEADS)
        ]
        for h in range(HEADS):
            total = jnp.zeros((size, LANES), F32)
            for j in range(fanout):
                total += jnp.where(lane == names[:, j : j + 1], spread[HEADS + h][j], 0.0)
            hits[h, at, :] = total.astype(BF)
        for part in range(stride):
            sums = [jnp.zeros((size, LANES), F32) for _ in range(2 * HEADS)]
            for j in range(fanout):
                nearby = rows_of(j, part)
                for k in range(2 * HEADS):
                    sums[k] += spread[k][j] * nearby
            for k in range(2 * HEADS):
                mix[k, at, part * LANES : (part + 1) * LANES] = sums[k].astype(BF)
        return carry

    lax.fori_loop(0, events // size, block, 0)

    for h, cut in enumerate(heads):
        grads[2 * columns : 3 * columns, cut] = mm_tn(mix[h], back[:, cut]).astype(BF)
        grads[columns : 2 * columns, cut] = mm_tn(mix[HEADS + h], query[:, cut]).astype(BF)
    for h, cut in enumerate(heads):
        back[:, cut] = mm(mix[h], value_weight[:, cut]).astype(BF)
        query[:, cut] = (
            mm(mix[HEADS + h], key_weight[:, cut])
            + mm(hits[h], high[:, cut])
            + mm(hits[h], low[:, cut])
        ).astype(BF)
    grads[:columns, :] = mm_tn(target[...], query[...]).astype(BF)
    grads[3 * columns :, :] = mm_tn(back[...], upstream[...]).astype(BF)
    embedding[...] = (mm(back[...], out_weight[...]) + target[...].astype(F32)).astype(BF)


def shards(
    event_node,
    neighbours,
    event_bucket,
    neighbour_bucket,
    edge_features,
    affinity,
    upstream,
    node_memory,
    edge_weight,
    time_message,
    input_weight,
    hidden_weight,
    gate_bias,
    time_key,
    query_weight,
    key_weight,
    value_weight,
    out_weight,
):
    devices = lax.axis_size("node")
    node_rows, columns = node_memory.shape
    events, fanout = neighbours.shape
    features = edge_features.shape[1]
    stride = columns // LANES
    slots = -(-(3 * events // devices) // 16) * 16
    vmem = pl.BlockSpec(memory_space=pltpu.VMEM)
    smem = pl.BlockSpec(memory_space=pltpu.SMEM)

    info = jnp.stack([event_node % node_rows, event_bucket, jnp.ones_like(event_node)])
    info = jnp.pad(info.astype(BF), ((0, 13), (0, 0)))
    owners = (event_node // node_rows).reshape(1, events)
    message_shape = jax.ShapeDtypeStruct((devices, slots + 16, features), BF)
    outgoing = pl.pallas_call(
        functools.partial(pack_kernel, devices, slots),
        out_shape=message_shape,
        in_specs=[vmem] * 3,
        out_specs=vmem,
        scratch_shapes=[pltpu.VMEM((devices, events), F32)],
        name="pack_step",
    )(edge_features, info, owners)
    inbox = pl.pallas_call(
        functools.partial(exchange_kernel, devices),
        out_shape=message_shape,
        in_specs=[vmem],
        out_specs=vmem,
        scratch_shapes=[
            pltpu.SemaphoreType.DMA((devices,)),
            pltpu.SemaphoreType.DMA((devices,)),
            pltpu.SemaphoreType.DMA,
        ],
        compiler_params=pltpu.CompilerParams(collective_id=0, has_side_effects=True),
        name="exchange_step",
    )(outgoing)
    chunk = 256
    new_memory, own_table = pl.pallas_call(
        functools.partial(memory_kernel, devices, slots, chunk),
        out_shape=(
            jax.ShapeDtypeStruct((node_rows, columns), BF),
            jax.ShapeDtypeStruct((node_rows * stride, LANES), BF),
        ),
        in_specs=[vmem] * 7,
        out_specs=(vmem, vmem),
        scratch_shapes=[
            pltpu.VMEM((devices * slots, features), BF),
            pltpu.VMEM((devices * slots, 16), F32),
            pltpu.VMEM((node_rows, columns), F32),
            pltpu.VMEM((node_rows, LANES), F32),
            pltpu.VMEM((node_rows * stride, LANES), F32),
        ],
        compiler_params=pltpu.CompilerParams(vmem_limit_bytes=VMEM_LIMIT),
        name="memory_step",
    )(
        inbox,
        node_memory,
        edge_weight,
        time_message,
        input_weight,
        hidden_weight,
        gate_bias.reshape(1, -1),
    )
    chips = devices // 2
    side = max(s for s in range(1, chips + 1) if chips % (s * s) == 0 and s**3 <= chips)
    line = chips // (side * side)
    subs = 2
    whole = pl.pallas_call(
        functools.partial(gather_kernel, line, side, subs),
        out_shape=jax.ShapeDtypeStruct((devices * node_rows * stride, LANES), BF),
        in_specs=[vmem],
        out_specs=pl.BlockSpec(memory_space=pl.ANY),
        scratch_shapes=[
            pltpu.SemaphoreType.DMA((chips * subs,)),
            pltpu.SemaphoreType.DMA((chips * subs,)),
            pltpu.SemaphoreType.DMA((subs, line - 1)),
            pltpu.SemaphoreType.DMA((line * subs, side - 1)),
            pltpu.SemaphoreType.DMA((line * subs, side, side - 1)),
            pltpu.SemaphoreType.DMA((chips * subs,)),
            pltpu.SemaphoreType.DMA,
        ],
        compiler_params=pltpu.CompilerParams(collective_id=2, has_side_effects=True),
        name="gather_step",
    )(own_table)

    ids = jnp.concatenate([neighbours.T.reshape(-1), event_node]) * stride
    gap = jnp.zeros((events, GROUP - fanout), F32)
    rest = jnp.zeros((events, LANES - HEADS * GROUP), F32)
    logits = jnp.concatenate([affinity, gap] * HEADS + [rest], axis=1)
    buckets = jnp.pad(neighbour_bucket, ((0, 0), (0, LANES - fanout)))
    resident = whole.size * 4 <= RESIDENT_LIMIT
    near_rows = (fanout + 1) * events * stride
    if resident:
        source = whole
        source_spec = pl.BlockSpec(memory_space=pl.ANY)
        extra = [
            pltpu.VMEM(whole.shape, BF),
            pltpu.VMEM(whole.shape, F32),
            pltpu.VMEM((near_rows, LANES), F32),
            pltpu.SemaphoreType.DMA((8,)),
        ]
    else:
        source = whole.astype(F32)
        source_spec = pl.BlockSpec(memory_space=pl.ANY)
        extra = [pltpu.VMEM((near_rows, LANES), F32), pltpu.SemaphoreType.DMA]
    embedding, grads = pl.pallas_call(
        functools.partial(event_kernel, resident, events, fanout),
        out_shape=(
            jax.ShapeDtypeStruct((events, columns), BF),
            jax.ShapeDtypeStruct((4 * columns, columns), BF),
        ),
        in_specs=[smem, source_spec] + [vmem] * 8,
        out_specs=(vmem, vmem),
        scratch_shapes=extra
        + [
            pltpu.VMEM((events, columns), BF),
            pltpu.VMEM((events, columns), BF),
            pltpu.VMEM((events, columns), BF),
            pltpu.VMEM((2 * HEADS, events, columns), F32),
            pltpu.VMEM((2 * HEADS, events, columns), BF),
            pltpu.VMEM((HEADS, events, LANES), BF),
            pltpu.VMEM((HEADS, events, LANES), F32),
        ],
        compiler_params=pltpu.CompilerParams(vmem_limit_bytes=VMEM_LIMIT),
        name="event_step",
    )(
        ids,
        source,
        buckets,
        logits,
        upstream,
        time_key,
        query_weight,
        key_weight,
        value_weight,
        out_weight,
    )
    factor = 1.0 / math.sqrt(events * devices)
    half = 2 * columns
    strands = max(1, min(4, half // (16 * chips)))
    total = pl.pallas_call(
        functools.partial(reduce_kernel, line, side, strands, factor),
        out_shape=jax.ShapeDtypeStruct((2 * half, columns), BF),
        in_specs=[vmem],
        out_specs=vmem,
        scratch_shapes=[
            pltpu.VMEM((half, columns), BF),
            pltpu.VMEM((half, columns), BF),
            pltpu.VMEM((half, columns), BF),
            pltpu.VMEM((half // side, columns), BF),
            pltpu.VMEM((half // side, columns), BF),
            pltpu.VMEM((half // (side * side), columns), BF),
            pltpu.VMEM((half // (side * side), columns), BF),
            pltpu.SemaphoreType.DMA((strands,)),
            pltpu.SemaphoreType.DMA((strands,)),
        ]
        + [
            pltpu.SemaphoreType.DMA((strands, places))
            for places in (side, side, line, line, side, side, side)
            for _ in range(2)
        ],
        compiler_params=pltpu.CompilerParams(
            collective_id=1, has_side_effects=True, vmem_limit_bytes=VMEM_LIMIT
        ),
        name="reduce_step",
    )(grads).astype(F32)
    return (embedding, new_memory) + tuple(
        total[part * columns : (part + 1) * columns] for part in range(4)
    )


def solution(mesh):
    placed = (
        P("node"),
        P("node", None),
        P("node"),
        P("node", None),
        P("node", None),
        P("node", None),
        P("node", None),
        P("node", None),
        P(),
        P(),
        P(),
        P(),
        P(),
        P(),
        P(),
        P(),
        P(),
        P(),
    )
    return jax.shard_map(
        shards,
        mesh=mesh,
        in_specs=placed,
        out_specs=(P("node", None), P("node", None), P(), P(), P(), P()),
        check_vma=False,
    )
```

```python
import functools
import math

import jax
import jax.numpy as jnp
from jax import lax
from jax.experimental import pallas as pl
from jax.experimental.pallas import tpu as pltpu
from jax.sharding import PartitionSpec as P

HEADS = 2
LANES = 128
GROUP = 32
BF = jnp.bfloat16
F32 = jnp.float32
VMEM_LIMIT = 60 * 1024 * 1024
RESIDENT_LIMIT = 20 * 1024 * 1024
NT = (((1,), (1,)), ((), ()))
TN = (((0,), (0,)), ((), ()))


def mm(a, b):
    return jnp.dot(a, b, preferred_element_type=F32)


def mm_nt(a, b):
    return lax.dot_general(a, b, NT, preferred_element_type=F32)


def mm_tn(a, b):
    return lax.dot_general(a, b, TN, preferred_element_type=F32)


def halves(table):
    high = table.astype(BF)
    low = (table - high.astype(F32)).astype(BF)
    return high, low


def pack_kernel(devices, slots, feats, meta, owners, outgoing, sel):
    events = feats.shape[0]
    ids = lax.broadcasted_iota(jnp.int32, (devices, events), 0)
    theirs = ids == owners[...]
    before = lax.broadcasted_iota(jnp.int32, (events, events), 0) < lax.broadcasted_iota(
        jnp.int32, (events, events), 1
    )
    rank = mm(theirs.astype(F32).astype(BF), before.astype(F32).astype(BF))
    sel[...] = jnp.where(theirs, rank, -1.0)
    slot_ids = lax.broadcasted_iota(jnp.int32, (slots, events), 0).astype(F32)
    lane_ids = lax.broadcasted_iota(jnp.int32, (LANES, events), 0).astype(F32)

    def pick(step, carry):
        for part in range(4):
            device = step * 4 + part
            row = sel[pl.ds(device, 1), :]
            hits = (slot_ids == row).astype(F32).astype(BF)
            outgoing[device, :slots, :] = mm(hits, feats[...]).astype(BF)
            turned = (lane_ids == row).astype(F32).astype(BF)
            outgoing[device, slots:, :] = mm_nt(meta[...], turned).astype(BF)
        return carry

    lax.fori_loop(0, devices // 4, pick, 0)


def exchange_kernel(devices, outgoing, inbox, send_sems, recv_sems, own_sem):
    me = lax.axis_index("node")
    barrier = pltpu.get_barrier_semaphore()

    def greet(step, carry):
        pl.semaphore_signal(
            barrier,
            inc=1,
            device_id=(lax.rem(me + step, devices),),
            device_id_type=pl.DeviceIdType.MESH,
        )
        return carry

    lax.fori_loop(1, devices, greet, 0)
    pl.semaphore_wait(barrier, devices - 1)

    def send(step):
        peer = lax.rem(me + step, devices)
        return pltpu.make_async_remote_copy(
            src_ref=outgoing.at[peer],
            dst_ref=inbox.at[me],
            send_sem=send_sems.at[peer],
            recv_sem=recv_sems.at[me],
            device_id=(peer,),
            device_id_type=pl.DeviceIdType.MESH,
        )

    def receive(step):
        peer = lax.rem(me + step, devices)
        return pltpu.make_async_remote_copy(
            src_ref=outgoing.at[peer],
            dst_ref=inbox.at[peer],
            send_sem=send_sems.at[peer],
            recv_sem=recv_sems.at[peer],
            device_id=(peer,),
            device_id_type=pl.DeviceIdType.MESH,
        )

    def start(step, carry):
        send(step).start()
        return carry

    def finish(step, carry):
        receive(step).wait_recv()
        send(step).wait_send()
        return carry

    lax.fori_loop(1, devices, start, 0)
    own = pltpu.make_async_copy(outgoing.at[me], inbox.at[me], own_sem)
    own.start()
    own.wait()
    lax.fori_loop(1, devices, finish, 0)


def reduce_kernel(
    line,
    side,
    strands,
    factor,
    grads,
    result,
    near,
    pair,
    first_land,
    first_sum,
    second_land,
    second_sum,
    line_land,
    pair_send,
    pair_recv,
    first_send,
    first_recv,
    second_send,
    second_recv,
    line_send,
    line_recv,
    line_back_send,
    line_back_recv,
    second_back_send,
    second_back_recv,
    first_back_send,
    first_back_recv,
    hop_send,
    hop_recv,
):
    me = lax.axis_index("node")
    core = lax.rem(me, 2)
    chip = me // 2
    partner = me + 1 - 2 * core
    low, mid, far = lax.rem(chip, side), lax.rem(chip // side, side), chip // (side * side)
    first = (1 - core) * low + core * mid
    second = (1 - core) * mid + core * low
    first_stride = 2 * (1 + core * (side - 1))
    second_stride = 2 * (side - core * (side - 1))
    half = grads.shape[0] // 2
    rows = half // strands
    rows_a = rows // side
    rows_b = rows_a // side
    rows_z = rows_b // line
    mesh_id = pl.DeviceIdType.MESH

    firsts = [lax.rem(first + step, side) for step in range(1, side)]
    seconds = [lax.rem(second + step, side) for step in range(1, side)]
    fars = [lax.rem(far + step, line) for step in range(1, line)]

    def first_device(place):
        return me + (place - first) * first_stride

    def second_device(place):
        return me + (place - second) * second_stride

    def far_device(place):
        return me + (place - far) * (2 * side * side)

    everyone = (
        [partner]
        + [first_device(place) for place in firsts]
        + [second_device(place) for place in seconds]
        + [far_device(place) for place in fars]
    )
    barrier = pltpu.get_barrier_semaphore()
    for device in everyone:
        pl.semaphore_signal(barrier, inc=1, device_id=(device,), device_id_type=mesh_id)
    pl.semaphore_wait(barrier, len(everyone))

    def span(start, size):
        return pl.ds(pl.multiple_of(start, 16), size)

    def remote(src, dst, send, recv, device):
        return pltpu.make_async_remote_copy(
            src_ref=src,
            dst_ref=dst,
            send_sem=send,
            recv_sem=recv,
            device_id=(device,),
            device_id_type=mesh_id,
        )

    def swap(s):
        return remote(
            grads.at[span((1 - core) * half + s * rows, rows)],
            near.at[span(s * rows, rows)],
            pair_send.at[s],
            pair_recv.at[s],
            partner,
        )

    def to_first(s, place, source):
        return remote(
            pair.at[span(s * rows + place * rows_a, rows_a)],
            first_land.at[span(s * rows + source * rows_a, rows_a)],
            first_send.at[s, place],
            first_recv.at[s, source],
            first_device(place),
        )

    def to_second(s, place, source):
        return remote(
            first_sum.at[span(s * rows_a + place * rows_b, rows_b)],
            second_land.at[span(s * rows_a + source * rows_b, rows_b)],
            second_send.at[s, place],
            second_recv.at[s, source],
            second_device(place),
        )

    def to_far(s, place, source):
        return remote(
            second_sum.at[span(s * rows_b + place * rows_z, rows_z)],
            line_land.at[span(s * rows_b + source * rows_z, rows_z)],
            line_send.at[s, place],
            line_recv.at[s, source],
            far_device(place),
        )

    def place_of(which, s, a, b=0, f=0):
        return which * half + s * rows + a * rows_a + b * rows_b + f * rows_z

    def spread(at, send, recv, device):
        return remote(result.at[at], result.at[at], send, recv, device)

    def back_far(s, place, source):
        at = span(place_of(core, s, first, second, source), rows_z)
        return spread(at, line_back_send.at[s, place], line_back_recv.at[s, source], far_device(place))

    def back_second(s, place, source):
        at = span(place_of(core, s, first, source), rows_b)
        return spread(
            at, second_back_send.at[s, place], second_back_recv.at[s, source], second_device(place)
        )

    def back_first(s, place, source):
        at = span(place_of(core, s, source), rows_a)
        return spread(
            at, first_back_send.at[s, place], first_back_recv.at[s, source], first_device(place)
        )

    def hop(s, source, which):
        at = span(place_of(which, s, source), rows_a)
        return spread(at, hop_send.at[s, source], hop_recv.at[s, source], partner)

    started = []

    def start(made):
        made.start()
        started.append(made)

    def stage_pair(s):
        swap(s).wait_recv()
        at = span(s * rows, rows)
        own = grads[span(core * half + s * rows, rows), :]
        pair[at, :] = (own.astype(F32) + near[at, :].astype(F32)).astype(BF)
        for place in firsts:
            start(to_first(s, place, first))

    def stage_first(s):
        total = pair[span(s * rows + first * rows_a, rows_a), :].astype(F32)
        for place in firsts:
            to_first(s, place, place).wait_recv()
            total += first_land[span(s * rows + place * rows_a, rows_a), :].astype(F32)
        first_sum[span(s * rows_a, rows_a), :] = total.astype(BF)
        for place in seconds:
            start(to_second(s, place, second))

    def stage_second(s):
        total = first_sum[span(s * rows_a + second * rows_b, rows_b), :].astype(F32)
        for place in seconds:
            to_second(s, place, place).wait_recv()
            total += second_land[span(s * rows_a + place * rows_b, rows_b), :].astype(F32)
        second_sum[span(s * rows_b, rows_b), :] = total.astype(BF)
        for place in fars:
            start(to_far(s, place, far))

    def stage_line(s):
        total = second_sum[span(s * rows_b + far * rows_z, rows_z), :].astype(F32)
        for place in fars:
            to_far(s, place, place).wait_recv()
            total += line_land[span(s * rows_b + place * rows_z, rows_z), :].astype(F32)
        result[span(place_of(core, s, first, second, far), rows_z), :] = (total * factor).astype(BF)
        for place in fars:
            start(back_far(s, place, far))

    def stage_back_line(s):
        for place in fars:
            back_far(s, place, place).wait_recv()
        for place in seconds:
            start(back_second(s, place, second))

    def stage_back_second(s):
        for place in seconds:
            back_second(s, place, place).wait_recv()
        for place in firsts:
            start(back_first(s, place, first))
        start(hop(s, first, core))

    def stage_back_first(s):
        for place in firsts:
            back_first(s, place, place).wait_recv()
            start(hop(s, place, core))

    for s in range(strands):
        start(swap(s))
    for s in range(strands):
        stage_pair(s)
    stages = [
        stage_first,
        stage_second,
        stage_line,
        stage_back_line,
        stage_back_second,
        stage_back_first,
    ]
    for step in range(strands + len(stages) - 1):
        for number, stage in enumerate(stages):
            if 0 <= step - number < strands:
                stage(step - number)
    for s in range(strands):
        for place in [first] + firsts:
            hop(s, place, 1 - core).wait_recv()
    for made in started:
        made.wait_send()


def memory_kernel(
    devices,
    slots,
    chunk,
    inbox,
    memory,
    edge_weight,
    time_message,
    input_weight,
    hidden_weight,
    gate_bias,
    out_memory,
    out_table,
    picked,
    picked_meta,
    totals,
    counts,
    wide,
):
    rows = memory.shape[0]
    columns = memory.shape[1]
    stride = columns // LANES
    turn = (
        lax.broadcasted_iota(jnp.int32, (slots, LANES), 0)
        == lax.broadcasted_iota(jnp.int32, (slots, LANES), 1)
    ).astype(F32).astype(BF)

    def pick(step, carry):
        for part in range(4):
            source = step * 4 + part
            at = pl.ds(pl.multiple_of(source * slots, slots), slots)
            picked[at, :] = inbox[source, :slots, :]
            picked_meta[at, :] = mm_nt(turn, inbox[source, slots:, :])
        return carry

    lax.fori_loop(0, devices // 4, pick, 0)
    totals[...] = jnp.zeros_like(totals)
    counts[...] = jnp.zeros_like(counts)
    high, low = halves(time_message[...])
    weight = edge_weight[...]

    def add(step, carry):
        at = pl.ds(pl.multiple_of(step * chunk, chunk), chunk)
        info = picked_meta[at, :]
        node, bucket, valid = info[:, 0:1], info[:, 1:2], info[:, 2:3]
        lanes = lax.broadcasted_iota(jnp.int32, (chunk, high.shape[0]), 1).astype(F32)
        picks = (lanes == bucket).astype(F32).astype(BF)
        pre = mm(picked[at, :], weight) + mm(picks, high) + mm(picks, low)
        message = (pre / (1.0 + jnp.exp(-pre))).astype(BF)
        ids = lax.broadcasted_iota(jnp.int32, (chunk, rows), 1).astype(F32)
        hot = jnp.where(ids == node, valid, 0.0).astype(BF)
        totals[...] += mm_tn(hot, message)
        counts[...] += mm_tn(hot, jnp.ones((chunk, LANES), BF))
        return carry

    lax.fori_loop(0, devices * slots // chunk, add, 0)
    count = counts[:, 0:1]
    aggregate = (totals[...] / jnp.maximum(count, 1.0)).astype(BF)
    previous = memory[...]

    def gate(which):
        cut = slice(which * columns, (which + 1) * columns)
        return (
            mm(aggregate, input_weight[:, cut]) + gate_bias[:, cut],
            mm(previous, hidden_weight[:, cut]),
        )

    from_input, from_hidden = gate(0)
    update = jax.nn.sigmoid(from_input + from_hidden)
    from_input, from_hidden = gate(1)
    resets = jax.nn.sigmoid(from_input + from_hidden)
    from_input, from_hidden = gate(2)
    candidate = jnp.tanh(from_input + resets * from_hidden)
    old = previous.astype(F32)
    fresh = (1.0 - update) * candidate + update * old
    fresh = jnp.where(count > 0, fresh, old)
    out_memory[...] = fresh.astype(BF)
    for part in range(stride):
        wide[pl.ds(part, rows, stride=stride), :] = fresh[:, part * LANES : (part + 1) * LANES]
    out_table[...] = wide[...].astype(BF)


def gather_kernel(
    line,
    side,
    subs,
    own,
    whole,
    recv,
    hop_recv,
    line_send,
    first_send,
    second_send,
    hop_send,
    own_sem,
):
    me = lax.axis_index("node")
    core = lax.rem(me, 2)
    chip = me // 2
    partner = me + 1 - 2 * core
    low, mid, far = lax.rem(chip, side), lax.rem(chip // side, side), chip // (side * side)
    first = (1 - core) * low + core * mid
    second = (1 - core) * mid + core * low
    first_stride = 1 + core * (side - 1)
    second_stride = side - core * (side - 1)
    rows = own.shape[0]
    size = rows // subs
    mesh_id = pl.DeviceIdType.MESH

    def chip_of(along, over, across):
        return (
            lax.rem(far + line - along, line) * side * side
            + lax.rem(first + side - over, side) * first_stride
            + lax.rem(second + side - across, side) * second_stride
        )

    peers = [2 * chip_of(line - step, 0, 0) + core for step in range(1, line)]
    first_peers = [2 * chip_of(0, side - step, 0) + core for step in range(1, side)]
    second_peers = [2 * chip_of(0, 0, side - step) + core for step in range(1, side)]
    everyone = peers + first_peers + second_peers + [partner]
    barrier = pltpu.get_barrier_semaphore()
    for device in everyone:
        pl.semaphore_signal(barrier, inc=1, device_id=(device,), device_id_type=mesh_id)
    pl.semaphore_wait(barrier, len(everyone))

    def at(source, part, kind):
        return pl.ds(pl.multiple_of((2 * source + kind) * rows + part * size, 16), size)

    def copy(source, part, mine, send_sem, device):
        src = own.at[pl.ds(part * size, size)] if mine else whole.at[at(source, part, core)]
        return pltpu.make_async_remote_copy(
            src_ref=src,
            dst_ref=whole.at[at(source, part, core)],
            send_sem=send_sem,
            recv_sem=recv.at[source * subs + part],
            device_id=(device,),
            device_id_type=mesh_id,
        )

    def hop(source, part, mine, kind):
        src = own.at[pl.ds(part * size, size)] if mine else whole.at[at(source, part, kind)]
        return pltpu.make_async_remote_copy(
            src_ref=src,
            dst_ref=whole.at[at(source, part, kind)],
            send_sem=hop_send.at[source * subs + part],
            recv_sem=hop_recv.at[source * subs + part],
            device_id=(partner,),
            device_id_type=mesh_id,
        )

    started = []

    def start(made):
        made.start()
        started.append(made)

    def landed(source, part):
        copy(source, part, False, hop_send.at[0], partner).wait_recv()

    stay = pltpu.make_async_copy(own, whole.at[pl.ds(pl.multiple_of(me * rows, 16), rows)], own_sem)
    stay.start()
    steps = line * subs
    for step in range(steps + 2):
        if step < steps:
            along, part = divmod(step, subs)
            source = chip_of(along, 0, 0)
            mine = along == 0
            if not mine:
                landed(source, part)
            for to, device in enumerate(first_peers):
                start(copy(source, part, mine, first_send.at[step, to], device))
            if mine:
                for to, device in enumerate(peers):
                    start(copy(source, part, mine, line_send.at[part, to], device))
            for to, device in enumerate(second_peers):
                start(copy(source, part, mine, second_send.at[step, 0, to], device))
            start(hop(source, part, mine, core))
        if 0 <= step - 1 < steps:
            along, part = divmod(step - 1, subs)
            for over in range(1, side):
                source = chip_of(along, over, 0)
                landed(source, part)
                for to, device in enumerate(second_peers):
                    start(copy(source, part, False, second_send.at[step - 1, over, to], device))
                start(hop(source, part, False, core))
        if 0 <= step - 2 < steps:
            along, part = divmod(step - 2, subs)
            for across in range(1, side):
                for over in range(side):
                    source = chip_of(along, over, across)
                    landed(source, part)
                    start(hop(source, part, False, core))
    stay.wait()
    for made in started:
        made.wait_send()

    def drain(source, carry):
        for part in range(subs):
            hop(source, part, False, 1 - core).wait_recv()
        return carry

    lax.fori_loop(0, line * side * side, drain, 0)


def event_kernel(
    resident,
    events,
    fanout,
    ids,
    own_ids,
    source,
    buckets,
    affinity,
    upstream,
    time_key,
    query_weight,
    key_weight,
    value_weight,
    out_weight,
    embedding,
    grads,
    *scratch,
):
    columns = upstream.shape[1]
    head = columns // HEADS
    stride = columns // LANES
    kinds = 2 * HEADS
    blocks = events // GROUP
    wide = fanout * GROUP
    tall = 2 * kinds * GROUP
    if resident:
        landing, table, near, sems, *scratch = scratch
        parts = sems.shape[0]
        size = landing.shape[0] // parts
        copies = []
        for part in range(parts):
            at = pl.ds(part * size, size)
            copies.append(pltpu.make_async_copy(source.at[at], landing.at[at], sems.at[part]))
            copies[-1].start()
    else:
        near, sem, *scratch = scratch
        picks = (fanout + 1) * events

        def request(start, row):
            pltpu.make_async_copy(
                source.at[pl.ds(pl.multiple_of(start * stride, stride), stride)],
                near.at[pl.ds(pl.multiple_of(row * stride, stride), stride)],
                sem,
            ).start()

        def request_all(e, carry):
            for j in range(fanout):
                request(ids[j, e], j * events + e)
            request(own_ids[e], fanout * events + e)
            return carry

        lax.fori_loop(0, events, request_all, 0)
    target, query, back, pull, pull_time, mix, hits, scores, close, hot, names, logits = scratch
    heads = [slice(h * head, (h + 1) * head) for h in range(HEADS)]
    high, low = halves(time_key[...])

    def keep(dest, kind, values):
        upper, lower = halves(values)
        for b in range(blocks):
            rows = slice(b * GROUP, (b + 1) * GROUP)
            first = b * tall + kind * GROUP
            dest[first : first + GROUP, :] = upper[rows, :]
            first += kinds * GROUP
            dest[first : first + GROUP, :] = lower[rows, :]

    back[...] = mm_nt(upstream[...], out_weight[...]).astype(BF)
    for h, cut in enumerate(heads):
        keep(pull, HEADS + h, mm_nt(back[:, cut], value_weight[:, cut]))
        keep(pull_time, HEADS + h, jnp.zeros((events, LANES), F32))
    even = (
        lax.broadcasted_iota(jnp.int32, (fanout, LANES), 0)
        == lax.broadcasted_iota(jnp.int32, (fanout, LANES), 1)
    ).astype(F32).astype(BF)
    names[...] = mm_tn(buckets[...].astype(F32).astype(BF), even)
    logits[...] = jnp.zeros_like(logits)
    logits[:fanout, :] = affinity[...]
    lane = lax.broadcasted_iota(jnp.int32, (GROUP, LANES), 1)
    lane_names = lane.astype(F32)

    def mark(b, carry):
        mine = names[pl.ds(pl.multiple_of(b * GROUP, GROUP), GROUP), :]
        for j in range(fanout):
            at = pl.ds(pl.multiple_of(b * wide + j * GROUP, GROUP), GROUP)
            hot[at, :] = (lane_names == mine[:, j : j + 1]).astype(F32).astype(BF)
        return carry

    lax.fori_loop(0, blocks, mark, 0)

    if resident:
        step_rows = 256
        for part in range(parts):
            copies[part].wait()

            def widen(step, carry, part=part):
                at = pl.ds(pl.multiple_of(part * size + step * step_rows, step_rows), step_rows)
                table[at, :] = landing[at, :].astype(F32)
                return carry

            lax.fori_loop(0, size // step_rows, widen, 0)

        def fetch(start, row):
            near[pl.ds(pl.multiple_of(row * stride, stride), stride), :] = table[
                pl.ds(pl.multiple_of(start * stride, stride), stride), :
            ]

        unroll = 16

        def fetch_own(step, carry):
            for place in range(unroll):
                e = step * unroll + place
                fetch(own_ids[e], fanout * events + e)
            return carry

        def fetch_near(step, carry):
            for place in range(2):
                e = step * 2 + place
                for j in range(fanout):
                    fetch(ids[j, e], j * events + e)
            return carry

        lax.fori_loop(0, events // unroll, fetch_own, 0)
        lax.fori_loop(0, events // 2, fetch_near, 0)
    else:
        pltpu.make_async_copy(source.at[pl.ds(0, picks * stride)], near, sem).wait()

    for part in range(stride):
        target[:, part * LANES : (part + 1) * LANES] = near[
            pl.ds(fanout * events * stride + part, events, stride=stride), :
        ].astype(BF)
    query[...] = mm(target[...], query_weight[...]).astype(BF)
    for h, cut in enumerate(heads):
        keep(pull, h, mm_nt(query[:, cut], key_weight[:, cut]))
        keep(pull_time, h, mm_nt(query[:, cut], high[:, cut]) + mm_nt(query[:, cut], low[:, cut]))

    scale = 1.0 / math.sqrt(head)
    pad = scores.shape[0] // blocks
    own = lax.rem(lane, GROUP) == lax.broadcasted_iota(jnp.int32, (GROUP, LANES), 0)
    row_ids = lax.broadcasted_iota(jnp.int32, (pad, LANES), 0)
    lane_ids = lax.broadcasted_iota(jnp.int32, (pad, LANES), 1)
    forward = lane_ids < HEADS * GROUP
    per_row = LANES // GROUP

    def score(b):
        first = b * GROUP
        for j in range(fanout):
            at = pl.ds(pl.multiple_of(b * wide + j * GROUP, GROUP), GROUP)
            for part in range(stride):
                close[at, part * LANES : (part + 1) * LANES] = near[
                    pl.ds((j * events + first) * stride + part, GROUP, stride=stride), :
                ].astype(BF)
        at = pl.ds(pl.multiple_of(b * wide, GROUP), wide)
        from_at = pl.ds(pl.multiple_of(b * tall, GROUP), tall)
        both = mm_nt(close[at, :], pull[from_at, :]) + mm_nt(hot[at, :], pull_time[from_at, :])
        both = both[:, :LANES] + both[:, LANES:]
        raw = jnp.zeros((pad, LANES), F32)
        for j in range(fanout):
            line = jnp.where(own, both[j * GROUP : (j + 1) * GROUP, :], 0.0)
            raw = jnp.where(row_ids == j, jnp.sum(line, axis=0, keepdims=True), raw)
        chunk = pl.multiple_of(b // per_row * LANES, LANES)
        piece = logits[:, pl.ds(chunk, LANES)]
        piece = pltpu.roll(piece, lax.rem(LANES - lax.rem(b, per_row) * GROUP, LANES), axis=1)
        given = piece
        for h in range(1, HEADS):
            moved = pltpu.roll(piece, h * GROUP, axis=1)
            given = jnp.where(lane_ids >= h * GROUP, moved, given)
        scores[pl.ds(pl.multiple_of(b * pad, pad), pad), :] = jnp.where(
            forward, raw * scale + given, raw
        )

    def score_two(step, carry):
        for place in range(2):
            score(step * 2 + place)
        return carry

    lax.fori_loop(0, blocks // 2, score_two, 0)

    for b in range(blocks):
        at = slice(b * pad, (b + 1) * pad)
        here = scores[at, :]
        active = row_ids < fanout
        top = jnp.max(jnp.where(active, here, -3.0e38), axis=0, keepdims=True)
        raised = jnp.where(active, jnp.exp(jnp.where(active, here - top, 0.0)), 0.0)
        probs = raised / jnp.sum(raised, axis=0, keepdims=True)
        slopes = pltpu.roll(here, HEADS * GROUP, axis=1).astype(BF).astype(F32)
        inner = jnp.sum(probs * slopes, axis=0, keepdims=True)
        slopes = probs * (slopes - inner) * scale
        scores[at, :] = jnp.where(forward, probs, pltpu.roll(slopes, HEADS * GROUP, axis=1))

    def blend(b):
        weights = scores[pl.ds(pl.multiple_of(b * pad, pad), pad), :]
        spread = jnp.concatenate(
            [
                jnp.where(own, jnp.broadcast_to(weights[j : j + 1, :], (GROUP, LANES)), 0.0)
                for j in range(fanout)
            ],
            axis=0,
        ).astype(BF)
        at = pl.ds(pl.multiple_of(b * wide, GROUP), wide)
        mixed = mm_tn(spread, close[at, :]).astype(BF)
        times = mm_tn(spread, hot[at, :]).astype(BF)
        to = pl.ds(pl.multiple_of(b * GROUP, GROUP), GROUP)
        for k in range(kinds):
            mix[k, to, :] = mixed[k * GROUP : (k + 1) * GROUP, :]
        for h in range(HEADS):
            hits[h, to, :] = times[(HEADS + h) * GROUP : (HEADS + h + 1) * GROUP, :]

    def blend_two(step, carry):
        for place in range(2):
            blend(step * 2 + place)
        return carry

    lax.fori_loop(0, blocks // 2, blend_two, 0)

    for h, cut in enumerate(heads):
        grads[2 * columns : 3 * columns, cut] = mm_tn(mix[h], back[:, cut]).astype(BF)
        grads[columns : 2 * columns, cut] = mm_tn(mix[HEADS + h], query[:, cut]).astype(BF)
    for h, cut in enumerate(heads):
        back[:, cut] = mm(mix[h], value_weight[:, cut]).astype(BF)
        query[:, cut] = (
            mm(mix[HEADS + h], key_weight[:, cut])
            + mm(hits[h], high[:, cut])
            + mm(hits[h], low[:, cut])
        ).astype(BF)
    grads[:columns, :] = mm_tn(target[...], query[...]).astype(BF)
    grads[3 * columns :, :] = mm_tn(back[...], upstream[...]).astype(BF)
    embedding[...] = (mm(back[...], out_weight[...]) + target[...].astype(F32)).astype(BF)


def shards(
    event_node,
    neighbours,
    event_bucket,
    neighbour_bucket,
    edge_features,
    affinity,
    upstream,
    node_memory,
    edge_weight,
    time_message,
    input_weight,
    hidden_weight,
    gate_bias,
    time_key,
    query_weight,
    key_weight,
    value_weight,
    out_weight,
):
    devices = lax.axis_size("node")
    node_rows, columns = node_memory.shape
    events, fanout = neighbours.shape
    features = edge_features.shape[1]
    stride = columns // LANES
    slots = -(-(3 * events // devices) // 16) * 16
    vmem = pl.BlockSpec(memory_space=pltpu.VMEM)
    smem = pl.BlockSpec(memory_space=pltpu.SMEM)

    info = jnp.stack([event_node % node_rows, event_bucket, jnp.ones_like(event_node)])
    info = jnp.pad(info.astype(BF), ((0, 13), (0, 0)))
    owners = (event_node // node_rows).reshape(1, events)
    message_shape = jax.ShapeDtypeStruct((devices, slots + 16, features), BF)
    outgoing = pl.pallas_call(
        functools.partial(pack_kernel, devices, slots),
        out_shape=message_shape,
        in_specs=[vmem] * 3,
        out_specs=vmem,
        scratch_shapes=[pltpu.VMEM((devices, events), F32)],
        name="pack_step",
    )(edge_features, info, owners)
    inbox = pl.pallas_call(
        functools.partial(exchange_kernel, devices),
        out_shape=message_shape,
        in_specs=[vmem],
        out_specs=vmem,
        scratch_shapes=[
            pltpu.SemaphoreType.DMA((devices,)),
            pltpu.SemaphoreType.DMA((devices,)),
            pltpu.SemaphoreType.DMA,
        ],
        compiler_params=pltpu.CompilerParams(collective_id=0, has_side_effects=True),
        name="exchange_step",
    )(outgoing)
    chunk = 256
    new_memory, own_table = pl.pallas_call(
        functools.partial(memory_kernel, devices, slots, chunk),
        out_shape=(
            jax.ShapeDtypeStruct((node_rows, columns), BF),
            jax.ShapeDtypeStruct((node_rows * stride, LANES), BF),
        ),
        in_specs=[vmem] * 7,
        out_specs=(vmem, vmem),
        scratch_shapes=[
            pltpu.VMEM((devices * slots, features), BF),
            pltpu.VMEM((devices * slots, 16), F32),
            pltpu.VMEM((node_rows, columns), F32),
            pltpu.VMEM((node_rows, LANES), F32),
            pltpu.VMEM((node_rows * stride, LANES), F32),
        ],
        compiler_params=pltpu.CompilerParams(vmem_limit_bytes=VMEM_LIMIT),
        name="memory_step",
    )(
        inbox,
        node_memory,
        edge_weight,
        time_message,
        input_weight,
        hidden_weight,
        gate_bias.reshape(1, -1),
    )
    chips = devices // 2
    side = max(s for s in range(1, chips + 1) if chips % (s * s) == 0 and s**3 <= chips)
    line = chips // (side * side)
    subs = 2
    whole = pl.pallas_call(
        functools.partial(gather_kernel, line, side, subs),
        out_shape=jax.ShapeDtypeStruct((devices * node_rows * stride, LANES), BF),
        in_specs=[vmem],
        out_specs=pl.BlockSpec(memory_space=pl.ANY),
        scratch_shapes=[
            pltpu.SemaphoreType.DMA((chips * subs,)),
            pltpu.SemaphoreType.DMA((chips * subs,)),
            pltpu.SemaphoreType.DMA((subs, line - 1)),
            pltpu.SemaphoreType.DMA((line * subs, side - 1)),
            pltpu.SemaphoreType.DMA((line * subs, side, side - 1)),
            pltpu.SemaphoreType.DMA((chips * subs,)),
            pltpu.SemaphoreType.DMA,
        ],
        compiler_params=pltpu.CompilerParams(collective_id=2, has_side_effects=True),
        name="gather_step",
    )(own_table)

    resident = whole.size * 4 <= RESIDENT_LIMIT
    near_rows = (fanout + 1) * events * stride
    if resident:
        source = whole
        source_spec = pl.BlockSpec(memory_space=pl.ANY)
        extra = [
            pltpu.VMEM(whole.shape, BF),
            pltpu.VMEM(whole.shape, F32),
            pltpu.VMEM((near_rows, LANES), F32),
            pltpu.SemaphoreType.DMA((8,)),
        ]
    else:
        source = whole.astype(F32)
        source_spec = pl.BlockSpec(memory_space=pl.ANY)
        extra = [pltpu.VMEM((near_rows, LANES), F32), pltpu.SemaphoreType.DMA]
    embedding, grads = pl.pallas_call(
        functools.partial(event_kernel, resident, events, fanout),
        out_shape=(
            jax.ShapeDtypeStruct((events, columns), BF),
            jax.ShapeDtypeStruct((4 * columns, columns), BF),
        ),
        in_specs=[smem, smem, source_spec] + [vmem] * 8,
        out_specs=(vmem, vmem),
        scratch_shapes=extra
        + [
            pltpu.VMEM((events, columns), BF),
            pltpu.VMEM((events, columns), BF),
            pltpu.VMEM((events, columns), BF),
            pltpu.VMEM((4 * HEADS * events, columns), BF),
            pltpu.VMEM((4 * HEADS * events, LANES), BF),
            pltpu.VMEM((2 * HEADS, events, columns), BF),
            pltpu.VMEM((HEADS, events, LANES), BF),
            pltpu.VMEM((events // GROUP * 16, LANES), F32),
            pltpu.VMEM((fanout * events, columns), BF),
            pltpu.VMEM((fanout * events, LANES), BF),
            pltpu.VMEM((events, LANES), F32),
            pltpu.VMEM((16, events), F32),
        ],
        compiler_params=pltpu.CompilerParams(vmem_limit_bytes=VMEM_LIMIT),
        name="event_step",
    )(
        neighbours.T,
        event_node,
        source,
        neighbour_bucket.T,
        affinity.T,
        upstream,
        time_key,
        query_weight,
        key_weight,
        value_weight,
        out_weight,
    )
    factor = 1.0 / math.sqrt(events * devices)
    half = 2 * columns
    strands = max(1, min(4, half // (16 * chips)))
    total = pl.pallas_call(
        functools.partial(reduce_kernel, line, side, strands, factor),
        out_shape=jax.ShapeDtypeStruct((2 * half, columns), BF),
        in_specs=[vmem],
        out_specs=vmem,
        scratch_shapes=[
            pltpu.VMEM((half, columns), BF),
            pltpu.VMEM((half, columns), BF),
            pltpu.VMEM((half, columns), BF),
            pltpu.VMEM((half // side, columns), BF),
            pltpu.VMEM((half // side, columns), BF),
            pltpu.VMEM((half // (side * side), columns), BF),
            pltpu.VMEM((half // (side * side), columns), BF),
            pltpu.SemaphoreType.DMA((strands,)),
            pltpu.SemaphoreType.DMA((strands,)),
        ]
        + [
            pltpu.SemaphoreType.DMA((strands, places))
            for places in (side, side, line, line, side, side, side)
            for _ in range(2)
        ],
        compiler_params=pltpu.CompilerParams(
            collective_id=1, has_side_effects=True, vmem_limit_bytes=VMEM_LIMIT
        ),
        name="reduce_step",
    )(grads).astype(F32)
    return (embedding, new_memory) + tuple(
        total[part * columns : (part + 1) * columns] for part in range(4)
    )


def solution(mesh):
    placed = (
        P("node"),
        P("node", None),
        P("node"),
        P("node", None),
        P("node", None),
        P("node", None),
        P("node", None),
        P("node", None),
        P(),
        P(),
        P(),
        P(),
        P(),
        P(),
        P(),
        P(),
        P(),
        P(),
    )
    return jax.shard_map(
        shards,
        mesh=mesh,
        in_specs=placed,
        out_specs=(P("node", None), P("node", None), P(), P(), P(), P()),
        check_vma=False,
    )
```

```python
import functools
import math

import jax
import jax.numpy as jnp
from jax import lax
from jax.experimental import pallas as pl
from jax.experimental.pallas import tpu as pltpu
from jax.sharding import PartitionSpec as P

HEADS = 2
LANES = 128
GROUP = 32
BF = jnp.bfloat16
F32 = jnp.float32
VMEM_LIMIT = 60 * 1024 * 1024
RESIDENT_LIMIT = 20 * 1024 * 1024
NT = (((1,), (1,)), ((), ()))
TN = (((0,), (0,)), ((), ()))


def mm(a, b):
    return jnp.dot(a, b, preferred_element_type=F32)


def mm_nt(a, b):
    return lax.dot_general(a, b, NT, preferred_element_type=F32)


def mm_tn(a, b):
    return lax.dot_general(a, b, TN, preferred_element_type=F32)


def halves(table):
    high = table.astype(BF)
    low = (table - high.astype(F32)).astype(BF)
    return high, low


def reduce_kernel(
    line,
    side,
    strands,
    factor,
    grads,
    result,
    near,
    pair,
    first_land,
    first_sum,
    second_land,
    second_sum,
    line_land,
    pair_send,
    pair_recv,
    first_send,
    first_recv,
    second_send,
    second_recv,
    line_send,
    line_recv,
    line_back_send,
    line_back_recv,
    second_back_send,
    second_back_recv,
    first_back_send,
    first_back_recv,
    hop_send,
    hop_recv,
):
    me = lax.axis_index("node")
    core = lax.rem(me, 2)
    chip = me // 2
    partner = me + 1 - 2 * core
    low, mid, far = lax.rem(chip, side), lax.rem(chip // side, side), chip // (side * side)
    first = (1 - core) * low + core * mid
    second = (1 - core) * mid + core * low
    first_stride = 2 * (1 + core * (side - 1))
    second_stride = 2 * (side - core * (side - 1))
    half = grads.shape[0] // 2
    rows = half // strands
    rows_a = rows // side
    rows_b = rows_a // side
    rows_z = rows_b // line
    mesh_id = pl.DeviceIdType.MESH

    firsts = [lax.rem(first + step, side) for step in range(1, side)]
    seconds = [lax.rem(second + step, side) for step in range(1, side)]
    fars = [lax.rem(far + step, line) for step in range(1, line)]

    def first_device(place):
        return me + (place - first) * first_stride

    def second_device(place):
        return me + (place - second) * second_stride

    def far_device(place):
        return me + (place - far) * (2 * side * side)

    everyone = (
        [partner]
        + [first_device(place) for place in firsts]
        + [second_device(place) for place in seconds]
        + [far_device(place) for place in fars]
    )
    barrier = pltpu.get_barrier_semaphore()
    for device in everyone:
        pl.semaphore_signal(barrier, inc=1, device_id=(device,), device_id_type=mesh_id)
    pl.semaphore_wait(barrier, len(everyone))

    def span(start, size):
        return pl.ds(pl.multiple_of(start, 16), size)

    def remote(src, dst, send, recv, device):
        return pltpu.make_async_remote_copy(
            src_ref=src,
            dst_ref=dst,
            send_sem=send,
            recv_sem=recv,
            device_id=(device,),
            device_id_type=mesh_id,
        )

    def swap(s):
        return remote(
            grads.at[span((1 - core) * half + s * rows, rows)],
            near.at[span(s * rows, rows)],
            pair_send.at[s],
            pair_recv.at[s],
            partner,
        )

    def to_first(s, place, source):
        return remote(
            pair.at[span(s * rows + place * rows_a, rows_a)],
            first_land.at[span(s * rows + source * rows_a, rows_a)],
            first_send.at[s, place],
            first_recv.at[s, source],
            first_device(place),
        )

    def to_second(s, place, source):
        return remote(
            first_sum.at[span(s * rows_a + place * rows_b, rows_b)],
            second_land.at[span(s * rows_a + source * rows_b, rows_b)],
            second_send.at[s, place],
            second_recv.at[s, source],
            second_device(place),
        )

    def to_far(s, place, source):
        return remote(
            second_sum.at[span(s * rows_b + place * rows_z, rows_z)],
            line_land.at[span(s * rows_b + source * rows_z, rows_z)],
            line_send.at[s, place],
            line_recv.at[s, source],
            far_device(place),
        )

    def place_of(which, s, a, b=0, f=0):
        return which * half + s * rows + a * rows_a + b * rows_b + f * rows_z

    def spread(at, send, recv, device):
        return remote(result.at[at], result.at[at], send, recv, device)

    def back_far(s, place, source):
        at = span(place_of(core, s, first, second, source), rows_z)
        return spread(at, line_back_send.at[s, place], line_back_recv.at[s, source], far_device(place))

    def back_second(s, place, source):
        at = span(place_of(core, s, first, source), rows_b)
        return spread(
            at, second_back_send.at[s, place], second_back_recv.at[s, source], second_device(place)
        )

    def back_first(s, place, source):
        at = span(place_of(core, s, source), rows_a)
        return spread(
            at, first_back_send.at[s, place], first_back_recv.at[s, source], first_device(place)
        )

    def hop(s, source, which):
        at = span(place_of(which, s, source), rows_a)
        return spread(at, hop_send.at[s, source], hop_recv.at[s, source], partner)

    started = []

    def start(made):
        made.start()
        started.append(made)

    def stage_pair(s):
        swap(s).wait_recv()
        at = span(s * rows, rows)
        own = grads[span(core * half + s * rows, rows), :]
        pair[at, :] = (own.astype(F32) + near[at, :].astype(F32)).astype(BF)
        for place in firsts:
            start(to_first(s, place, first))

    def stage_first(s):
        total = pair[span(s * rows + first * rows_a, rows_a), :].astype(F32)
        for place in firsts:
            to_first(s, place, place).wait_recv()
            total += first_land[span(s * rows + place * rows_a, rows_a), :].astype(F32)
        first_sum[span(s * rows_a, rows_a), :] = total.astype(BF)
        for place in seconds:
            start(to_second(s, place, second))

    def stage_second(s):
        total = first_sum[span(s * rows_a + second * rows_b, rows_b), :].astype(F32)
        for place in seconds:
            to_second(s, place, place).wait_recv()
            total += second_land[span(s * rows_a + place * rows_b, rows_b), :].astype(F32)
        second_sum[span(s * rows_b, rows_b), :] = total.astype(BF)
        for place in fars:
            start(to_far(s, place, far))

    def stage_line(s):
        total = second_sum[span(s * rows_b + far * rows_z, rows_z), :].astype(F32)
        for place in fars:
            to_far(s, place, place).wait_recv()
            total += line_land[span(s * rows_b + place * rows_z, rows_z), :].astype(F32)
        result[span(place_of(core, s, first, second, far), rows_z), :] = (total * factor).astype(BF)
        for place in fars:
            start(back_far(s, place, far))

    def stage_back_line(s):
        for place in fars:
            back_far(s, place, place).wait_recv()
        for place in seconds:
            start(back_second(s, place, second))

    def stage_back_second(s):
        for place in seconds:
            back_second(s, place, place).wait_recv()
        for place in firsts:
            start(back_first(s, place, first))
        start(hop(s, first, core))

    def stage_back_first(s):
        for place in firsts:
            back_first(s, place, place).wait_recv()
            start(hop(s, place, core))

    for s in range(strands):
        start(swap(s))
    for s in range(strands):
        stage_pair(s)
    stages = [
        stage_first,
        stage_second,
        stage_line,
        stage_back_line,
        stage_back_second,
        stage_back_first,
    ]
    for step in range(strands + len(stages) - 1):
        for number, stage in enumerate(stages):
            if 0 <= step - number < strands:
                stage(step - number)
    for s in range(strands):
        for place in [first] + firsts:
            hop(s, place, 1 - core).wait_recv()
    for made in started:
        made.wait_send()


def gather_blocks(
    line,
    side,
    subs,
    own,
    whole,
    recv,
    hop_recv,
    line_send,
    first_send,
    second_send,
    hop_send,
    own_sem,
    prepare,
):
    me = lax.axis_index("node")
    core = lax.rem(me, 2)
    chip = me // 2
    partner = me + 1 - 2 * core
    low, mid, far = lax.rem(chip, side), lax.rem(chip // side, side), chip // (side * side)
    first = (1 - core) * low + core * mid
    second = (1 - core) * mid + core * low
    first_stride = 1 + core * (side - 1)
    second_stride = side - core * (side - 1)
    plane = side * side
    rows = own.shape[0]
    size = rows // subs
    mesh_id = pl.DeviceIdType.MESH

    def chip_of(place, over, across):
        return (
            place * plane
            + lax.rem(first + over, side) * first_stride
            + lax.rem(second + across, side) * second_stride
        )

    first_peers = [2 * chip_of(far, step, 0) + core for step in range(1, side)]
    second_peers = [2 * chip_of(far, 0, step) + core for step in range(1, side)]

    def at(source, part, kind):
        return pl.ds(pl.multiple_of((2 * source + kind) * rows + part * size, 16), size)

    def piece(source, part, kind, mine):
        return own.at[pl.ds(part * size, size)] if mine else whole.at[at(source, part, kind)]

    def copy(source, part, mine, send_sem, device):
        return pltpu.make_async_remote_copy(
            src_ref=piece(source, part, core, mine),
            dst_ref=whole.at[at(source, part, core)],
            send_sem=send_sem,
            recv_sem=recv.at[source * subs + part],
            device_id=(device,),
            device_id_type=mesh_id,
        )

    def hop(source, part, mine, kind):
        return pltpu.make_async_remote_copy(
            src_ref=piece(source, part, kind, mine),
            dst_ref=whole.at[at(source, part, kind)],
            send_sem=hop_send.at[source * subs + part],
            recv_sem=hop_recv.at[source * subs + part],
            device_id=(partner,),
            device_id_type=mesh_id,
        )

    def along(place, part, mine, way):
        return copy(
            chip_of(place, 0, 0),
            part,
            mine,
            line_send.at[place * subs + part, way],
            me + (1 - 2 * way) * 2 * plane,
        )

    def over_first(place, part, mine, to):
        return copy(
            chip_of(place, 0, 0), part, mine, first_send.at[place * subs + part, to], first_peers[to]
        )

    def over_second(place, over, part, mine, to):
        return copy(
            chip_of(place, over, 0),
            part,
            mine,
            second_send.at[place * subs + part, over, to],
            second_peers[to],
        )

    def landed(source, part):
        copy(source, part, False, hop_send.at[0], partner).wait_recv()

    stay = pltpu.make_async_copy(own, whole.at[pl.ds(pl.multiple_of(me * rows, 16), rows)], own_sem)

    def arrive(place, part, mine, ways):
        source = chip_of(place, 0, 0)
        if mine:
            prepare(part)
        else:
            landed(source, part)
        for way in ways:
            open_end = far < line - 1 if way == 0 else far > 0

            @pl.when(open_end)
            def _(way=way):
                along(place, part, mine, way).start()

        for to in range(side - 1):
            over_first(place, part, mine, to).start()
        for to in range(side - 1):
            over_second(place, 0, part, mine, to).start()
        hop(source, part, mine, core).start()
        if mine and part == subs - 1:
            stay.start()

    def pass_on(place, part):
        for over in range(1, side):
            source = chip_of(place, over, 0)
            landed(source, part)
            for to in range(side - 1):
                over_second(place, over, part, False, to).start()
            hop(source, part, False, core).start()

    def finish(place, part):
        for across in range(1, side):
            for over in range(side):
                source = chip_of(place, over, across)
                landed(source, part)
                hop(source, part, False, core).start()

    units = [(0, 0)] + [(reach, way) for reach in range(1, line) for way in range(2)]
    work = [(reach, way, part) for reach, way in units for part in range(subs)]

    def run(item, stage):
        reach, way, part = item
        place = far - reach if way == 0 else far + reach

        def body():
            if stage == 0:
                arrive(place, part, reach == 0, (0, 1) if reach == 0 else (way,))
            elif stage == 1:
                pass_on(place, part)
            else:
                finish(place, part)

        if reach == 0:
            body()
        else:
            pl.when(place >= 0 if way == 0 else place < line)(body)

    lags = (0, 3, 6)
    for step in range(len(work) + lags[-1]):
        for stage, lag in enumerate(lags):
            if 0 <= step - lag < len(work):
                run(work[step - lag], stage)
    stay.wait()

    def drain(place, carry):
        for part in range(subs):
            for to in range(side - 1):
                over_first(place, part, False, to).wait_send()
                for over in range(side):
                    over_second(place, over, part, False, to).wait_send()

            @pl.when((place <= far) & (far < line - 1))
            def _(part=part):
                along(place, part, False, 0).wait_send()

            @pl.when((place >= far) & (far > 0))
            def _(part=part):
                along(place, part, False, 1).wait_send()

            for over in range(side):
                for across in range(side):
                    hop(chip_of(place, over, across), part, False, core).wait_send()
        return carry

    lax.fori_loop(0, line, drain, 0)

    def drain_hops(source, carry):
        for part in range(subs):
            hop(source, part, False, 1 - core).wait_recv()
        return carry

    lax.fori_loop(0, line * plane, drain_hops, 0)


def front_kernel(
    devices,
    slots,
    line,
    side,
    subs,
    node,
    bucket,
    feats,
    memory,
    edge_weight,
    time_message,
    input_weight,
    hidden_weight,
    gate_bias,
    out_memory,
    whole,
    outgoing,
    inbox,
    sel,
    meta,
    hidden,
    picked,
    picked_meta,
    totals,
    counts,
    wide,
    table,
    send_sems,
    recv_sems,
    *gather_sems,
):
    me = lax.axis_index("node")
    events = feats.shape[0]
    rows, columns = memory.shape
    stride = columns // LANES
    batch = 4
    mesh_id = pl.DeviceIdType.MESH
    barrier = pltpu.get_barrier_semaphore()

    def greet(step, carry):
        pl.semaphore_signal(
            barrier, inc=1, device_id=(lax.rem(me + step, devices),), device_id_type=mesh_id
        )
        return carry

    lax.fori_loop(1, devices, greet, 0)

    ids = lax.broadcasted_iota(jnp.int32, (devices, events), 0) * rows
    names = node[...]
    theirs = (names >= ids) & (names < ids + rows)
    before = lax.broadcasted_iota(jnp.int32, (events, events), 0) < lax.broadcasted_iota(
        jnp.int32, (events, events), 1
    )
    rank = mm(theirs.astype(F32).astype(BF), before.astype(F32).astype(BF))
    sel[...] = jnp.where(theirs, rank, -1.0)
    within = jnp.sum(jnp.where(theirs, names - ids, 0).astype(F32), axis=0, keepdims=True)
    kind = lax.broadcasted_iota(jnp.int32, (16, events), 0)
    meta[...] = jnp.where(
        kind == 0,
        within,
        jnp.where(kind == 1, bucket[...].astype(F32), jnp.where(kind == 2, 1.0, 0.0)),
    ).astype(BF)
    slot_ids = lax.broadcasted_iota(jnp.int32, (slots, events), 0).astype(F32)
    lane_ids = lax.broadcasted_iota(jnp.int32, (LANES, events), 0).astype(F32)
    pl.semaphore_wait(barrier, devices - 1)

    def send(peer):
        return pltpu.make_async_remote_copy(
            src_ref=outgoing.at[peer],
            dst_ref=inbox.at[me],
            send_sem=send_sems.at[peer],
            recv_sem=recv_sems.at[me],
            device_id=(peer,),
            device_id_type=mesh_id,
        )

    def receive(peer):
        return pltpu.make_async_remote_copy(
            src_ref=outgoing.at[peer],
            dst_ref=inbox.at[peer],
            send_sem=send_sems.at[peer],
            recv_sem=recv_sems.at[peer],
            device_id=(peer,),
            device_id_type=mesh_id,
        )

    def pack(peer):
        row = sel[pl.ds(peer, 1), :]
        hits = (slot_ids == row).astype(F32).astype(BF)
        turned = (lane_ids == row).astype(F32).astype(BF)
        return mm(hits, feats[...]).astype(BF), mm_nt(meta[...], turned).astype(BF)

    def pack_batch(step, own):
        for part in range(batch):
            peer = lax.rem(me + step * batch + part, devices)
            rows_of, info = pack(peer)
            if own and part == 0:
                inbox[me, :slots, :] = rows_of
                inbox[me, slots:, :] = info
            else:
                outgoing[peer, :slots, :] = rows_of
                outgoing[peer, slots:, :] = info
                send(peer).start()

    pack_batch(0, True)

    def pack_rest(step, carry):
        pack_batch(step, False)
        return carry

    lax.fori_loop(1, devices // batch, pack_rest, 0)

    previous = memory[...]
    for part in range(3):
        cut = slice(part * columns, (part + 1) * columns)
        hidden[:, cut] = mm(previous, hidden_weight[:, cut])
    totals[...] = jnp.zeros_like(totals)
    counts[...] = jnp.zeros_like(counts)
    high, low = halves(time_message[...])
    weight = edge_weight[...]
    turn = (
        lax.broadcasted_iota(jnp.int32, (slots, LANES), 0)
        == lax.broadcasted_iota(jnp.int32, (slots, LANES), 1)
    ).astype(F32).astype(BF)
    chunk = batch * slots

    def add_batch(step, own):
        for part in range(batch):
            peer = lax.rem(me + devices - step * batch - part, devices)
            if not (own and part == 0):
                receive(peer).wait_recv()
            at = slice(part * slots, (part + 1) * slots)
            picked[at, :] = inbox[peer, :slots, :]
            picked_meta[at, :] = mm_nt(turn, inbox[peer, slots:, :])
        info = picked_meta[...]
        place, when, valid = info[:, 0:1], info[:, 1:2], info[:, 2:3]
        lanes = lax.broadcasted_iota(jnp.int32, (chunk, high.shape[0]), 1).astype(F32)
        picks = (lanes == when).astype(F32).astype(BF)
        pre = mm(picked[...], weight) + mm(picks, high) + mm(picks, low)
        message = (pre / (1.0 + jnp.exp(-pre))).astype(BF)
        node_ids = lax.broadcasted_iota(jnp.int32, (chunk, rows), 1).astype(F32)
        marks = jnp.where(node_ids == place, valid, 0.0).astype(BF)
        totals[...] += mm_tn(marks, message)
        counts[...] += mm_tn(marks, jnp.ones((chunk, LANES), BF))

    add_batch(0, True)

    def add_rest(step, carry):
        add_batch(step, False)
        return carry

    lax.fori_loop(1, devices // batch, add_rest, 0)

    def prepare(part):
        size = rows // subs
        at = slice(part * size, (part + 1) * size)
        count = counts[at, 0:1]
        aggregate = (totals[at, :] / jnp.maximum(count, 1.0)).astype(BF)

        def gate(which):
            cut = slice(which * columns, (which + 1) * columns)
            bias = jnp.concatenate(
                [gate_bias[which * stride + p : which * stride + p + 1, :] for p in range(stride)],
                axis=1,
            )
            return mm(aggregate, input_weight[:, cut]) + bias, hidden[at, cut]

        from_input, from_hidden = gate(0)
        update = jax.nn.sigmoid(from_input + from_hidden)
        from_input, from_hidden = gate(1)
        resets = jax.nn.sigmoid(from_input + from_hidden)
        from_input, from_hidden = gate(2)
        candidate = jnp.tanh(from_input + resets * from_hidden)
        old = memory[at, :].astype(F32)
        fresh = (1.0 - update) * candidate + update * old
        fresh = jnp.where(count > 0, fresh, old)
        out_memory[at, :] = fresh.astype(BF)
        first = part * size * stride
        for p in range(stride):
            wide[pl.ds(first + p, size, stride=stride), :] = fresh[:, p * LANES : (p + 1) * LANES]
        at = slice(first, first + size * stride)
        table[at, :] = wide[at, :].astype(BF)

    gather_blocks(line, side, subs, table, whole, *gather_sems, prepare)

    def drain(step, carry):
        send(lax.rem(me + step, devices)).wait_send()
        return carry

    lax.fori_loop(1, devices, drain, 0)


def event_kernel(
    resident,
    events,
    fanout,
    ids,
    own_ids,
    source,
    buckets,
    affinity,
    upstream,
    time_key,
    query_weight,
    key_weight,
    value_weight,
    out_weight,
    embedding,
    grads,
    *scratch,
):
    columns = upstream.shape[1]
    head = columns // HEADS
    stride = columns // LANES
    kinds = 2 * HEADS
    blocks = events // GROUP
    wide = fanout * GROUP
    tall = 2 * kinds * GROUP
    if resident:
        landing, table, near, sems, *scratch = scratch
        parts = sems.shape[0]
        size = landing.shape[0] // parts
        copies = []
        for part in range(parts):
            at = pl.ds(part * size, size)
            copies.append(pltpu.make_async_copy(source.at[at], landing.at[at], sems.at[part]))
            copies[-1].start()
    else:
        near, sem, *scratch = scratch
        picks = (fanout + 1) * events

        def request(start, row):
            pltpu.make_async_copy(
                source.at[pl.ds(pl.multiple_of(start * stride, stride), stride)],
                near.at[pl.ds(pl.multiple_of(row * stride, stride), stride)],
                sem,
            ).start()

        def request_all(e, carry):
            for j in range(fanout):
                request(ids[j, e], j * events + e)
            request(own_ids[e], fanout * events + e)
            return carry

        lax.fori_loop(0, events, request_all, 0)
    target, query, back, pull, pull_time, mix, hits, scores, close, hot, names, logits = scratch
    heads = [slice(h * head, (h + 1) * head) for h in range(HEADS)]
    high, low = halves(time_key[...])

    def keep(dest, kind, values):
        upper, lower = halves(values)
        for b in range(blocks):
            rows = slice(b * GROUP, (b + 1) * GROUP)
            first = b * tall + kind * GROUP
            dest[first : first + GROUP, :] = upper[rows, :]
            first += kinds * GROUP
            dest[first : first + GROUP, :] = lower[rows, :]

    back[...] = mm_nt(upstream[...], out_weight[...]).astype(BF)
    for h, cut in enumerate(heads):
        keep(pull, HEADS + h, mm_nt(back[:, cut], value_weight[:, cut]))
        keep(pull_time, HEADS + h, jnp.zeros((events, LANES), F32))
    even = (
        lax.broadcasted_iota(jnp.int32, (fanout, LANES), 0)
        == lax.broadcasted_iota(jnp.int32, (fanout, LANES), 1)
    ).astype(F32).astype(BF)
    names[...] = mm_tn(buckets[...].astype(F32).astype(BF), even)
    logits[...] = jnp.zeros_like(logits)
    logits[:fanout, :] = affinity[...]
    lane = lax.broadcasted_iota(jnp.int32, (GROUP, LANES), 1)
    lane_names = lane.astype(F32)

    def mark(b, carry):
        mine = names[pl.ds(pl.multiple_of(b * GROUP, GROUP), GROUP), :]
        for j in range(fanout):
            at = pl.ds(pl.multiple_of(b * wide + j * GROUP, GROUP), GROUP)
            hot[at, :] = (lane_names == mine[:, j : j + 1]).astype(F32).astype(BF)
        return carry

    lax.fori_loop(0, blocks, mark, 0)

    if resident:
        step_rows = 256
        for part in range(parts):
            copies[part].wait()

            def widen(step, carry, part=part):
                at = pl.ds(pl.multiple_of(part * size + step * step_rows, step_rows), step_rows)
                table[at, :] = landing[at, :].astype(F32)
                return carry

            lax.fori_loop(0, size // step_rows, widen, 0)

        def fetch(start, row):
            near[pl.ds(pl.multiple_of(row * stride, stride), stride), :] = table[
                pl.ds(pl.multiple_of(start * stride, stride), stride), :
            ]

        unroll = 16

        def fetch_own(step, carry):
            for place in range(unroll):
                e = step * unroll + place
                fetch(own_ids[e], fanout * events + e)
            return carry

        def fetch_near(step, carry):
            for place in range(2):
                e = step * 2 + place
                for j in range(fanout):
                    fetch(ids[j, e], j * events + e)
            return carry

        lax.fori_loop(0, events // unroll, fetch_own, 0)
        lax.fori_loop(0, events // 2, fetch_near, 0)
    else:
        pltpu.make_async_copy(source.at[pl.ds(0, picks * stride)], near, sem).wait()

    for part in range(stride):
        target[:, part * LANES : (part + 1) * LANES] = near[
            pl.ds(fanout * events * stride + part, events, stride=stride), :
        ].astype(BF)
    query[...] = mm(target[...], query_weight[...]).astype(BF)
    for h, cut in enumerate(heads):
        keep(pull, h, mm_nt(query[:, cut], key_weight[:, cut]))
        keep(pull_time, h, mm_nt(query[:, cut], high[:, cut]) + mm_nt(query[:, cut], low[:, cut]))

    scale = 1.0 / math.sqrt(head)
    pad = scores.shape[0] // blocks
    own = lax.rem(lane, GROUP) == lax.broadcasted_iota(jnp.int32, (GROUP, LANES), 0)
    row_ids = lax.broadcasted_iota(jnp.int32, (pad, LANES), 0)
    lane_ids = lax.broadcasted_iota(jnp.int32, (pad, LANES), 1)
    forward = lane_ids < HEADS * GROUP
    per_row = LANES // GROUP

    def score(b):
        first = b * GROUP
        for j in range(fanout):
            at = pl.ds(pl.multiple_of(b * wide + j * GROUP, GROUP), GROUP)
            for part in range(stride):
                close[at, part * LANES : (part + 1) * LANES] = near[
                    pl.ds((j * events + first) * stride + part, GROUP, stride=stride), :
                ].astype(BF)
        at = pl.ds(pl.multiple_of(b * wide, GROUP), wide)
        from_at = pl.ds(pl.multiple_of(b * tall, GROUP), tall)
        both = mm_nt(close[at, :], pull[from_at, :]) + mm_nt(hot[at, :], pull_time[from_at, :])
        both = both[:, :LANES] + both[:, LANES:]
        raw = jnp.zeros((pad, LANES), F32)
        for j in range(fanout):
            line = jnp.where(own, both[j * GROUP : (j + 1) * GROUP, :], 0.0)
            raw = jnp.where(row_ids == j, jnp.sum(line, axis=0, keepdims=True), raw)
        chunk = pl.multiple_of(b // per_row * LANES, LANES)
        piece = logits[:, pl.ds(chunk, LANES)]
        piece = pltpu.roll(piece, lax.rem(LANES - lax.rem(b, per_row) * GROUP, LANES), axis=1)
        given = piece
        for h in range(1, HEADS):
            moved = pltpu.roll(piece, h * GROUP, axis=1)
            given = jnp.where(lane_ids >= h * GROUP, moved, given)
        scores[pl.ds(pl.multiple_of(b * pad, pad), pad), :] = jnp.where(
            forward, raw * scale + given, raw
        )

    def score_two(step, carry):
        for place in range(2):
            score(step * 2 + place)
        return carry

    lax.fori_loop(0, blocks // 2, score_two, 0)

    for b in range(blocks):
        at = slice(b * pad, (b + 1) * pad)
        here = scores[at, :]
        active = row_ids < fanout
        top = jnp.max(jnp.where(active, here, -3.0e38), axis=0, keepdims=True)
        raised = jnp.where(active, jnp.exp(jnp.where(active, here - top, 0.0)), 0.0)
        probs = raised / jnp.sum(raised, axis=0, keepdims=True)
        slopes = pltpu.roll(here, HEADS * GROUP, axis=1).astype(BF).astype(F32)
        inner = jnp.sum(probs * slopes, axis=0, keepdims=True)
        slopes = probs * (slopes - inner) * scale
        scores[at, :] = jnp.where(forward, probs, pltpu.roll(slopes, HEADS * GROUP, axis=1))

    def blend(b):
        weights = scores[pl.ds(pl.multiple_of(b * pad, pad), pad), :]
        spread = jnp.concatenate(
            [
                jnp.where(own, jnp.broadcast_to(weights[j : j + 1, :], (GROUP, LANES)), 0.0)
                for j in range(fanout)
            ],
            axis=0,
        ).astype(BF)
        at = pl.ds(pl.multiple_of(b * wide, GROUP), wide)
        mixed = mm_tn(spread, close[at, :]).astype(BF)
        times = mm_tn(spread, hot[at, :]).astype(BF)
        to = pl.ds(pl.multiple_of(b * GROUP, GROUP), GROUP)
        for k in range(kinds):
            mix[k, to, :] = mixed[k * GROUP : (k + 1) * GROUP, :]
        for h in range(HEADS):
            hits[h, to, :] = times[(HEADS + h) * GROUP : (HEADS + h + 1) * GROUP, :]

    def blend_two(step, carry):
        for place in range(2):
            blend(step * 2 + place)
        return carry

    lax.fori_loop(0, blocks // 2, blend_two, 0)

    for h, cut in enumerate(heads):
        grads[2 * columns : 3 * columns, cut] = mm_tn(mix[h], back[:, cut]).astype(BF)
        grads[columns : 2 * columns, cut] = mm_tn(mix[HEADS + h], query[:, cut]).astype(BF)
    for h, cut in enumerate(heads):
        back[:, cut] = mm(mix[h], value_weight[:, cut]).astype(BF)
        query[:, cut] = (
            mm(mix[HEADS + h], key_weight[:, cut])
            + mm(hits[h], high[:, cut])
            + mm(hits[h], low[:, cut])
        ).astype(BF)
    grads[:columns, :] = mm_tn(target[...], query[...]).astype(BF)
    grads[3 * columns :, :] = mm_tn(back[...], upstream[...]).astype(BF)
    embedding[...] = (mm(back[...], out_weight[...]) + target[...].astype(F32)).astype(BF)


def shards(
    event_node,
    neighbours,
    event_bucket,
    neighbour_bucket,
    edge_features,
    affinity,
    upstream,
    node_memory,
    edge_weight,
    time_message,
    input_weight,
    hidden_weight,
    gate_bias,
    time_key,
    query_weight,
    key_weight,
    value_weight,
    out_weight,
):
    devices = lax.axis_size("node")
    node_rows, columns = node_memory.shape
    events, fanout = neighbours.shape
    features = edge_features.shape[1]
    stride = columns // LANES
    slots = -(-(3 * events // devices) // 16) * 16
    vmem = pl.BlockSpec(memory_space=pltpu.VMEM)
    smem = pl.BlockSpec(memory_space=pltpu.SMEM)

    chips = devices // 2
    side = max(s for s in range(1, chips + 1) if chips % (s * s) == 0 and s**3 <= chips)
    line = chips // (side * side)
    subs = 2
    batch_rows = 4 * slots
    dma = pltpu.SemaphoreType.DMA
    new_memory, whole = pl.pallas_call(
        functools.partial(front_kernel, devices, slots, line, side, subs),
        out_shape=(
            jax.ShapeDtypeStruct((node_rows, columns), BF),
            jax.ShapeDtypeStruct((devices * node_rows * stride, LANES), BF),
        ),
        in_specs=[vmem] * 9,
        out_specs=(vmem, pl.BlockSpec(memory_space=pl.ANY)),
        scratch_shapes=[
            pltpu.VMEM((devices, slots + 16, features), BF),
            pltpu.VMEM((devices, slots + 16, features), BF),
            pltpu.VMEM((devices, events), F32),
            pltpu.VMEM((16, events), BF),
            pltpu.VMEM((node_rows, 3 * columns), F32),
            pltpu.VMEM((batch_rows, features), BF),
            pltpu.VMEM((batch_rows, 16), F32),
            pltpu.VMEM((node_rows, columns), F32),
            pltpu.VMEM((node_rows, LANES), F32),
            pltpu.VMEM((node_rows * stride, LANES), F32),
            pltpu.VMEM((node_rows * stride, LANES), BF),
            dma((devices,)),
            dma((devices,)),
            dma((chips * subs,)),
            dma((chips * subs,)),
            dma((line * subs, 2)),
            dma((line * subs, side - 1)),
            dma((line * subs, side, side - 1)),
            dma((chips * subs,)),
            dma,
        ],
        compiler_params=pltpu.CompilerParams(
            collective_id=0, has_side_effects=True, vmem_limit_bytes=VMEM_LIMIT
        ),
        name="front_step",
    )(
        event_node.reshape(1, events),
        event_bucket.reshape(1, events),
        edge_features,
        node_memory,
        edge_weight,
        time_message,
        input_weight,
        hidden_weight,
        gate_bias.reshape(-1, LANES),
    )

    resident = whole.size * 4 <= RESIDENT_LIMIT
    near_rows = (fanout + 1) * events * stride
    if resident:
        source = whole
        source_spec = pl.BlockSpec(memory_space=pl.ANY)
        extra = [
            pltpu.VMEM(whole.shape, BF),
            pltpu.VMEM(whole.shape, F32),
            pltpu.VMEM((near_rows, LANES), F32),
            pltpu.SemaphoreType.DMA((8,)),
        ]
    else:
        source = whole.astype(F32)
        source_spec = pl.BlockSpec(memory_space=pl.ANY)
        extra = [pltpu.VMEM((near_rows, LANES), F32), pltpu.SemaphoreType.DMA]
    embedding, grads = pl.pallas_call(
        functools.partial(event_kernel, resident, events, fanout),
        out_shape=(
            jax.ShapeDtypeStruct((events, columns), BF),
            jax.ShapeDtypeStruct((4 * columns, columns), BF),
        ),
        in_specs=[smem, smem, source_spec] + [vmem] * 8,
        out_specs=(vmem, vmem),
        scratch_shapes=extra
        + [
            pltpu.VMEM((events, columns), BF),
            pltpu.VMEM((events, columns), BF),
            pltpu.VMEM((events, columns), BF),
            pltpu.VMEM((4 * HEADS * events, columns), BF),
            pltpu.VMEM((4 * HEADS * events, LANES), BF),
            pltpu.VMEM((2 * HEADS, events, columns), BF),
            pltpu.VMEM((HEADS, events, LANES), BF),
            pltpu.VMEM((events // GROUP * 16, LANES), F32),
            pltpu.VMEM((fanout * events, columns), BF),
            pltpu.VMEM((fanout * events, LANES), BF),
            pltpu.VMEM((events, LANES), F32),
            pltpu.VMEM((16, events), F32),
        ],
        compiler_params=pltpu.CompilerParams(vmem_limit_bytes=VMEM_LIMIT),
        name="event_step",
    )(
        neighbours.T,
        event_node,
        source,
        neighbour_bucket.T,
        affinity.T,
        upstream,
        time_key,
        query_weight,
        key_weight,
        value_weight,
        out_weight,
    )
    factor = 1.0 / math.sqrt(events * devices)
    half = 2 * columns
    strands = max(1, min(4, half // (16 * chips)))
    total = pl.pallas_call(
        functools.partial(reduce_kernel, line, side, strands, factor),
        out_shape=jax.ShapeDtypeStruct((2 * half, columns), BF),
        in_specs=[vmem],
        out_specs=vmem,
        scratch_shapes=[
            pltpu.VMEM((half, columns), BF),
            pltpu.VMEM((half, columns), BF),
            pltpu.VMEM((half, columns), BF),
            pltpu.VMEM((half // side, columns), BF),
            pltpu.VMEM((half // side, columns), BF),
            pltpu.VMEM((half // (side * side), columns), BF),
            pltpu.VMEM((half // (side * side), columns), BF),
            pltpu.SemaphoreType.DMA((strands,)),
            pltpu.SemaphoreType.DMA((strands,)),
        ]
        + [
            pltpu.SemaphoreType.DMA((strands, places))
            for places in (side, side, line, line, side, side, side)
            for _ in range(2)
        ],
        compiler_params=pltpu.CompilerParams(
            collective_id=1, has_side_effects=True, vmem_limit_bytes=VMEM_LIMIT
        ),
        name="reduce_step",
    )(grads).astype(F32)
    return (embedding, new_memory) + tuple(
        total[part * columns : (part + 1) * columns] for part in range(4)
    )


def solution(mesh):
    placed = (
        P("node"),
        P("node", None),
        P("node"),
        P("node", None),
        P("node", None),
        P("node", None),
        P("node", None),
        P("node", None),
        P(),
        P(),
        P(),
        P(),
        P(),
        P(),
        P(),
        P(),
        P(),
        P(),
    )
    return jax.shard_map(
        shards,
        mesh=mesh,
        in_specs=placed,
        out_specs=(P("node", None), P("node", None), P(), P(), P(), P()),
        check_vma=False,
    )
```

```python
import functools
import math

import jax
import jax.numpy as jnp
from jax import lax
from jax.experimental import pallas as pl
from jax.experimental.pallas import tpu as pltpu
from jax.sharding import PartitionSpec as P

HEADS = 2
LANES = 128
GROUP = 32
BF = jnp.bfloat16
F32 = jnp.float32
VMEM_LIMIT = 60 * 1024 * 1024
RESIDENT_LIMIT = 20 * 1024 * 1024
NT = (((1,), (1,)), ((), ()))
TN = (((0,), (0,)), ((), ()))


def mm(a, b):
    return jnp.dot(a, b, preferred_element_type=F32)


def mm_nt(a, b):
    return lax.dot_general(a, b, NT, preferred_element_type=F32)


def mm_tn(a, b):
    return lax.dot_general(a, b, TN, preferred_element_type=F32)


def halves(table):
    high = table.astype(BF)
    low = (table - high.astype(F32)).astype(BF)
    return high, low


def reduce_phase(line, side, strands, factor, r, meet, steps):
    (grads, result, near, pair) = (r.grads, r.result, r.swapped, r.pair)
    (first_land, first_sum) = (r.first_land, r.first_sum)
    (second_land, second_sum, line_land) = (r.second_land, r.second_sum, r.line_land)
    (pair_send, pair_recv) = (r.pair_send, r.pair_recv)
    (first_send, first_recv, second_send, second_recv, line_send, line_recv) = r.out_sems
    (line_back_send, line_back_recv, second_back_send, second_back_recv) = r.back_sems[:4]
    (first_back_send, first_back_recv, hop_send, hop_recv) = r.back_sems[4:]
    me = lax.axis_index("node")
    core = lax.rem(me, 2)
    chip = me // 2
    partner = me + 1 - 2 * core
    low, mid, far = lax.rem(chip, side), lax.rem(chip // side, side), chip // (side * side)
    first = (1 - core) * low + core * mid
    second = (1 - core) * mid + core * low
    first_stride = 2 * (1 + core * (side - 1))
    second_stride = 2 * (side - core * (side - 1))
    half = grads.shape[0] // 2
    rows = half // strands
    rows_a = rows // side
    rows_b = rows_a // side
    rows_z = rows_b // line
    mesh_id = pl.DeviceIdType.MESH

    firsts = [lax.rem(first + step, side) for step in range(1, side)]
    seconds = [lax.rem(second + step, side) for step in range(1, side)]
    fars = [lax.rem(far + step, line) for step in range(1, line)]

    def first_device(place):
        return me + (place - first) * first_stride

    def second_device(place):
        return me + (place - second) * second_stride

    def far_device(place):
        return me + (place - far) * (2 * side * side)

    everyone = (
        [partner]
        + [first_device(place) for place in firsts]
        + [second_device(place) for place in seconds]
        + [far_device(place) for place in fars]
    )
    if meet:
        barrier = pltpu.get_barrier_semaphore()
        for device in everyone:
            pl.semaphore_signal(barrier, inc=1, device_id=(device,), device_id_type=mesh_id)
        pl.semaphore_wait(barrier, len(everyone))

    def span(start, size):
        return pl.ds(pl.multiple_of(start, 16), size)

    def remote(src, dst, send, recv, device):
        return pltpu.make_async_remote_copy(
            src_ref=src,
            dst_ref=dst,
            send_sem=send,
            recv_sem=recv,
            device_id=(device,),
            device_id_type=mesh_id,
        )

    def swap(s):
        return remote(
            grads.at[span((1 - core) * half + s * rows, rows)],
            near.at[span(s * rows, rows)],
            pair_send.at[s],
            pair_recv.at[s],
            partner,
        )

    def to_first(s, place, source):
        return remote(
            pair.at[span(s * rows + place * rows_a, rows_a)],
            first_land.at[span(s * rows + source * rows_a, rows_a)],
            first_send.at[s, place],
            first_recv.at[s, source],
            first_device(place),
        )

    def to_second(s, place, source):
        return remote(
            first_sum.at[span(s * rows_a + place * rows_b, rows_b)],
            second_land.at[span(s * rows_a + source * rows_b, rows_b)],
            second_send.at[s, place],
            second_recv.at[s, source],
            second_device(place),
        )

    def to_far(s, place, source):
        return remote(
            second_sum.at[span(s * rows_b + place * rows_z, rows_z)],
            line_land.at[span(s * rows_b + source * rows_z, rows_z)],
            line_send.at[s, place],
            line_recv.at[s, source],
            far_device(place),
        )

    def place_of(which, s, a, b=0, f=0):
        return which * half + s * rows + a * rows_a + b * rows_b + f * rows_z

    def spread(at, send, recv, device):
        return remote(result.at[at], result.at[at], send, recv, device)

    def back_far(s, place, source):
        at = span(place_of(core, s, first, second, source), rows_z)
        return spread(at, line_back_send.at[s, place], line_back_recv.at[s, source], far_device(place))

    def back_second(s, place, source):
        at = span(place_of(core, s, first, source), rows_b)
        return spread(
            at, second_back_send.at[s, place], second_back_recv.at[s, source], second_device(place)
        )

    def back_first(s, place, source):
        at = span(place_of(core, s, source), rows_a)
        return spread(
            at, first_back_send.at[s, place], first_back_recv.at[s, source], first_device(place)
        )

    def hop(s, source, which):
        at = span(place_of(which, s, source), rows_a)
        return spread(at, hop_send.at[s, source], hop_recv.at[s, source], partner)

    started = []

    def start(made):
        made.start()
        started.append(made)

    def stage_pair(s):
        swap(s).wait_recv()
        at = span(s * rows, rows)
        own = grads[span(core * half + s * rows, rows), :]
        pair[at, :] = (own.astype(F32) + near[at, :].astype(F32)).astype(BF)
        for place in firsts:
            start(to_first(s, place, first))

    def stage_first(s):
        total = pair[span(s * rows + first * rows_a, rows_a), :].astype(F32)
        for place in firsts:
            to_first(s, place, place).wait_recv()
            total += first_land[span(s * rows + place * rows_a, rows_a), :].astype(F32)
        first_sum[span(s * rows_a, rows_a), :] = total.astype(BF)
        for place in seconds:
            start(to_second(s, place, second))

    def stage_second(s):
        total = first_sum[span(s * rows_a + second * rows_b, rows_b), :].astype(F32)
        for place in seconds:
            to_second(s, place, place).wait_recv()
            total += second_land[span(s * rows_a + place * rows_b, rows_b), :].astype(F32)
        second_sum[span(s * rows_b, rows_b), :] = total.astype(BF)
        for place in fars:
            start(to_far(s, place, far))

    def stage_line(s):
        total = second_sum[span(s * rows_b + far * rows_z, rows_z), :].astype(F32)
        for place in fars:
            to_far(s, place, place).wait_recv()
            total += line_land[span(s * rows_b + place * rows_z, rows_z), :].astype(F32)
        result[span(place_of(core, s, first, second, far), rows_z), :] = (total * factor).astype(BF)
        for place in fars:
            start(back_far(s, place, far))

    def stage_back_line(s):
        for place in fars:
            back_far(s, place, place).wait_recv()
        for place in seconds:
            start(back_second(s, place, second))

    def stage_back_second(s):
        for place in seconds:
            back_second(s, place, place).wait_recv()
        for place in firsts:
            start(back_first(s, place, first))
        start(hop(s, first, core))

    def stage_back_first(s):
        for place in firsts:
            back_first(s, place, place).wait_recv()
            start(hop(s, place, core))

    early = strands // 2
    steps[0]()
    for s in range(early):
        start(swap(s))
    steps[1]()
    for s in range(early):
        stage_pair(s)
    steps[2]()
    for s in range(early, strands):
        start(swap(s))
    steps[3]()
    for s in range(early, strands):
        stage_pair(s)
    stages = [
        stage_first,
        stage_second,
        stage_line,
        stage_back_line,
        stage_back_second,
        stage_back_first,
    ]
    for step in range(strands + len(stages) - 1):
        for number, stage in enumerate(stages):
            if 0 <= step - number < strands:
                stage(step - number)
    for s in range(strands):
        for place in [first] + firsts:
            hop(s, place, 1 - core).wait_recv()
    for made in started:
        made.wait_send()


def gather_blocks(
    line,
    side,
    subs,
    own,
    whole,
    recv,
    hop_recv,
    line_send,
    first_send,
    second_send,
    hop_send,
    own_sem,
    prepare,
    idle,
    arrived,
):
    me = lax.axis_index("node")
    core = lax.rem(me, 2)
    chip = me // 2
    partner = me + 1 - 2 * core
    low, mid, far = lax.rem(chip, side), lax.rem(chip // side, side), chip // (side * side)
    first = (1 - core) * low + core * mid
    second = (1 - core) * mid + core * low
    first_stride = 1 + core * (side - 1)
    second_stride = side - core * (side - 1)
    plane = side * side
    rows = own.shape[0]
    size = rows // subs
    mesh_id = pl.DeviceIdType.MESH

    def chip_of(place, over, across):
        return (
            place * plane
            + lax.rem(first + over, side) * first_stride
            + lax.rem(second + across, side) * second_stride
        )

    first_peers = [2 * chip_of(far, step, 0) + core for step in range(1, side)]
    second_peers = [2 * chip_of(far, 0, step) + core for step in range(1, side)]

    def at(source, part, kind):
        return pl.ds(pl.multiple_of((2 * source + kind) * rows + part * size, 16), size)

    def piece(source, part, kind, mine):
        return own.at[pl.ds(part * size, size)] if mine else whole.at[at(source, part, kind)]

    def copy(source, part, mine, send_sem, device):
        return pltpu.make_async_remote_copy(
            src_ref=piece(source, part, core, mine),
            dst_ref=whole.at[at(source, part, core)],
            send_sem=send_sem,
            recv_sem=recv.at[source * subs + part],
            device_id=(device,),
            device_id_type=mesh_id,
        )

    def hop(source, part, mine, kind):
        return pltpu.make_async_remote_copy(
            src_ref=piece(source, part, kind, mine),
            dst_ref=whole.at[at(source, part, kind)],
            send_sem=hop_send.at[source * subs + part],
            recv_sem=hop_recv.at[source * subs + part],
            device_id=(partner,),
            device_id_type=mesh_id,
        )

    def along(place, part, mine, way):
        return copy(
            chip_of(place, 0, 0),
            part,
            mine,
            line_send.at[place * subs + part, way],
            me + (1 - 2 * way) * 2 * plane,
        )

    def over_first(place, part, mine, to):
        return copy(
            chip_of(place, 0, 0), part, mine, first_send.at[place * subs + part, to], first_peers[to]
        )

    def over_second(place, over, part, mine, to):
        return copy(
            chip_of(place, over, 0),
            part,
            mine,
            second_send.at[place * subs + part, over, to],
            second_peers[to],
        )

    def landed(source, part):
        copy(source, part, False, hop_send.at[0], partner).wait_recv()

    def settle(source, part, kind):
        if arrived is not None:
            start = pl.multiple_of((2 * source + kind) * rows + part * size, 16)
            arrived(whole, start, start, size)

    stay = None
    if arrived is None:
        mine_at = pl.ds(pl.multiple_of(me * rows, 16), rows)
        stay = pltpu.make_async_copy(own, whole.at[mine_at], own_sem)

    def arrive(place, part, mine, ways):
        source = chip_of(place, 0, 0)
        if mine:
            prepare(part)
        else:
            landed(source, part)
        for way in ways:
            open_end = far < line - 1 if way == 0 else far > 0

            @pl.when(open_end)
            def _(way=way):
                along(place, part, mine, way).start()

        for to in range(side - 1):
            over_first(place, part, mine, to).start()
        for to in range(side - 1):
            over_second(place, 0, part, mine, to).start()
        hop(source, part, mine, core).start()
        if not mine:
            settle(source, part, core)
        elif arrived is not None:
            arrived(own, part * size, pl.multiple_of(me * rows + part * size, 16), size)
        if mine and part == subs - 1:
            if stay is not None:
                stay.start()
            idle()

    def pass_on(place, part):
        for over in range(1, side):
            source = chip_of(place, over, 0)
            landed(source, part)
            for to in range(side - 1):
                over_second(place, over, part, False, to).start()
            hop(source, part, False, core).start()
            settle(source, part, core)

    def finish(place, part):
        for across in range(1, side):
            for over in range(side):
                source = chip_of(place, over, across)
                landed(source, part)
                hop(source, part, False, core).start()
                settle(source, part, core)

    def receive_hops(place, part):
        for over in range(side):
            for across in range(side):
                source = chip_of(place, over, across)
                hop(source, part, False, 1 - core).wait_recv()
                settle(source, part, 1 - core)

    units = [(0, 0)] + [(reach, way) for reach in range(1, line) for way in range(2)]
    work = [(reach, way, part) for reach, way in units for part in range(subs)]

    def run(item, stage):
        reach, way, part = item
        place = far - reach if way == 0 else far + reach

        def body():
            if stage == 0:
                arrive(place, part, reach == 0, (0, 1) if reach == 0 else (way,))
            elif stage == 1:
                pass_on(place, part)
            elif stage == 2:
                finish(place, part)
            else:
                receive_hops(place, part)

        if reach == 0:
            body()
        else:
            pl.when(place >= 0 if way == 0 else place < line)(body)

    lags = (0, 3, 6, 8)
    for step in range(len(work) + lags[-1]):
        for stage, lag in enumerate(lags):
            if 0 <= step - lag < len(work):
                run(work[step - lag], stage)
    if stay is not None:
        stay.wait()

    def drain(place, carry):
        for part in range(subs):
            for to in range(side - 1):
                over_first(place, part, False, to).wait_send()
                for over in range(side):
                    over_second(place, over, part, False, to).wait_send()

            @pl.when((place <= far) & (far < line - 1))
            def _(part=part):
                along(place, part, False, 0).wait_send()

            @pl.when((place >= far) & (far > 0))
            def _(part=part):
                along(place, part, False, 1).wait_send()

            for over in range(side):
                for across in range(side):
                    hop(chip_of(place, over, across), part, False, core).wait_send()
        return carry

    lax.fori_loop(0, line, drain, 0)


def front_phase(devices, slots, line, side, subs, r, idle, late_idle, arrived):
    me = lax.axis_index("node")
    (node, bucket, feats, memory) = (r.node, r.bucket, r.feats, r.memory)
    (outgoing, inbox, sel, meta, hidden) = (r.outgoing, r.inbox, r.sel, r.meta, r.hidden)
    (picked, picked_meta, totals, counts) = (r.picked, r.picked_meta, r.totals, r.counts)
    (send_sems, recv_sems) = (r.send_sems, r.recv_sems)
    events = feats.shape[0]
    rows, columns = memory.shape
    stride = columns // LANES
    batch = 4
    mesh_id = pl.DeviceIdType.MESH
    barrier = pltpu.get_barrier_semaphore()

    def greet(step, carry):
        pl.semaphore_signal(
            barrier, inc=1, device_id=(lax.rem(me + step, devices),), device_id_type=mesh_id
        )
        return carry

    lax.fori_loop(1, devices, greet, 0)

    ids = lax.broadcasted_iota(jnp.int32, (devices, events), 0) * rows
    names = node[...]
    theirs = (names >= ids) & (names < ids + rows)
    before = lax.broadcasted_iota(jnp.int32, (events, events), 0) < lax.broadcasted_iota(
        jnp.int32, (events, events), 1
    )
    rank = mm(theirs.astype(F32).astype(BF), before.astype(F32).astype(BF))
    sel[...] = jnp.where(theirs, rank, -1.0)
    within = jnp.sum(jnp.where(theirs, names - ids, 0).astype(F32), axis=0, keepdims=True)
    kind = lax.broadcasted_iota(jnp.int32, (16, events), 0)
    meta[...] = jnp.where(
        kind == 0,
        within,
        jnp.where(kind == 1, bucket[...].astype(F32), jnp.where(kind == 2, 1.0, 0.0)),
    ).astype(BF)
    slot_ids = lax.broadcasted_iota(jnp.int32, (slots, events), 0).astype(F32)
    lane_ids = lax.broadcasted_iota(jnp.int32, (LANES, events), 0).astype(F32)
    pl.semaphore_wait(barrier, devices - 1)

    def send(peer):
        return pltpu.make_async_remote_copy(
            src_ref=outgoing.at[peer],
            dst_ref=inbox.at[me],
            send_sem=send_sems.at[peer],
            recv_sem=recv_sems.at[me],
            device_id=(peer,),
            device_id_type=mesh_id,
        )

    def receive(peer):
        return pltpu.make_async_remote_copy(
            src_ref=outgoing.at[peer],
            dst_ref=inbox.at[peer],
            send_sem=send_sems.at[peer],
            recv_sem=recv_sems.at[peer],
            device_id=(peer,),
            device_id_type=mesh_id,
        )

    def pack(peer):
        row = sel[pl.ds(peer, 1), :]
        hits = (slot_ids == row).astype(F32).astype(BF)
        turned = (lane_ids == row).astype(F32).astype(BF)
        return mm(hits, feats[...]).astype(BF), mm_nt(meta[...], turned).astype(BF)

    def pack_batch(step, own):
        for part in range(batch):
            peer = lax.rem(me + step * batch + part, devices)
            rows_of, info = pack(peer)
            if own and part == 0:
                inbox[me, :slots, :] = rows_of
                inbox[me, slots:, :] = info
            else:
                outgoing[peer, :slots, :] = rows_of
                outgoing[peer, slots:, :] = info
                send(peer).start()

    pack_batch(0, True)

    def pack_rest(step, carry):
        pack_batch(step, False)
        return carry

    lax.fori_loop(1, devices // batch, pack_rest, 0)

    r.need('hidden_weight')
    previous = memory[...]
    for part in range(3):
        cut = slice(part * columns, (part + 1) * columns)
        hidden[:, cut] = mm(previous, r.hidden_weight[:, cut])
    idle()
    totals[...] = jnp.zeros_like(totals)
    counts[...] = jnp.zeros_like(counts)
    high, low = halves(r.time_message[...])
    weight = r.edge_weight[...]
    turn = (
        lax.broadcasted_iota(jnp.int32, (slots, LANES), 0)
        == lax.broadcasted_iota(jnp.int32, (slots, LANES), 1)
    ).astype(F32).astype(BF)
    chunk = batch * slots

    def add_batch(step, own):
        for part in range(batch):
            peer = lax.rem(me + devices - step * batch - part, devices)
            if not (own and part == 0):
                receive(peer).wait_recv()
            at = slice(part * slots, (part + 1) * slots)
            picked[at, :] = inbox[peer, :slots, :]
            picked_meta[at, :] = mm_nt(turn, inbox[peer, slots:, :])
        info = picked_meta[...]
        place, when, valid = info[:, 0:1], info[:, 1:2], info[:, 2:3]
        lanes = lax.broadcasted_iota(jnp.int32, (chunk, high.shape[0]), 1).astype(F32)
        picks = (lanes == when).astype(F32).astype(BF)
        pre = mm(picked[...], weight) + mm(picks, high) + mm(picks, low)
        message = (pre / (1.0 + jnp.exp(-pre))).astype(BF)
        node_ids = lax.broadcasted_iota(jnp.int32, (chunk, rows), 1).astype(F32)
        marks = jnp.where(node_ids == place, valid, 0.0).astype(BF)
        totals[...] += mm_tn(marks, message)
        counts[...] += mm_tn(marks, jnp.ones((chunk, LANES), BF))

    add_batch(0, True)

    def add_rest(step, carry):
        add_batch(step, False)
        return carry

    lax.fori_loop(1, devices // batch, add_rest, 0)

    r.need('input_weight')

    def prepare(part):
        size = rows // subs
        at = slice(part * size, (part + 1) * size)
        count = counts[at, 0:1]
        aggregate = (totals[at, :] / jnp.maximum(count, 1.0)).astype(BF)

        def gate(which):
            cut = slice(which * columns, (which + 1) * columns)
            bias = jnp.concatenate(
                [r.gate_bias[which * stride + p : which * stride + p + 1, :] for p in range(stride)],
                axis=1,
            )
            return mm(aggregate, r.input_weight[:, cut]) + bias, hidden[at, cut]

        from_input, from_hidden = gate(0)
        update = jax.nn.sigmoid(from_input + from_hidden)
        from_input, from_hidden = gate(1)
        resets = jax.nn.sigmoid(from_input + from_hidden)
        from_input, from_hidden = gate(2)
        candidate = jnp.tanh(from_input + resets * from_hidden)
        old = memory[at, :].astype(F32)
        fresh = (1.0 - update) * candidate + update * old
        fresh = jnp.where(count > 0, fresh, old)
        r.out_memory[at, :] = fresh.astype(BF)
        first = part * size * stride
        for p in range(stride):
            r.wide[pl.ds(first + p, size, stride=stride), :] = fresh[:, p * LANES : (p + 1) * LANES]
        at = slice(first, first + size * stride)
        r.own_table[at, :] = r.wide[at, :].astype(BF)

    gather_blocks(
        line,
        side,
        subs,
        r.own_table,
        r.whole,
        r.gather_recv,
        r.gather_hop_recv,
        r.gather_line_send,
        r.gather_first_send,
        r.gather_second_send,
        r.gather_hop_send,
        r.gather_own,
        prepare,
        late_idle,
        arrived,
    )

    def drain(step, carry):
        send(lax.rem(me + step, devices)).wait_send()
        return carry

    lax.fori_loop(1, devices, drain, 0)


def keep(blocks, tall, dest, kind, values):
    upper, lower = halves(values)
    for b in range(blocks):
        rows = slice(b * GROUP, (b + 1) * GROUP)
        first = b * tall + kind * GROUP
        dest[first : first + GROUP, :] = upper[rows, :]
        first += 2 * HEADS * GROUP
        dest[first : first + GROUP, :] = lower[rows, :]


def head_cuts(columns):
    head = columns // HEADS
    return [slice(h * head, (h + 1) * head) for h in range(HEADS)]


def early_products(r):
    events, columns = r.back.shape
    blocks = events // GROUP
    tall = 4 * HEADS * GROUP
    r.need("upstream")
    r.need("out_weight")
    r.need("value_weight")
    r.back[...] = mm_nt(r.upstream[...], r.out_weight[...]).astype(BF)
    for h, cut in enumerate(head_cuts(columns)):
        keep(blocks, tall, r.pull, HEADS + h, mm_nt(r.back[:, cut], r.value_weight[:, cut]))
        keep(blocks, tall, r.pull_time, HEADS + h, jnp.zeros((events, LANES), F32))


def early_marks(r):
    fanout, events = r.buckets.shape
    blocks = events // GROUP
    wide = fanout * GROUP
    even = (
        lax.broadcasted_iota(jnp.int32, (fanout, LANES), 0)
        == lax.broadcasted_iota(jnp.int32, (fanout, LANES), 1)
    ).astype(F32).astype(BF)
    r.names[...] = mm_tn(r.buckets[...].astype(F32).astype(BF), even)
    r.logits[...] = jnp.zeros_like(r.logits)
    r.logits[:fanout, :] = r.affinity[...]
    lane_names = lax.broadcasted_iota(jnp.int32, (GROUP, LANES), 1).astype(F32)

    def mark(b, carry):
        mine = r.names[pl.ds(pl.multiple_of(b * GROUP, GROUP), GROUP), :]
        for j in range(fanout):
            at = pl.ds(pl.multiple_of(b * wide + j * GROUP, GROUP), GROUP)
            r.hot[at, :] = (lane_names == mine[:, j : j + 1]).astype(F32).astype(BF)
        return carry

    lax.fori_loop(0, blocks, mark, 0)


def event_phase(r, fetch_targets, fetch_block):
    events, columns = r.back.shape
    fanout = r.buckets.shape[0]
    head = columns // HEADS
    stride = columns // LANES
    kinds = 2 * HEADS
    blocks = events // GROUP
    wide = fanout * GROUP
    tall = 2 * kinds * GROUP
    rows_all = fanout * events
    heads = head_cuts(columns)
    (target, query, pull, pull_time) = (r.target, r.query, r.pull, r.pull_time)
    (mix, hits, scores, close, hot, logits) = (r.mix, r.hits, r.scores, r.close, r.hot, r.logits)
    high, low = halves(r.time_key[...])
    lane = lax.broadcasted_iota(jnp.int32, (GROUP, LANES), 1)

    fetch_targets()
    fetch_block(0, r.near[0])
    for part in range(stride):
        target[:, part * LANES : (part + 1) * LANES] = r.own_near[
            pl.ds(part, events, stride=stride), :
        ].astype(BF)
    r.need("query_weight")
    r.need("key_weight")
    query[...] = mm(target[...], r.query_weight[...]).astype(BF)
    for h, cut in enumerate(heads):
        keep(blocks, tall, pull, h, mm_nt(query[:, cut], r.key_weight[:, cut]))
        keep(
            blocks,
            tall,
            pull_time,
            h,
            mm_nt(query[:, cut], high[:, cut]) + mm_nt(query[:, cut], low[:, cut]),
        )

    scale = 1.0 / math.sqrt(head)
    pad = scores.shape[0] // blocks
    own = lax.rem(lane, GROUP) == lax.broadcasted_iota(jnp.int32, (GROUP, LANES), 0)
    row_ids = lax.broadcasted_iota(jnp.int32, (pad, LANES), 0)
    lane_ids = lax.broadcasted_iota(jnp.int32, (pad, LANES), 1)
    forward = lane_ids < HEADS * GROUP
    per_row = LANES // GROUP

    def close_rows(b):
        return jnp.concatenate(
            [
                close[pl.ds(pl.multiple_of(part * rows_all + b * wide, GROUP), wide), :]
                for part in range(stride)
            ],
            axis=1,
        )

    def score(b, near):
        for part in range(stride):
            at = pl.ds(pl.multiple_of(part * rows_all + b * wide, GROUP), wide)
            close[at, :] = near[pl.ds(part, wide, stride=stride), :].astype(BF)
        at = pl.ds(pl.multiple_of(b * wide, GROUP), wide)
        from_at = pl.ds(pl.multiple_of(b * tall, GROUP), tall)
        both = mm_nt(close_rows(b), pull[from_at, :]) + mm_nt(hot[at, :], pull_time[from_at, :])
        both = both[:, :LANES] + both[:, LANES:]
        raw = jnp.zeros((pad, LANES), F32)
        for j in range(fanout):
            line = jnp.where(own, both[j * GROUP : (j + 1) * GROUP, :], 0.0)
            raw = jnp.where(row_ids == j, jnp.sum(line, axis=0, keepdims=True), raw)
        chunk = pl.multiple_of(b // per_row * LANES, LANES)
        piece = logits[:, pl.ds(chunk, LANES)]
        piece = pltpu.roll(piece, lax.rem(LANES - lax.rem(b, per_row) * GROUP, LANES), axis=1)
        given = piece
        for h in range(1, HEADS):
            moved = pltpu.roll(piece, h * GROUP, axis=1)
            given = jnp.where(lane_ids >= h * GROUP, moved, given)
        scores[pl.ds(pl.multiple_of(b * pad, pad), pad), :] = jnp.where(
            forward, raw * scale + given, raw
        )

    def score_two(step, carry):
        b = step * 2
        fetch_block(b + 1, r.near[1])
        score(b, r.near[0])
        fetch_block(b + 2, r.near[0])
        score(b + 1, r.near[1])
        return carry

    lax.fori_loop(0, blocks // 2 - 1, score_two, 0)
    fetch_block(blocks - 1, r.near[1])
    score(blocks - 2, r.near[0])
    score(blocks - 1, r.near[1])

    for b in range(blocks):
        at = slice(b * pad, (b + 1) * pad)
        here = scores[at, :]
        active = row_ids < fanout
        top = jnp.max(jnp.where(active, here, -3.0e38), axis=0, keepdims=True)
        raised = jnp.where(active, jnp.exp(jnp.where(active, here - top, 0.0)), 0.0)
        probs = raised / jnp.sum(raised, axis=0, keepdims=True)
        slopes = pltpu.roll(here, HEADS * GROUP, axis=1).astype(BF).astype(F32)
        inner = jnp.sum(probs * slopes, axis=0, keepdims=True)
        slopes = probs * (slopes - inner) * scale
        scores[at, :] = jnp.where(forward, probs, pltpu.roll(slopes, HEADS * GROUP, axis=1))

    def blend(b):
        weights = scores[pl.ds(pl.multiple_of(b * pad, pad), pad), :]
        spread = jnp.concatenate(
            [
                jnp.where(own, jnp.broadcast_to(weights[j : j + 1, :], (GROUP, LANES)), 0.0)
                for j in range(fanout)
            ],
            axis=0,
        ).astype(BF)
        at = pl.ds(pl.multiple_of(b * wide, GROUP), wide)
        mixed = mm_tn(spread, close_rows(b)).astype(BF)
        times = mm_tn(spread, hot[at, :]).astype(BF)
        to = pl.ds(pl.multiple_of(b * GROUP, GROUP), GROUP)
        for k in range(kinds):
            mix[k, to, :] = mixed[k * GROUP : (k + 1) * GROUP, :]
        for h in range(HEADS):
            hits[h, to, :] = times[(HEADS + h) * GROUP : (HEADS + h + 1) * GROUP, :]

    def blend_two(step, carry):
        for place in range(2):
            blend(step * 2 + place)
        return carry

    lax.fori_loop(0, blocks // 2, blend_two, 0)


def gradient_steps(r):
    (target, query, back, mix, hits, grads) = (r.target, r.query, r.back, r.mix, r.hits, r.grads)
    events, columns = back.shape
    heads = head_cuts(columns)
    high, low = halves(r.time_key[...])

    def value_and_key():
        for h, cut in enumerate(heads):
            grads[2 * columns : 3 * columns, cut] = mm_tn(mix[h], back[:, cut]).astype(BF)
            grads[:columns, cut] = mm_tn(mix[HEADS + h], query[:, cut]).astype(BF)

    def cotangents():
        for h, cut in enumerate(heads):
            back[:, cut] = mm(mix[h], r.value_weight[:, cut]).astype(BF)
            query[:, cut] = (
                mm(mix[HEADS + h], r.key_weight[:, cut])
                + mm(hits[h], high[:, cut])
                + mm(hits[h], low[:, cut])
            ).astype(BF)

    def query_and_out():
        grads[columns : 2 * columns, :] = mm_tn(target[...], query[...]).astype(BF)
        grads[3 * columns :, :] = mm_tn(back[...], r.upstream[...]).astype(BF)

    def embed():
        r.embedding[...] = (mm(back[...], r.out_weight[...]) + target[...].astype(F32)).astype(BF)

    return value_and_key, cotangents, query_and_out, embed


class Refs:
    def __init__(self, names, refs, staged):
        for name, ref in zip(names, refs, strict=True):
            setattr(self, name, ref)
        self.copies = {}
        for place, name in enumerate(staged):
            copy = pltpu.make_async_copy(
                getattr(self, name), getattr(self, name + "_here"), self.stage_sems.at[place]
            )
            copy.start()
            self.copies[name] = copy
            setattr(self, name, getattr(self, name + "_here"))
        if hasattr(self, "near_first"):
            self.near = (self.near_first, self.near_second)
        if hasattr(self, "grads"):
            self.out_sems = [getattr(self, name) for name in OUT_SEMS]
            self.back_sems = [getattr(self, name) for name in BACK_SEMS]

    def need(self, name):
        copy = self.copies.pop(name, None)
        if copy is not None:
            copy.wait()


OUT_SEMS = [f"out{place}" for place in range(6)]
BACK_SEMS = [f"back{place}" for place in range(8)]
FRONT_STAGED = ("hidden_weight", "input_weight")
EVENT_STAGED = ("upstream", "out_weight", "value_weight", "query_weight", "key_weight")


def front_kernel(sizes, names, *refs):
    r = Refs(names, refs, FRONT_STAGED)
    front_phase(*sizes, r, lambda: None, lambda: None, None)


def fetch_kernel(ids, own_ids, source, dest, sem):
    fanout, events = ids.shape
    stride = dest.shape[0] // ((fanout + 1) * events)
    wide = fanout * GROUP

    def request(start, row):
        pltpu.make_async_copy(
            source.at[pl.ds(pl.multiple_of(start * stride, stride), stride)],
            dest.at[pl.ds(pl.multiple_of(row * stride, stride), stride)],
            sem,
        ).start()

    def request_all(e, carry):
        for j in range(fanout):
            request(ids[j, e], e // GROUP * wide + j * GROUP + e % GROUP)
        request(own_ids[e], fanout * events + e)
        return carry

    lax.fori_loop(0, events, request_all, 0)
    pltpu.make_async_copy(source.at[pl.ds(0, dest.shape[0])], dest, sem).wait()


def event_kernel(reduce_sizes, names, *refs):
    r = Refs(names, refs, EVENT_STAGED)
    fanout, events = r.buckets.shape
    block_rows = r.near_first.shape[0]
    early_products(r)
    early_marks(r)

    def fetch_targets():
        copy = pltpu.make_async_copy(
            r.rows.at[pl.ds(events // GROUP * block_rows, r.own_near.shape[0])],
            r.own_near,
            r.fetch_sem,
        )
        copy.start()
        copy.wait()

    def fetch_block(b, near):
        first = pl.multiple_of(b * block_rows, block_rows)
        copy = pltpu.make_async_copy(r.rows.at[pl.ds(first, block_rows)], near, r.fetch_sem)
        copy.start()
        copy.wait()

    event_phase(r, fetch_targets, fetch_block)
    reduce_phase(*reduce_sizes, r, True, gradient_steps(r))


def whole_kernel(front_sizes, reduce_sizes, names, *refs):
    r = Refs(names, refs, FRONT_STAGED + EVENT_STAGED)
    fanout, events = r.buckets.shape
    stride = r.own_near.shape[0] // events
    table = r.table
    r.close = r.whole

    def arrived(source, first, start, size):
        step_rows = 128

        def widen(step, carry):
            from_at = pl.ds(pl.multiple_of(first + step * step_rows, 16), step_rows)
            to_at = pl.ds((start + step * step_rows) // stride, step_rows // stride)
            rows = source[from_at, :].astype(F32)
            table[to_at] = rows.reshape(step_rows // stride, stride, LANES)
            return carry

        lax.fori_loop(0, size // step_rows, widen, 0)

    front_phase(*front_sizes, r, lambda: early_products(r), lambda: early_marks(r), arrived)

    def move(start, dest, row):
        dest[pl.ds(pl.multiple_of(row * stride, stride), stride), :] = table[start]

    def fetch_targets():
        unroll = 16

        def some(step, carry):
            for place in range(unroll):
                e = step * unroll + place
                move(r.own_ids[e], r.own_near, e)
            return carry

        lax.fori_loop(0, events // unroll, some, 0)

    def fetch_block(b, near):
        for e in range(GROUP):
            for j in range(fanout):
                move(r.ids[j, b * GROUP + e], near, j * GROUP + e)

    event_phase(r, fetch_targets, fetch_block)
    reduce_phase(*reduce_sizes, r, False, gradient_steps(r))


def shards(
    event_node,
    neighbours,
    event_bucket,
    neighbour_bucket,
    edge_features,
    affinity,
    upstream,
    node_memory,
    edge_weight,
    time_message,
    input_weight,
    hidden_weight,
    gate_bias,
    time_key,
    query_weight,
    key_weight,
    value_weight,
    out_weight,
):
    devices = lax.axis_size("node")
    node_rows, columns = node_memory.shape
    events, fanout = neighbours.shape
    features = edge_features.shape[1]
    stride = columns // LANES
    slots = -(-(3 * events // devices) // 16) * 16
    chips = devices // 2
    side = max(s for s in range(1, chips + 1) if chips % (s * s) == 0 and s**3 <= chips)
    line = chips // (side * side)
    subs = 2
    half = 2 * columns
    strands = max(1, min(4, half // (16 * chips)))
    factor = 1.0 / math.sqrt(events * devices)
    front_sizes = (devices, slots, line, side, subs)
    reduce_sizes = (line, side, strands, factor)
    table_rows = devices * node_rows * stride
    close_rows = fanout * events * stride
    resident = table_rows * LANES * 4 <= RESIDENT_LIMIT
    vmem = pl.BlockSpec(memory_space=pltpu.VMEM)
    smem = pl.BlockSpec(memory_space=pltpu.SMEM)
    hbm = pl.BlockSpec(memory_space=pl.ANY)
    dma = pltpu.SemaphoreType.DMA

    def buffer(rows, width, dtype=BF):
        return pltpu.VMEM((rows, width), dtype)

    front_in = {
        "node": (event_node.reshape(1, events), vmem),
        "bucket": (event_bucket.reshape(1, events), vmem),
        "feats": (edge_features, vmem),
        "memory": (node_memory, vmem),
        "edge_weight": (edge_weight, vmem),
        "time_message": (time_message, vmem),
        "input_weight": (input_weight, hbm),
        "hidden_weight": (hidden_weight, hbm),
        "gate_bias": (gate_bias.reshape(-1, LANES), vmem),
    }
    event_in = {
        "buckets": (neighbour_bucket.T, vmem),
        "affinity": (affinity.T, vmem),
        "upstream": (upstream, hbm),
        "time_key": (time_key, vmem),
        "query_weight": (query_weight, hbm),
        "key_weight": (key_weight, hbm),
        "value_weight": (value_weight, hbm),
        "out_weight": (out_weight, hbm),
    }
    index_in = {"ids": (neighbours.T, smem), "own_ids": (event_node, smem)}
    memory_out = {"out_memory": (jax.ShapeDtypeStruct((node_rows, columns), BF), vmem)}
    event_out = {
        "embedding": (jax.ShapeDtypeStruct((events, columns), BF), vmem),
        "result": (jax.ShapeDtypeStruct((2 * half, columns), BF), vmem),
    }
    front_scratch = {
        "outgoing": pltpu.VMEM((devices, slots + 16, features), BF),
        "inbox": pltpu.VMEM((devices, slots + 16, features), BF),
        "sel": buffer(devices, events, F32),
        "meta": buffer(16, events),
        "hidden": buffer(node_rows, 3 * columns, F32),
        "picked": buffer(4 * slots, features),
        "picked_meta": buffer(4 * slots, 16, F32),
        "totals": buffer(node_rows, columns, F32),
        "counts": buffer(node_rows, LANES, F32),
        "wide": buffer(node_rows * stride, LANES, F32),
        "own_table": buffer(node_rows * stride, LANES),
        "send_sems": dma((devices,)),
        "recv_sems": dma((devices,)),
        "gather_recv": dma((chips * subs,)),
        "gather_hop_recv": dma((chips * subs,)),
        "gather_line_send": dma((line * subs, 2)),
        "gather_first_send": dma((line * subs, side - 1)),
        "gather_second_send": dma((line * subs, side, side - 1)),
        "gather_hop_send": dma((chips * subs,)),
        "gather_own": dma,
    }
    event_scratch = {
        "target": buffer(events, columns),
        "query": buffer(events, columns),
        "back": buffer(events, columns),
        "pull": buffer(4 * HEADS * events, columns),
        "pull_time": buffer(4 * HEADS * events, LANES),
        "mix": pltpu.VMEM((2 * HEADS, events, columns), BF),
        "hits": pltpu.VMEM((HEADS, events, LANES), BF),
        "scores": buffer(events // GROUP * 16, LANES, F32),
        "hot": buffer(fanout * events, LANES),
        "names": buffer(events, LANES, F32),
        "logits": buffer(16, events, F32),
        "own_near": buffer(events * stride, LANES, F32),
        "near_first": buffer(fanout * GROUP * stride, LANES, F32),
        "near_second": buffer(fanout * GROUP * stride, LANES, F32),
        "grads": buffer(2 * half, columns),
        "swapped": buffer(half, columns),
        "pair": buffer(half, columns),
        "first_land": buffer(half, columns),
        "first_sum": buffer(half // side, columns),
        "second_land": buffer(half // side, columns),
        "second_sum": buffer(half // (side * side), columns),
        "line_land": buffer(half // (side * side), columns),
        "pair_send": dma((strands,)),
        "pair_recv": dma((strands,)),
    }
    places = (side, side, line)
    for name, place in zip(OUT_SEMS, range(6)):
        event_scratch[name] = dma((strands, places[place // 2]))
    places = (line, side, side, side)
    for name, place in zip(BACK_SEMS, range(8)):
        event_scratch[name] = dma((strands, places[place // 2]))

    def call(kernel, sizes, name, number, inputs, outputs, scratch, staged):
        scratch = dict(scratch)
        for key in staged:
            array = inputs[key][0]
            scratch[key + "_here"] = pltpu.VMEM(array.shape, array.dtype)
        scratch["stage_sems"] = dma((len(staged),))
        names = list(inputs) + list(outputs) + list(scratch)
        return pl.pallas_call(
            functools.partial(kernel, *sizes, names),
            out_shape=tuple(shape for shape, _ in outputs.values()),
            in_specs=[spec for _, spec in inputs.values()],
            out_specs=tuple(spec for _, spec in outputs.values()),
            scratch_shapes=list(scratch.values()),
            compiler_params=pltpu.CompilerParams(
                collective_id=number, has_side_effects=True, vmem_limit_bytes=VMEM_LIMIT
            ),
            name=name,
        )(*[array for array, _ in inputs.values()])

    if resident:
        new_memory, embedding, total = call(
            whole_kernel,
            (front_sizes, reduce_sizes),
            "whole_step",
            0,
            front_in | event_in | index_in,
            memory_out | event_out,
            front_scratch
            | event_scratch
            | {
                "whole": buffer(max(table_rows, close_rows), LANES),
                "table": pltpu.VMEM((table_rows // stride, stride, LANES), F32),
            },
            FRONT_STAGED + EVENT_STAGED,
        )
    else:
        new_memory, whole = call(
            front_kernel,
            (front_sizes,),
            "front_step",
            0,
            front_in,
            memory_out | {"whole": (jax.ShapeDtypeStruct((table_rows, LANES), BF), hbm)},
            front_scratch,
            FRONT_STAGED,
        )
        rows = pl.pallas_call(
            fetch_kernel,
            out_shape=jax.ShapeDtypeStruct(((fanout + 1) * events * stride, LANES), F32),
            in_specs=[smem, smem, hbm],
            out_specs=hbm,
            scratch_shapes=[dma],
            name="fetch_step",
        )(neighbours.T, event_node, whole.astype(F32))
        embedding, total = call(
            event_kernel,
            (reduce_sizes,),
            "event_step",
            1,
            event_in | {"rows": (rows, hbm)},
            event_out,
            event_scratch | {"close": buffer(close_rows, LANES), "fetch_sem": dma},
            EVENT_STAGED,
        )
    total = total.astype(F32)
    return (embedding, new_memory) + tuple(
        total[part * columns : (part + 1) * columns] for part in (1, 0, 2, 3)
    )


def solution(mesh):
    placed = (
        P("node"),
        P("node", None),
        P("node"),
        P("node", None),
        P("node", None),
        P("node", None),
        P("node", None),
        P("node", None),
        P(),
        P(),
        P(),
        P(),
        P(),
        P(),
        P(),
        P(),
        P(),
        P(),
    )
    return jax.shard_map(
        shards,
        mesh=mesh,
        in_specs=placed,
        out_specs=(P("node", None), P("node", None), P(), P(), P(), P()),
        check_vma=False,
    )
```

```python
import functools
import math

import jax
import jax.numpy as jnp
from jax import lax
from jax.experimental import pallas as pl
from jax.experimental.pallas import tpu as pltpu
from jax.sharding import PartitionSpec as P

HEADS = 2
LANES = 128
GROUP = 32
BF = jnp.bfloat16
F32 = jnp.float32
VMEM_LIMIT = 60 * 1024 * 1024
RESIDENT_LIMIT = 20 * 1024 * 1024
NT = (((1,), (1,)), ((), ()))
TN = (((0,), (0,)), ((), ()))


def mm(a, b):
    return jnp.dot(a, b, preferred_element_type=F32)


def mm_nt(a, b):
    return lax.dot_general(a, b, NT, preferred_element_type=F32)


def mm_tn(a, b):
    return lax.dot_general(a, b, TN, preferred_element_type=F32)


def halves(table):
    high = table.astype(BF)
    low = (table - high.astype(F32)).astype(BF)
    return high, low


def reduce_phase(line, side, strands, factor, r, meet, steps):
    (grads, result, near, pair) = (r.grads, r.result, r.swapped, r.pair)
    (plane_land, plane_sum, line_land) = (r.plane_land, r.plane_sum, r.line_land)
    (pair_send, pair_recv, plane_send, plane_recv, line_send, line_recv) = r.out_sems
    (line_back_send, line_back_recv, plane_back_send, plane_back_recv) = r.back_sems[:4]
    hop_send, hop_recv = r.back_sems[4:]
    me = lax.axis_index("node")
    core = lax.rem(me, 2)
    chip = me // 2
    partner = me + 1 - 2 * core
    plane = side * side
    spot, far = lax.rem(chip, plane), chip // plane
    half = grads.shape[0] // 2
    rows = half // strands
    rows_p = rows // plane
    rows_z = rows_p // line
    mesh_id = pl.DeviceIdType.MESH

    spots = [lax.rem(spot + step, plane) for step in range(1, plane)]
    fars = [lax.rem(far + step, line) for step in range(1, line)]

    def spot_device(place):
        return me + (place - spot) * 2

    def far_device(place):
        return me + (place - far) * (2 * plane)

    everyone = (
        [partner]
        + [spot_device(place) for place in spots]
        + [far_device(place) for place in fars]
    )
    if meet:
        barrier = pltpu.get_barrier_semaphore()
        for device in everyone:
            pl.semaphore_signal(barrier, inc=1, device_id=(device,), device_id_type=mesh_id)
        pl.semaphore_wait(barrier, len(everyone))

    def span(start, size):
        return pl.ds(pl.multiple_of(start, 16), size)

    def remote(src, dst, send, recv, device):
        return pltpu.make_async_remote_copy(
            src_ref=src,
            dst_ref=dst,
            send_sem=send,
            recv_sem=recv,
            device_id=(device,),
            device_id_type=mesh_id,
        )

    def swap(s):
        return remote(
            grads.at[span((1 - core) * half + s * rows, rows)],
            near.at[span(s * rows, rows)],
            pair_send.at[s],
            pair_recv.at[s],
            partner,
        )

    def to_plane(s, place, source):
        return remote(
            pair.at[span(s * rows + place * rows_p, rows_p)],
            plane_land.at[span(s * rows + source * rows_p, rows_p)],
            plane_send.at[s, place],
            plane_recv.at[s, source],
            spot_device(place),
        )

    def to_far(s, place, source):
        return remote(
            plane_sum.at[span(s * rows_p + place * rows_z, rows_z)],
            line_land.at[span(s * rows_p + source * rows_z, rows_z)],
            line_send.at[s, place],
            line_recv.at[s, source],
            far_device(place),
        )

    def place_of(which, s, q, f=0):
        return which * half + s * rows + q * rows_p + f * rows_z

    def spread(at, send, recv, device):
        return remote(result.at[at], result.at[at], send, recv, device)

    def back_far(s, place, source):
        at = span(place_of(core, s, spot, source), rows_z)
        return spread(at, line_back_send.at[s, place], line_back_recv.at[s, source], far_device(place))

    def back_plane(s, place, source):
        at = span(place_of(core, s, source), rows_p)
        return spread(
            at, plane_back_send.at[s, place], plane_back_recv.at[s, source], spot_device(place)
        )

    def hop(s, which):
        at = span(place_of(which, s, 0), rows)
        return spread(at, hop_send.at[s], hop_recv.at[s], partner)

    started = []

    def start(made):
        made.start()
        started.append(made)

    def stage_pair(s):
        swap(s).wait_recv()
        at = span(s * rows, rows)
        own = grads[span(core * half + s * rows, rows), :]
        pair[at, :] = (own.astype(F32) + near[at, :].astype(F32)).astype(BF)
        for place in spots:
            start(to_plane(s, place, spot))

    def stage_plane(s):
        total = pair[span(s * rows + spot * rows_p, rows_p), :].astype(F32)
        for place in spots:
            to_plane(s, place, place).wait_recv()
            total += plane_land[span(s * rows + place * rows_p, rows_p), :].astype(F32)
        plane_sum[span(s * rows_p, rows_p), :] = total.astype(BF)
        for place in fars:
            start(to_far(s, place, far))

    def stage_line(s):
        total = plane_sum[span(s * rows_p + far * rows_z, rows_z), :].astype(F32)
        for place in fars:
            to_far(s, place, place).wait_recv()
            total += line_land[span(s * rows_p + place * rows_z, rows_z), :].astype(F32)
        result[span(place_of(core, s, spot, far), rows_z), :] = (total * factor).astype(BF)
        for place in fars:
            start(back_far(s, place, far))

    def stage_back_line(s):
        for place in fars:
            back_far(s, place, place).wait_recv()
        for place in spots:
            start(back_plane(s, place, spot))

    def stage_back_plane(s):
        for place in spots:
            back_plane(s, place, place).wait_recv()
        start(hop(s, core))

    early = strands // 2
    steps[0]()
    for s in range(early):
        start(swap(s))
    steps[1]()
    for s in range(early):
        stage_pair(s)
    steps[2]()
    for s in range(early, strands):
        start(swap(s))
    steps[3]()
    for s in range(early, strands):
        stage_pair(s)
    stages = [stage_plane, stage_line, stage_back_line, stage_back_plane]
    for step in range(strands + len(stages) - 1):
        for number, stage in enumerate(stages):
            if 0 <= step - number < strands:
                stage(step - number)
    leaving = []
    for s in range(strands):
        hop(s, 1 - core).wait_recv()
        for which in range(2):
            at = pl.ds(which * half + s * rows, rows)
            leaving.append(
                pltpu.make_async_copy(result.at[at], r.result_out.at[at], r.result_sems.at[s, which])
            )
            leaving[-1].start()
    for made in started:
        made.wait_send()
    for copy in leaving:
        copy.wait()


def gather_blocks(
    line,
    side,
    subs,
    own,
    whole,
    recv,
    hop_recv,
    line_send,
    first_send,
    second_send,
    hop_send,
    own_sem,
    prepare,
    idle,
    arrived,
):
    me = lax.axis_index("node")
    core = lax.rem(me, 2)
    chip = me // 2
    partner = me + 1 - 2 * core
    low, mid, far = lax.rem(chip, side), lax.rem(chip // side, side), chip // (side * side)
    first = (1 - core) * low + core * mid
    second = (1 - core) * mid + core * low
    first_stride = 1 + core * (side - 1)
    second_stride = side - core * (side - 1)
    plane = side * side
    rows = own.shape[0]
    size = rows // subs
    mesh_id = pl.DeviceIdType.MESH

    def chip_of(place, over, across):
        return (
            place * plane
            + lax.rem(first + over, side) * first_stride
            + lax.rem(second + across, side) * second_stride
        )

    first_peers = [2 * chip_of(far, step, 0) + core for step in range(1, side)]
    second_peers = [2 * chip_of(far, 0, step) + core for step in range(1, side)]

    def at(source, part, kind):
        return pl.ds(pl.multiple_of((2 * source + kind) * rows + part * size, 16), size)

    def piece(source, part, kind, mine):
        return own.at[pl.ds(part * size, size)] if mine else whole.at[at(source, part, kind)]

    def copy(source, part, mine, send_sem, device):
        return pltpu.make_async_remote_copy(
            src_ref=piece(source, part, core, mine),
            dst_ref=whole.at[at(source, part, core)],
            send_sem=send_sem,
            recv_sem=recv.at[source * subs + part],
            device_id=(device,),
            device_id_type=mesh_id,
        )

    def hop(source, part, mine, kind):
        return pltpu.make_async_remote_copy(
            src_ref=piece(source, part, kind, mine),
            dst_ref=whole.at[at(source, part, kind)],
            send_sem=hop_send.at[source * subs + part],
            recv_sem=hop_recv.at[source * subs + part],
            device_id=(partner,),
            device_id_type=mesh_id,
        )

    def along(place, part, mine, way):
        return copy(
            chip_of(place, 0, 0),
            part,
            mine,
            line_send.at[place * subs + part, way],
            me + (1 - 2 * way) * 2 * plane,
        )

    def over_first(place, part, mine, to):
        return copy(
            chip_of(place, 0, 0), part, mine, first_send.at[place * subs + part, to], first_peers[to]
        )

    def over_second(place, over, part, mine, to):
        return copy(
            chip_of(place, over, 0),
            part,
            mine,
            second_send.at[place * subs + part, over, to],
            second_peers[to],
        )

    def landed(source, part):
        copy(source, part, False, hop_send.at[0], partner).wait_recv()

    def settle(source, part, kind):
        if arrived is not None:
            start = pl.multiple_of((2 * source + kind) * rows + part * size, 16)
            arrived(whole, start, start, size)

    stay = None
    if arrived is None:
        mine_at = pl.ds(pl.multiple_of(me * rows, 16), rows)
        stay = pltpu.make_async_copy(own, whole.at[mine_at], own_sem)

    def arrive(place, part, mine, ways):
        source = chip_of(place, 0, 0)
        if mine:
            prepare(part)
        else:
            landed(source, part)
        for way in ways:
            open_end = far < line - 1 if way == 0 else far > 0

            @pl.when(open_end)
            def _(way=way):
                along(place, part, mine, way).start()

        for to in range(side - 1):
            over_first(place, part, mine, to).start()
        for to in range(side - 1):
            over_second(place, 0, part, mine, to).start()
        hop(source, part, mine, core).start()
        if not mine:
            settle(source, part, core)
        elif arrived is not None:
            arrived(own, part * size, pl.multiple_of(me * rows + part * size, 16), size)
        if mine and part == subs - 1:
            if stay is not None:
                stay.start()
            idle()

    def pass_on(place, part):
        for over in range(1, side):
            source = chip_of(place, over, 0)
            landed(source, part)
            for to in range(side - 1):
                over_second(place, over, part, False, to).start()
            hop(source, part, False, core).start()
            settle(source, part, core)

    def finish(place, part):
        for across in range(1, side):
            for over in range(side):
                source = chip_of(place, over, across)
                landed(source, part)
                hop(source, part, False, core).start()
                settle(source, part, core)

    def receive_hops(place, part):
        for over in range(side):
            for across in range(side):
                source = chip_of(place, over, across)
                hop(source, part, False, 1 - core).wait_recv()
                settle(source, part, 1 - core)

    units = [(0, 0)] + [(reach, way) for reach in range(1, line) for way in range(2)]
    work = [(reach, way, part) for reach, way in units for part in range(subs)]

    def run(item, stage):
        reach, way, part = item
        place = far - reach if way == 0 else far + reach

        def body():
            if stage == 0:
                arrive(place, part, reach == 0, (0, 1) if reach == 0 else (way,))
            elif stage == 1:
                pass_on(place, part)
            elif stage == 2:
                finish(place, part)
            else:
                receive_hops(place, part)

        if reach == 0:
            body()
        else:
            pl.when(place >= 0 if way == 0 else place < line)(body)

    lags = (0, 3, 6, 8)
    for step in range(len(work) + lags[-1]):
        for stage, lag in enumerate(lags):
            if 0 <= step - lag < len(work):
                run(work[step - lag], stage)
    if stay is not None:
        stay.wait()

    def drain(place, carry):
        for part in range(subs):
            for to in range(side - 1):
                over_first(place, part, False, to).wait_send()
                for over in range(side):
                    over_second(place, over, part, False, to).wait_send()

            @pl.when((place <= far) & (far < line - 1))
            def _(part=part):
                along(place, part, False, 0).wait_send()

            @pl.when((place >= far) & (far > 0))
            def _(part=part):
                along(place, part, False, 1).wait_send()

            for over in range(side):
                for across in range(side):
                    hop(chip_of(place, over, across), part, False, core).wait_send()
        return carry

    lax.fori_loop(0, line, drain, 0)


def front_phase(devices, slots, line, side, subs, r, idle, late_idle, arrived):
    me = lax.axis_index("node")
    (node, bucket, feats, memory) = (r.node, r.bucket, r.feats, r.memory)
    (outgoing, inbox, sel, meta, hidden) = (r.outgoing, r.inbox, r.sel, r.meta, r.hidden)
    (picked, picked_meta, totals, counts) = (r.picked, r.picked_meta, r.totals, r.counts)
    (send_sems, recv_sems) = (r.send_sems, r.recv_sems)
    events = feats.shape[0]
    rows, columns = memory.shape
    stride = columns // LANES
    batch = 4
    mesh_id = pl.DeviceIdType.MESH
    barrier = pltpu.get_barrier_semaphore()

    def greet(step, carry):
        pl.semaphore_signal(
            barrier, inc=1, device_id=(lax.rem(me + step, devices),), device_id_type=mesh_id
        )
        return carry

    lax.fori_loop(1, devices, greet, 0)

    ids = lax.broadcasted_iota(jnp.int32, (devices, events), 0) * rows
    names = node[...]
    theirs = (names >= ids) & (names < ids + rows)
    before = lax.broadcasted_iota(jnp.int32, (events, events), 0) < lax.broadcasted_iota(
        jnp.int32, (events, events), 1
    )
    rank = mm(theirs.astype(F32).astype(BF), before.astype(F32).astype(BF))
    sel[...] = jnp.where(theirs, rank, -1.0)
    within = jnp.sum(jnp.where(theirs, names - ids, 0).astype(F32), axis=0, keepdims=True)
    kind = lax.broadcasted_iota(jnp.int32, (16, events), 0)
    meta[...] = jnp.where(
        kind == 0,
        within,
        jnp.where(kind == 1, bucket[...].astype(F32), jnp.where(kind == 2, 1.0, 0.0)),
    ).astype(BF)
    slot_ids = lax.broadcasted_iota(jnp.int32, (slots, events), 0).astype(F32)
    lane_ids = lax.broadcasted_iota(jnp.int32, (LANES, events), 0).astype(F32)
    pl.semaphore_wait(barrier, devices - 1)

    def send(peer):
        return pltpu.make_async_remote_copy(
            src_ref=outgoing.at[peer],
            dst_ref=inbox.at[me],
            send_sem=send_sems.at[peer],
            recv_sem=recv_sems.at[me],
            device_id=(peer,),
            device_id_type=mesh_id,
        )

    def receive(peer):
        return pltpu.make_async_remote_copy(
            src_ref=outgoing.at[peer],
            dst_ref=inbox.at[peer],
            send_sem=send_sems.at[peer],
            recv_sem=recv_sems.at[peer],
            device_id=(peer,),
            device_id_type=mesh_id,
        )

    def pack(peer):
        row = sel[pl.ds(peer, 1), :]
        hits = (slot_ids == row).astype(F32).astype(BF)
        turned = (lane_ids == row).astype(F32).astype(BF)
        return mm(hits, feats[...]).astype(BF), mm_nt(meta[...], turned).astype(BF)

    def pack_batch(step, own):
        for part in range(batch):
            peer = lax.rem(me + step * batch + part, devices)
            rows_of, info = pack(peer)
            if own and part == 0:
                inbox[me, :slots, :] = rows_of
                inbox[me, slots:, :] = info
            else:
                outgoing[peer, :slots, :] = rows_of
                outgoing[peer, slots:, :] = info
                send(peer).start()

    pack_batch(0, True)

    def pack_rest(step, carry):
        pack_batch(step, False)
        return carry

    lax.fori_loop(1, devices // batch, pack_rest, 0)

    r.need("hidden_weight")
    previous = memory[...]
    for part in range(3):
        cut = slice(part * columns, (part + 1) * columns)
        hidden[:, cut] = mm(previous, r.hidden_weight[:, cut])
    idle()
    totals[...] = jnp.zeros_like(totals)
    counts[...] = jnp.zeros_like(counts)
    high, low = halves(r.time_message[...])
    weight = r.edge_weight[...]
    turn = (
        lax.broadcasted_iota(jnp.int32, (slots, LANES), 0)
        == lax.broadcasted_iota(jnp.int32, (slots, LANES), 1)
    ).astype(F32).astype(BF)
    chunk = batch * slots

    def add_batch(step, own):
        for part in range(batch):
            peer = lax.rem(me + devices - step * batch - part, devices)
            if not (own and part == 0):
                receive(peer).wait_recv()
            at = slice(part * slots, (part + 1) * slots)
            picked[at, :] = inbox[peer, :slots, :]
            picked_meta[at, :] = mm_nt(turn, inbox[peer, slots:, :])
        info = picked_meta[...]
        place, when, valid = info[:, 0:1], info[:, 1:2], info[:, 2:3]
        lanes = lax.broadcasted_iota(jnp.int32, (chunk, high.shape[0]), 1).astype(F32)
        picks = (lanes == when).astype(F32).astype(BF)
        pre = mm(picked[...], weight) + mm(picks, high) + mm(picks, low)
        message = (pre / (1.0 + jnp.exp(-pre))).astype(BF)
        node_ids = lax.broadcasted_iota(jnp.int32, (chunk, rows), 1).astype(F32)
        marks = jnp.where(node_ids == place, valid, 0.0).astype(BF)
        totals[...] += mm_tn(marks, message)
        counts[...] += mm_tn(marks, jnp.ones((chunk, LANES), BF))

    add_batch(0, True)

    def add_rest(step, carry):
        add_batch(step, False)
        return carry

    lax.fori_loop(1, devices // batch, add_rest, 0)

    r.need("input_weight")

    def prepare(part):
        size = rows // subs
        at = slice(part * size, (part + 1) * size)
        count = counts[at, 0:1]
        aggregate = (totals[at, :] / jnp.maximum(count, 1.0)).astype(BF)

        def gate(which):
            cut = slice(which * columns, (which + 1) * columns)
            bias = jnp.concatenate(
                [r.gate_bias[which * stride + p : which * stride + p + 1, :] for p in range(stride)],
                axis=1,
            )
            return mm(aggregate, r.input_weight[:, cut]) + bias, hidden[at, cut]

        from_input, from_hidden = gate(0)
        update = jax.nn.sigmoid(from_input + from_hidden)
        from_input, from_hidden = gate(1)
        resets = jax.nn.sigmoid(from_input + from_hidden)
        from_input, from_hidden = gate(2)
        candidate = jnp.tanh(from_input + resets * from_hidden)
        old = memory[at, :].astype(F32)
        fresh = (1.0 - update) * candidate + update * old
        fresh = jnp.where(count > 0, fresh, old)
        r.out_memory[at, :] = fresh.astype(BF)
        first = part * size * stride
        for p in range(stride):
            r.wide[pl.ds(first + p, size, stride=stride), :] = fresh[:, p * LANES : (p + 1) * LANES]
        at = slice(first, first + size * stride)
        r.own_table[at, :] = r.wide[at, :].astype(BF)
        if part == subs - 1:
            r.leave("out_memory")

    gather_blocks(
        line,
        side,
        subs,
        r.own_table,
        r.whole,
        r.gather_recv,
        r.gather_hop_recv,
        r.gather_line_send,
        r.gather_first_send,
        r.gather_second_send,
        r.gather_hop_send,
        r.gather_own,
        prepare,
        late_idle,
        arrived,
    )

    def drain(step, carry):
        send(lax.rem(me + step, devices)).wait_send()
        return carry

    lax.fori_loop(1, devices, drain, 0)


def keep(blocks, tall, dest, kind, values):
    upper, lower = halves(values)
    for b in range(blocks):
        rows = slice(b * GROUP, (b + 1) * GROUP)
        first = b * tall + kind * GROUP
        dest[first : first + GROUP, :] = upper[rows, :]
        first += 2 * HEADS * GROUP
        dest[first : first + GROUP, :] = lower[rows, :]


def head_cuts(columns):
    head = columns // HEADS
    return [slice(h * head, (h + 1) * head) for h in range(HEADS)]


def early_products(r):
    events, columns = r.back.shape
    blocks = events // GROUP
    tall = 4 * HEADS * GROUP
    r.need("upstream")
    r.need("out_weight")
    r.need("value_weight")
    r.back[...] = mm_nt(r.upstream[...], r.out_weight[...]).astype(BF)
    for h, cut in enumerate(head_cuts(columns)):
        keep(blocks, tall, r.pull, HEADS + h, mm_nt(r.back[:, cut], r.value_weight[:, cut]))
        keep(blocks, tall, r.pull_time, HEADS + h, jnp.zeros((events, LANES), F32))


def early_marks(r):
    fanout, events = r.buckets.shape
    blocks = events // GROUP
    wide = fanout * GROUP
    even = (
        lax.broadcasted_iota(jnp.int32, (fanout, LANES), 0)
        == lax.broadcasted_iota(jnp.int32, (fanout, LANES), 1)
    ).astype(F32).astype(BF)
    r.names[...] = mm_tn(r.buckets[...].astype(F32).astype(BF), even)
    r.logits[...] = jnp.zeros_like(r.logits)
    r.logits[:fanout, :] = r.affinity[...]
    lane_names = lax.broadcasted_iota(jnp.int32, (GROUP, LANES), 1).astype(F32)

    def mark(b, carry):
        mine = r.names[pl.ds(pl.multiple_of(b * GROUP, GROUP), GROUP), :]
        for j in range(fanout):
            at = pl.ds(pl.multiple_of(b * wide + j * GROUP, GROUP), GROUP)
            r.hot[at, :] = (lane_names == mine[:, j : j + 1]).astype(F32).astype(BF)
        return carry

    lax.fori_loop(0, blocks, mark, 0)


def event_phase(r, fetch_targets, fetch_block):
    events, columns = r.back.shape
    fanout = r.buckets.shape[0]
    head = columns // HEADS
    stride = columns // LANES
    kinds = 2 * HEADS
    blocks = events // GROUP
    wide = fanout * GROUP
    tall = 2 * kinds * GROUP
    rows_all = fanout * events
    heads = head_cuts(columns)
    (target, query, pull, pull_time) = (r.target, r.query, r.pull, r.pull_time)
    (mix, hits, scores, close, hot, logits) = (r.mix, r.hits, r.scores, r.close, r.hot, r.logits)
    high, low = halves(r.time_key[...])
    lane = lax.broadcasted_iota(jnp.int32, (GROUP, LANES), 1)

    fetch_targets()
    fetch_block(0, r.near[0])
    for part in range(stride):
        target[:, part * LANES : (part + 1) * LANES] = r.own_near[
            pl.ds(part, events, stride=stride), :
        ].astype(BF)
    r.need("query_weight")
    r.need("key_weight")
    query[...] = mm(target[...], r.query_weight[...]).astype(BF)
    for h, cut in enumerate(heads):
        keep(blocks, tall, pull, h, mm_nt(query[:, cut], r.key_weight[:, cut]))
        keep(
            blocks,
            tall,
            pull_time,
            h,
            mm_nt(query[:, cut], high[:, cut]) + mm_nt(query[:, cut], low[:, cut]),
        )

    scale = 1.0 / math.sqrt(head)
    pad = scores.shape[0] // blocks
    own = lax.rem(lane, GROUP) == lax.broadcasted_iota(jnp.int32, (GROUP, LANES), 0)
    row_ids = lax.broadcasted_iota(jnp.int32, (pad, LANES), 0)
    lane_ids = lax.broadcasted_iota(jnp.int32, (pad, LANES), 1)
    forward = lane_ids < HEADS * GROUP
    per_row = LANES // GROUP

    def close_rows(b):
        return jnp.concatenate(
            [
                close[pl.ds(pl.multiple_of(part * rows_all + b * wide, GROUP), wide), :]
                for part in range(stride)
            ],
            axis=1,
        )

    def score(b, near):
        for part in range(stride):
            at = pl.ds(pl.multiple_of(part * rows_all + b * wide, GROUP), wide)
            close[at, :] = near[pl.ds(part, wide, stride=stride), :].astype(BF)
        at = pl.ds(pl.multiple_of(b * wide, GROUP), wide)
        from_at = pl.ds(pl.multiple_of(b * tall, GROUP), tall)
        both = mm_nt(close_rows(b), pull[from_at, :]) + mm_nt(hot[at, :], pull_time[from_at, :])
        both = both[:, :LANES] + both[:, LANES:]
        raw = jnp.zeros((pad, LANES), F32)
        for j in range(fanout):
            line = jnp.where(own, both[j * GROUP : (j + 1) * GROUP, :], 0.0)
            raw = jnp.where(row_ids == j, jnp.sum(line, axis=0, keepdims=True), raw)
        chunk = pl.multiple_of(b // per_row * LANES, LANES)
        piece = logits[:, pl.ds(chunk, LANES)]
        piece = pltpu.roll(piece, lax.rem(LANES - lax.rem(b, per_row) * GROUP, LANES), axis=1)
        given = piece
        for h in range(1, HEADS):
            moved = pltpu.roll(piece, h * GROUP, axis=1)
            given = jnp.where(lane_ids >= h * GROUP, moved, given)
        scores[pl.ds(pl.multiple_of(b * pad, pad), pad), :] = jnp.where(
            forward, raw * scale + given, raw
        )

    def score_two(step, carry):
        b = step * 2
        fetch_block(b + 1, r.near[1])
        score(b, r.near[0])
        fetch_block(b + 2, r.near[0])
        score(b + 1, r.near[1])
        return carry

    lax.fori_loop(0, blocks // 2 - 1, score_two, 0)
    fetch_block(blocks - 1, r.near[1])
    score(blocks - 2, r.near[0])
    score(blocks - 1, r.near[1])

    for b in range(blocks):
        at = slice(b * pad, (b + 1) * pad)
        here = scores[at, :]
        active = row_ids < fanout
        top = jnp.max(jnp.where(active, here, -3.0e38), axis=0, keepdims=True)
        raised = jnp.where(active, jnp.exp(jnp.where(active, here - top, 0.0)), 0.0)
        probs = raised / jnp.sum(raised, axis=0, keepdims=True)
        slopes = pltpu.roll(here, HEADS * GROUP, axis=1).astype(BF).astype(F32)
        inner = jnp.sum(probs * slopes, axis=0, keepdims=True)
        slopes = probs * (slopes - inner) * scale
        scores[at, :] = jnp.where(forward, probs, pltpu.roll(slopes, HEADS * GROUP, axis=1))

    def blend(b):
        weights = scores[pl.ds(pl.multiple_of(b * pad, pad), pad), :]
        spread = jnp.concatenate(
            [
                jnp.where(own, jnp.broadcast_to(weights[j : j + 1, :], (GROUP, LANES)), 0.0)
                for j in range(fanout)
            ],
            axis=0,
        ).astype(BF)
        at = pl.ds(pl.multiple_of(b * wide, GROUP), wide)
        mixed = mm_tn(spread, close_rows(b)).astype(BF)
        times = mm_tn(spread, hot[at, :]).astype(BF)
        to = pl.ds(pl.multiple_of(b * GROUP, GROUP), GROUP)
        for k in range(kinds):
            mix[k, to, :] = mixed[k * GROUP : (k + 1) * GROUP, :]
        for h in range(HEADS):
            hits[h, to, :] = times[(HEADS + h) * GROUP : (HEADS + h + 1) * GROUP, :]

    def blend_two(step, carry):
        for place in range(2):
            blend(step * 2 + place)
        return carry

    lax.fori_loop(0, blocks // 2, blend_two, 0)


def gradient_steps(r):
    (target, query, back, mix, hits, grads) = (r.target, r.query, r.back, r.mix, r.hits, r.grads)
    events, columns = back.shape
    heads = head_cuts(columns)
    high, low = halves(r.time_key[...])

    def value_and_key():
        for h, cut in enumerate(heads):
            grads[2 * columns : 3 * columns, cut] = mm_tn(mix[h], back[:, cut]).astype(BF)
            grads[:columns, cut] = mm_tn(mix[HEADS + h], query[:, cut]).astype(BF)

    def cotangents():
        for h, cut in enumerate(heads):
            back[:, cut] = mm(mix[h], r.value_weight[:, cut]).astype(BF)
            query[:, cut] = (
                mm(mix[HEADS + h], r.key_weight[:, cut])
                + mm(hits[h], high[:, cut])
                + mm(hits[h], low[:, cut])
            ).astype(BF)

    def query_and_out():
        grads[columns : 2 * columns, :] = mm_tn(target[...], query[...]).astype(BF)
        grads[3 * columns :, :] = mm_tn(back[...], r.upstream[...]).astype(BF)

    def embed():
        r.embedding[...] = (mm(back[...], r.out_weight[...]) + target[...].astype(F32)).astype(BF)
        r.leave("embedding")

    return value_and_key, cotangents, query_and_out, embed


class Refs:
    def __init__(self, names, refs, staged):
        for name, ref in zip(names, refs, strict=True):
            setattr(self, name, ref)
        self.copies = {}
        self.leaving = []
        for place, name in enumerate(staged):
            copy = pltpu.make_async_copy(
                getattr(self, name), getattr(self, name + "_here"), self.stage_sems.at[place]
            )
            copy.start()
            self.copies[name] = copy
            setattr(self, name, getattr(self, name + "_here"))
        if hasattr(self, "near_first"):
            self.near = (self.near_first, self.near_second)
        if hasattr(self, "grads"):
            self.out_sems = [getattr(self, name) for name in OUT_SEMS]
            self.back_sems = [getattr(self, name) for name in BACK_SEMS]

    def leave(self, name):
        copy = pltpu.make_async_copy(
            getattr(self, name), getattr(self, name + "_out"), getattr(self, name + "_sem")
        )
        copy.start()
        self.leaving.append(copy)

    def finish(self):
        for copy in self.leaving:
            copy.wait()

    def need(self, name):
        copy = self.copies.pop(name, None)
        if copy is not None:
            copy.wait()


OUT_SEMS = [f"out{place}" for place in range(6)]
BACK_SEMS = [f"back{place}" for place in range(6)]
FRONT_STAGED = ("hidden_weight", "input_weight")
EVENT_STAGED = ("upstream", "out_weight", "value_weight", "query_weight", "key_weight")


def front_kernel(sizes, names, *refs):
    r = Refs(names, refs, FRONT_STAGED)
    front_phase(*sizes, r, lambda: None, lambda: None, None)
    r.finish()


def fetch_kernel(ids, own_ids, source, dest, sem):
    fanout, events = ids.shape
    stride = dest.shape[0] // ((fanout + 1) * events)
    wide = fanout * GROUP

    def request(start, row):
        pltpu.make_async_copy(
            source.at[pl.ds(pl.multiple_of(start * stride, stride), stride)],
            dest.at[pl.ds(pl.multiple_of(row * stride, stride), stride)],
            sem,
        ).start()

    def request_all(e, carry):
        for j in range(fanout):
            request(ids[j, e], e // GROUP * wide + j * GROUP + e % GROUP)
        request(own_ids[e], fanout * events + e)
        return carry

    lax.fori_loop(0, events, request_all, 0)
    pltpu.make_async_copy(source.at[pl.ds(0, dest.shape[0])], dest, sem).wait()


def event_kernel(reduce_sizes, names, *refs):
    r = Refs(names, refs, EVENT_STAGED)
    fanout, events = r.buckets.shape
    block_rows = r.near_first.shape[0]
    early_products(r)
    early_marks(r)

    def fetch_targets():
        copy = pltpu.make_async_copy(
            r.rows.at[pl.ds(events // GROUP * block_rows, r.own_near.shape[0])],
            r.own_near,
            r.fetch_sem,
        )
        copy.start()
        copy.wait()

    def fetch_block(b, near):
        first = pl.multiple_of(b * block_rows, block_rows)
        copy = pltpu.make_async_copy(r.rows.at[pl.ds(first, block_rows)], near, r.fetch_sem)
        copy.start()
        copy.wait()

    event_phase(r, fetch_targets, fetch_block)
    reduce_phase(*reduce_sizes, r, True, gradient_steps(r))
    r.finish()


def whole_kernel(front_sizes, reduce_sizes, names, *refs):
    r = Refs(names, refs, FRONT_STAGED + EVENT_STAGED)
    fanout, events = r.buckets.shape
    stride = r.own_near.shape[0] // events
    table = r.table
    r.close = r.whole

    def arrived(source, first, start, size):
        step_rows = 128

        def widen(step, carry):
            from_at = pl.ds(pl.multiple_of(first + step * step_rows, 16), step_rows)
            to_at = pl.ds((start + step * step_rows) // stride, step_rows // stride)
            rows = source[from_at, :].astype(F32)
            table[to_at] = rows.reshape(step_rows // stride, stride, LANES)
            return carry

        lax.fori_loop(0, size // step_rows, widen, 0)

    front_phase(*front_sizes, r, lambda: early_products(r), lambda: early_marks(r), arrived)

    def move(start, dest, row):
        dest[pl.ds(pl.multiple_of(row * stride, stride), stride), :] = table[start]

    def fetch_targets():
        unroll = 16

        def some(step, carry):
            for place in range(unroll):
                e = step * unroll + place
                move(r.own_ids[e], r.own_near, e)
            return carry

        lax.fori_loop(0, events // unroll, some, 0)

    def fetch_block(b, near):
        for e in range(GROUP):
            for j in range(fanout):
                move(r.ids[j, b * GROUP + e], near, j * GROUP + e)

    event_phase(r, fetch_targets, fetch_block)
    reduce_phase(*reduce_sizes, r, False, gradient_steps(r))
    r.finish()


def finish_kernel(order, total, embedding, memory, *rest):
    outs, (here, wide, *passing, read_sems, write_sems, in_sems, out_sems) = rest[:6], rest[6:]
    grads, kept = outs[:4], outs[4:]
    columns = grads[0].shape[0]
    per = read_sems.shape[0] // 4
    size = columns // per
    reads, writes, enter = [], [], []
    for place in range(4 * per):
        at = pl.ds(place * size, size)
        reads.append(pltpu.make_async_copy(total.at[at], here.at[at], read_sems.at[place]))
        reads[-1].start()
    for place, source in enumerate((embedding, memory)):
        enter.append(pltpu.make_async_copy(source, passing[place], in_sems.at[place]))
        enter[-1].start()
    for place in range(4 * per):
        at = pl.ds(place * size, size)
        reads[place].wait()
        wide[at, :] = here[at, :].astype(F32)
        to = grads[order[place // per]].at[pl.ds(place % per * size, size)]
        writes.append(pltpu.make_async_copy(wide.at[at], to, write_sems.at[place]))
        writes[-1].start()
    for place in range(2):
        enter[place].wait()
        writes.append(pltpu.make_async_copy(passing[place], kept[place], out_sems.at[place]))
        writes[-1].start()
    for copy in writes:
        copy.wait()


def shards(
    event_node,
    neighbours,
    event_bucket,
    neighbour_bucket,
    edge_features,
    affinity,
    upstream,
    node_memory,
    edge_weight,
    time_message,
    input_weight,
    hidden_weight,
    gate_bias,
    time_key,
    query_weight,
    key_weight,
    value_weight,
    out_weight,
):
    devices = lax.axis_size("node")
    node_rows, columns = node_memory.shape
    events, fanout = neighbours.shape
    features = edge_features.shape[1]
    stride = columns // LANES
    slots = -(-(3 * events // devices) // 16) * 16
    chips = devices // 2
    side = max(s for s in range(1, chips + 1) if chips % (s * s) == 0 and s**3 <= chips)
    line = chips // (side * side)
    subs = 2
    half = 2 * columns
    strands = max(1, min(4, half // (16 * chips)))
    factor = 1.0 / math.sqrt(events * devices)
    front_sizes = (devices, slots, line, side, subs)
    reduce_sizes = (line, side, strands, factor)
    table_rows = devices * node_rows * stride
    close_rows = fanout * events * stride
    resident = table_rows * LANES * 4 <= RESIDENT_LIMIT
    vmem = pl.BlockSpec(memory_space=pltpu.VMEM)
    smem = pl.BlockSpec(memory_space=pltpu.SMEM)
    hbm = pl.BlockSpec(memory_space=pl.ANY)
    dma = pltpu.SemaphoreType.DMA

    def buffer(rows, width, dtype=BF):
        return pltpu.VMEM((rows, width), dtype)

    front_in = {
        "node": (event_node.reshape(1, events), vmem),
        "bucket": (event_bucket.reshape(1, events), vmem),
        "feats": (edge_features, vmem),
        "memory": (node_memory, vmem),
        "edge_weight": (edge_weight, vmem),
        "time_message": (time_message, vmem),
        "input_weight": (input_weight, hbm),
        "hidden_weight": (hidden_weight, hbm),
        "gate_bias": (gate_bias.reshape(-1, LANES), vmem),
    }
    event_in = {
        "buckets": (neighbour_bucket.T, vmem),
        "affinity": (affinity.T, vmem),
        "upstream": (upstream, hbm),
        "time_key": (time_key, vmem),
        "query_weight": (query_weight, hbm),
        "key_weight": (key_weight, hbm),
        "value_weight": (value_weight, hbm),
        "out_weight": (out_weight, hbm),
    }
    index_in = {"ids": (neighbours.T, smem), "own_ids": (event_node, smem)}
    memory_out = {"out_memory_out": (jax.ShapeDtypeStruct((node_rows, columns), BF), hbm)}
    event_out = {
        "embedding_out": (jax.ShapeDtypeStruct((events, columns), BF), hbm),
        "result_out": (jax.ShapeDtypeStruct((2 * half, columns), BF), hbm),
    }
    front_scratch = {
        "outgoing": pltpu.VMEM((devices, slots + 16, features), BF),
        "inbox": pltpu.VMEM((devices, slots + 16, features), BF),
        "sel": buffer(devices, events, F32),
        "meta": buffer(16, events),
        "hidden": buffer(node_rows, 3 * columns, F32),
        "picked": buffer(4 * slots, features),
        "picked_meta": buffer(4 * slots, 16, F32),
        "totals": buffer(node_rows, columns, F32),
        "counts": buffer(node_rows, LANES, F32),
        "wide": buffer(node_rows * stride, LANES, F32),
        "own_table": buffer(node_rows * stride, LANES),
        "send_sems": dma((devices,)),
        "recv_sems": dma((devices,)),
        "gather_recv": dma((chips * subs,)),
        "gather_hop_recv": dma((chips * subs,)),
        "gather_line_send": dma((line * subs, 2)),
        "gather_first_send": dma((line * subs, side - 1)),
        "gather_second_send": dma((line * subs, side, side - 1)),
        "gather_hop_send": dma((chips * subs,)),
        "gather_own": dma,
        "out_memory": buffer(node_rows, columns),
        "out_memory_sem": dma,
    }
    event_scratch = {
        "target": buffer(events, columns),
        "query": buffer(events, columns),
        "back": buffer(events, columns),
        "pull": buffer(4 * HEADS * events, columns),
        "pull_time": buffer(4 * HEADS * events, LANES),
        "mix": pltpu.VMEM((2 * HEADS, events, columns), BF),
        "hits": pltpu.VMEM((HEADS, events, LANES), BF),
        "scores": buffer(events // GROUP * 16, LANES, F32),
        "hot": buffer(fanout * events, LANES),
        "names": buffer(events, LANES, F32),
        "logits": buffer(16, events, F32),
        "own_near": buffer(events * stride, LANES, F32),
        "near_first": buffer(fanout * GROUP * stride, LANES, F32),
        "near_second": buffer(fanout * GROUP * stride, LANES, F32),
        "grads": buffer(2 * half, columns),
        "swapped": buffer(half, columns),
        "pair": buffer(half, columns),
        "plane_land": buffer(half, columns),
        "plane_sum": buffer(half // (side * side), columns),
        "line_land": buffer(half // (side * side), columns),
        "embedding": buffer(events, columns),
        "embedding_sem": dma,
        "result": buffer(2 * half, columns),
        "result_sems": dma((strands, 2)),
    }
    plane = side * side
    for name, shape in zip(
        OUT_SEMS + BACK_SEMS,
        [(strands,)] * 2
        + [(strands, plane)] * 2
        + [(strands, line)] * 4
        + [(strands, plane)] * 2
        + [(strands,)] * 2,
    ):
        event_scratch[name] = dma(shape)

    def call(kernel, sizes, name, number, inputs, outputs, scratch, staged):
        scratch = dict(scratch)
        for key in staged:
            array = inputs[key][0]
            scratch[key + "_here"] = pltpu.VMEM(array.shape, array.dtype)
        scratch["stage_sems"] = dma((len(staged),))
        names = list(inputs) + list(outputs) + list(scratch)
        return pl.pallas_call(
            functools.partial(kernel, *sizes, names),
            out_shape=tuple(shape for shape, _ in outputs.values()),
            in_specs=[spec for _, spec in inputs.values()],
            out_specs=tuple(spec for _, spec in outputs.values()),
            scratch_shapes=list(scratch.values()),
            compiler_params=pltpu.CompilerParams(
                collective_id=number, has_side_effects=True, vmem_limit_bytes=VMEM_LIMIT
            ),
            name=name,
        )(*[array for array, _ in inputs.values()])

    if resident:
        new_memory, embedding, total = call(
            whole_kernel,
            (front_sizes, reduce_sizes),
            "whole_step",
            0,
            front_in | event_in | index_in,
            memory_out | event_out,
            front_scratch
            | event_scratch
            | {
                "whole": buffer(max(table_rows, close_rows), LANES),
                "table": pltpu.VMEM((table_rows // stride, stride, LANES), F32),
            },
            FRONT_STAGED + EVENT_STAGED,
        )
    else:
        new_memory, whole = call(
            front_kernel,
            (front_sizes,),
            "front_step",
            0,
            front_in,
            memory_out | {"whole": (jax.ShapeDtypeStruct((table_rows, LANES), BF), hbm)},
            front_scratch,
            FRONT_STAGED,
        )
        rows = pl.pallas_call(
            fetch_kernel,
            out_shape=jax.ShapeDtypeStruct(((fanout + 1) * events * stride, LANES), F32),
            in_specs=[smem, smem, hbm],
            out_specs=hbm,
            scratch_shapes=[dma],
            name="fetch_step",
        )(neighbours.T, event_node, whole.astype(F32))
        embedding, total = call(
            event_kernel,
            (reduce_sizes,),
            "event_step",
            1,
            event_in | {"rows": (rows, hbm)},
            event_out,
            event_scratch | {"close": buffer(close_rows, LANES), "fetch_sem": dma},
            EVENT_STAGED,
        )
    per = 2
    grad_shape = jax.ShapeDtypeStruct((columns, columns), F32)
    *grads, embedding, new_memory = pl.pallas_call(
        functools.partial(finish_kernel, (1, 0, 2, 3)),
        out_shape=(grad_shape,) * 4
        + (
            jax.ShapeDtypeStruct(embedding.shape, BF),
            jax.ShapeDtypeStruct(new_memory.shape, BF),
        ),
        in_specs=[hbm] * 3,
        out_specs=(hbm,) * 6,
        scratch_shapes=[
            buffer(4 * columns, columns),
            buffer(4 * columns, columns, F32),
            buffer(events, columns),
            buffer(node_rows, columns),
            dma((4 * per,)),
            dma((4 * per,)),
            dma((2,)),
            dma((2,)),
        ],
        compiler_params=pltpu.CompilerParams(vmem_limit_bytes=VMEM_LIMIT),
        name="finish_step",
    )(total, embedding, new_memory)
    return (embedding, new_memory) + tuple(grads)


def solution(mesh):
    placed = (
        P("node"),
        P("node", None),
        P("node"),
        P("node", None),
        P("node", None),
        P("node", None),
        P("node", None),
        P("node", None),
        P(),
        P(),
        P(),
        P(),
        P(),
        P(),
        P(),
        P(),
        P(),
        P(),
    )
    return jax.shard_map(
        shards,
        mesh=mesh,
        in_specs=placed,
        out_specs=(P("node", None), P("node", None), P(), P(), P(), P()),
        check_vma=False,
    )
```

```python
import functools
import math

import jax
import jax.numpy as jnp
from jax import lax
from jax.experimental import pallas as pl
from jax.experimental.pallas import tpu as pltpu
from jax.sharding import PartitionSpec as P

HEADS = 2
LANES = 128
GROUP = 32
BF = jnp.bfloat16
F32 = jnp.float32
VMEM_LIMIT = 60 * 1024 * 1024
RESIDENT_LIMIT = 20 * 1024 * 1024
NT = (((1,), (1,)), ((), ()))
TN = (((0,), (0,)), ((), ()))


def mm(a, b):
    return jnp.dot(a, b, preferred_element_type=F32)


def mm_nt(a, b):
    return lax.dot_general(a, b, NT, preferred_element_type=F32)


def mm_tn(a, b):
    return lax.dot_general(a, b, TN, preferred_element_type=F32)


def halves(table):
    high = table.astype(BF)
    low = (table - high.astype(F32)).astype(BF)
    return high, low


def reduce_phase(line, side, strands, factor, r, meet, steps):
    (grads, result, near, pair) = (r.grads, r.result, r.swapped, r.pair)
    (plane_land, plane_sum, line_land) = (r.plane_land, r.plane_sum, r.line_land)
    (pair_send, pair_recv, plane_send, plane_recv, line_send, line_recv) = r.out_sems
    (line_back_send, line_back_recv, plane_back_send, plane_back_recv) = r.back_sems[:4]
    hop_send, hop_recv = r.back_sems[4:]
    me = lax.axis_index("node")
    core = lax.rem(me, 2)
    chip = me // 2
    partner = me + 1 - 2 * core
    plane = side * side
    spot, far = lax.rem(chip, plane), chip // plane
    half = grads.shape[0] // 2
    rows = half // strands
    rows_p = rows // plane
    rows_z = rows_p // line
    mesh_id = pl.DeviceIdType.MESH

    def across(place, step, count):
        if count & (count - 1):
            return lax.rem(place + step, count)
        bit = 1
        out = place
        while bit <= step:
            if step & bit:
                out += bit - 2 * bit * lax.rem(place // bit, 2)
            bit *= 2
        return out

    spots = [across(spot, step, plane) for step in range(plane - 1, 0, -1)]
    fars = [across(far, step, line) for step in range(line - 1, 0, -1)]

    def spot_device(place):
        return me + (place - spot) * 2

    def far_device(place):
        return me + (place - far) * (2 * plane)

    everyone = (
        [partner]
        + [spot_device(place) for place in spots]
        + [far_device(place) for place in fars]
    )
    if meet:
        barrier = pltpu.get_barrier_semaphore()
        for device in everyone:
            pl.semaphore_signal(barrier, inc=1, device_id=(device,), device_id_type=mesh_id)
        pl.semaphore_wait(barrier, len(everyone))

    def span(start, size):
        return pl.ds(pl.multiple_of(start, 16), size)

    def remote(src, dst, send, recv, device):
        return pltpu.make_async_remote_copy(
            src_ref=src,
            dst_ref=dst,
            send_sem=send,
            recv_sem=recv,
            device_id=(device,),
            device_id_type=mesh_id,
        )

    def swap(s):
        return remote(
            grads.at[span((1 - core) * half + s * rows, rows)],
            near.at[span(s * rows, rows)],
            pair_send.at[s],
            pair_recv.at[s],
            partner,
        )

    def to_plane(s, place, source):
        return remote(
            pair.at[span(s * rows + place * rows_p, rows_p)],
            plane_land.at[span(s * rows + source * rows_p, rows_p)],
            plane_send.at[s, place],
            plane_recv.at[s, source],
            spot_device(place),
        )

    def to_far(s, place, source):
        return remote(
            plane_sum.at[span(s * rows_p + place * rows_z, rows_z)],
            line_land.at[span(s * rows_p + source * rows_z, rows_z)],
            line_send.at[s, place],
            line_recv.at[s, source],
            far_device(place),
        )

    def place_of(which, s, q, f=0):
        return which * half + s * rows + q * rows_p + f * rows_z

    def spread(at, send, recv, device):
        return remote(result.at[at], result.at[at], send, recv, device)

    def back_far(s, place, source):
        at = span(place_of(core, s, spot, source), rows_z)
        return spread(at, line_back_send.at[s, place], line_back_recv.at[s, source], far_device(place))

    def back_plane(s, place, source):
        at = span(place_of(core, s, source), rows_p)
        return spread(
            at, plane_back_send.at[s, place], plane_back_recv.at[s, source], spot_device(place)
        )

    def hop(s, which):
        at = span(place_of(which, s, 0), rows)
        return spread(at, hop_send.at[s], hop_recv.at[s], partner)

    started = []

    def start(made):
        made.start()
        started.append(made)

    def stage_pair(s):
        swap(s).wait_recv()
        at = span(s * rows, rows)
        own = grads[span(core * half + s * rows, rows), :]
        pair[at, :] = (own.astype(F32) + near[at, :].astype(F32)).astype(BF)
        for place in spots:
            start(to_plane(s, place, spot))

    def stage_plane(s):
        total = pair[span(s * rows + spot * rows_p, rows_p), :].astype(F32)
        for place in spots:
            to_plane(s, place, place).wait_recv()
            total += plane_land[span(s * rows + place * rows_p, rows_p), :].astype(F32)
        plane_sum[span(s * rows_p, rows_p), :] = total.astype(BF)
        for place in fars:
            start(to_far(s, place, far))

    def stage_line(s):
        total = plane_sum[span(s * rows_p + far * rows_z, rows_z), :].astype(F32)
        for place in fars:
            to_far(s, place, place).wait_recv()
            total += line_land[span(s * rows_p + place * rows_z, rows_z), :].astype(F32)
        result[span(place_of(core, s, spot, far), rows_z), :] = (total * factor).astype(BF)
        for place in fars:
            start(back_far(s, place, far))

    def stage_back_line(s):
        for place in fars:
            back_far(s, place, place).wait_recv()
        for place in spots:
            start(back_plane(s, place, spot))

    def stage_back_plane(s):
        for place in spots:
            back_plane(s, place, place).wait_recv()
        start(hop(s, core))

    early = strands // 2
    steps[0]()
    for s in range(early):
        start(swap(s))
    steps[1]()
    for s in range(early):
        stage_pair(s)
    steps[2]()
    for s in range(early, strands):
        start(swap(s))
    steps[3]()
    for s in range(early, strands):
        stage_pair(s)
    stages = [stage_plane, stage_line, stage_back_line, stage_back_plane]
    for step in range(strands + len(stages) - 1):
        for number, stage in enumerate(stages):
            if 0 <= step - number < strands:
                stage(step - number)
    leaving = []
    for s in range(strands):
        hop(s, 1 - core).wait_recv()
        for which in range(2):
            at = pl.ds(which * half + s * rows, rows)
            leaving.append(
                pltpu.make_async_copy(result.at[at], r.result_out.at[at], r.result_sems.at[s, which])
            )
            leaving[-1].start()
    for made in started:
        made.wait_send()
    for copy in leaving:
        copy.wait()


def gather_blocks(
    line,
    side,
    subs,
    own,
    whole,
    recv,
    hop_recv,
    line_send,
    first_send,
    second_send,
    hop_send,
    own_sem,
    prepare,
    idle,
    arrived,
):
    me = lax.axis_index("node")
    core = lax.rem(me, 2)
    chip = me // 2
    partner = me + 1 - 2 * core
    low, mid, far = lax.rem(chip, side), lax.rem(chip // side, side), chip // (side * side)
    first = (1 - core) * low + core * mid
    second = (1 - core) * mid + core * low
    first_stride = 1 + core * (side - 1)
    second_stride = side - core * (side - 1)
    plane = side * side
    rows = own.shape[0]
    size = rows // subs
    mesh_id = pl.DeviceIdType.MESH

    def chip_of(place, over, across):
        return (
            place * plane
            + lax.rem(first + over, side) * first_stride
            + lax.rem(second + across, side) * second_stride
        )

    first_peers = [2 * chip_of(far, step, 0) + core for step in range(1, side)]
    second_peers = [2 * chip_of(far, 0, step) + core for step in range(1, side)]

    def at(source, part, kind):
        return pl.ds(pl.multiple_of((2 * source + kind) * rows + part * size, 16), size)

    def piece(source, part, kind, mine):
        return own.at[pl.ds(part * size, size)] if mine else whole.at[at(source, part, kind)]

    def copy(source, part, mine, send_sem, device):
        return pltpu.make_async_remote_copy(
            src_ref=piece(source, part, core, mine),
            dst_ref=whole.at[at(source, part, core)],
            send_sem=send_sem,
            recv_sem=recv.at[source * subs + part],
            device_id=(device,),
            device_id_type=mesh_id,
        )

    def hop(source, part, mine, kind):
        return pltpu.make_async_remote_copy(
            src_ref=piece(source, part, kind, mine),
            dst_ref=whole.at[at(source, part, kind)],
            send_sem=hop_send.at[source * subs + part],
            recv_sem=hop_recv.at[source * subs + part],
            device_id=(partner,),
            device_id_type=mesh_id,
        )

    def along(place, part, mine, way):
        return copy(
            chip_of(place, 0, 0),
            part,
            mine,
            line_send.at[place * subs + part, way],
            me + (1 - 2 * way) * 2 * plane,
        )

    def over_first(place, part, mine, to):
        return copy(
            chip_of(place, 0, 0), part, mine, first_send.at[place * subs + part, to], first_peers[to]
        )

    def over_second(place, over, part, mine, to):
        return copy(
            chip_of(place, over, 0),
            part,
            mine,
            second_send.at[place * subs + part, over, to],
            second_peers[to],
        )

    def landed(source, part):
        copy(source, part, False, hop_send.at[0], partner).wait_recv()

    def settle(source, part, kind):
        if arrived is not None:
            start = pl.multiple_of((2 * source + kind) * rows + part * size, 16)
            arrived(whole, start, start, size)

    stay = None
    if arrived is None:
        mine_at = pl.ds(pl.multiple_of(me * rows, 16), rows)
        stay = pltpu.make_async_copy(own, whole.at[mine_at], own_sem)

    def arrive(place, part, mine, ways):
        source = chip_of(place, 0, 0)
        if mine:
            prepare(part)
        else:
            landed(source, part)
        for way in ways:
            open_end = far < line - 1 if way == 0 else far > 0

            @pl.when(open_end)
            def _(way=way):
                along(place, part, mine, way).start()

        for to in range(side - 1):
            over_first(place, part, mine, to).start()
        for to in range(side - 1):
            over_second(place, 0, part, mine, to).start()
        hop(source, part, mine, core).start()
        if not mine:
            settle(source, part, core)
        elif arrived is not None:
            arrived(own, part * size, pl.multiple_of(me * rows + part * size, 16), size)
        if mine and part == subs - 1:
            if stay is not None:
                stay.start()
            idle()

    def pass_on(place, part):
        for over in range(1, side):
            source = chip_of(place, over, 0)
            landed(source, part)
            for to in range(side - 1):
                over_second(place, over, part, False, to).start()
            hop(source, part, False, core).start()
            settle(source, part, core)

    def finish(place, part):
        for across in range(1, side):
            for over in range(side):
                source = chip_of(place, over, across)
                landed(source, part)
                hop(source, part, False, core).start()
                settle(source, part, core)

    def receive_hops(place, part):
        for over in range(side):
            for across in range(side):
                source = chip_of(place, over, across)
                hop(source, part, False, 1 - core).wait_recv()
                settle(source, part, 1 - core)

    units = [(0, 0)] + [(reach, way) for reach in range(1, line) for way in range(2)]
    work = [(reach, way, part) for reach, way in units for part in range(subs)]

    def run(item, stage):
        reach, way, part = item
        place = far - reach if way == 0 else far + reach

        def body():
            if stage == 0:
                arrive(place, part, reach == 0, (0, 1) if reach == 0 else (way,))
            elif stage == 1:
                pass_on(place, part)
            elif stage == 2:
                finish(place, part)
            else:
                receive_hops(place, part)

        if reach == 0:
            body()
        else:
            pl.when(place >= 0 if way == 0 else place < line)(body)

    lags = (0, 4, 8, 10)
    for step in range(len(work) + lags[-1]):
        for stage, lag in enumerate(lags):
            if 0 <= step - lag < len(work):
                run(work[step - lag], stage)
    if stay is not None:
        stay.wait()

    def drain(place, carry):
        for part in range(subs):
            for to in range(side - 1):
                over_first(place, part, False, to).wait_send()
                for over in range(side):
                    over_second(place, over, part, False, to).wait_send()

            @pl.when((place <= far) & (far < line - 1))
            def _(part=part):
                along(place, part, False, 0).wait_send()

            @pl.when((place >= far) & (far > 0))
            def _(part=part):
                along(place, part, False, 1).wait_send()

            for over in range(side):
                for across in range(side):
                    hop(chip_of(place, over, across), part, False, core).wait_send()
        return carry

    lax.fori_loop(0, line, drain, 0)


def front_phase(devices, slots, line, side, subs, r, idle, late_idle, arrived):
    me = lax.axis_index("node")
    (node, bucket, feats, memory) = (r.node, r.bucket, r.feats, r.memory)
    (outgoing, inbox, sel, meta, hidden) = (r.outgoing, r.inbox, r.sel, r.meta, r.hidden)
    (picked, picked_meta, totals, counts) = (r.picked, r.picked_meta, r.totals, r.counts)
    (send_sems, recv_sems) = (r.send_sems, r.recv_sems)
    events = feats.shape[0]
    rows, columns = memory.shape
    stride = columns // LANES
    batch = 4
    mesh_id = pl.DeviceIdType.MESH
    barrier = pltpu.get_barrier_semaphore()

    def greet(step, carry):
        pl.semaphore_signal(
            barrier, inc=1, device_id=(lax.rem(me + step, devices),), device_id_type=mesh_id
        )
        return carry

    lax.fori_loop(1, devices, greet, 0)

    ids = lax.broadcasted_iota(jnp.int32, (devices, events), 0) * rows
    names = node[...]
    theirs = (names >= ids) & (names < ids + rows)
    before = lax.broadcasted_iota(jnp.int32, (events, events), 0) < lax.broadcasted_iota(
        jnp.int32, (events, events), 1
    )
    rank = mm(theirs.astype(F32).astype(BF), before.astype(F32).astype(BF))
    sel[...] = jnp.where(theirs, rank, -1.0)
    within = jnp.sum(jnp.where(theirs, names - ids, 0).astype(F32), axis=0, keepdims=True)
    kind = lax.broadcasted_iota(jnp.int32, (16, events), 0)
    meta[...] = jnp.where(
        kind == 0,
        within,
        jnp.where(kind == 1, bucket[...].astype(F32), jnp.where(kind == 2, 1.0, 0.0)),
    ).astype(BF)
    slot_ids = lax.broadcasted_iota(jnp.int32, (slots, events), 0).astype(F32)
    lane_ids = lax.broadcasted_iota(jnp.int32, (LANES, events), 0).astype(F32)
    pl.semaphore_wait(barrier, devices - 1)

    def send(peer):
        return pltpu.make_async_remote_copy(
            src_ref=outgoing.at[peer],
            dst_ref=inbox.at[me],
            send_sem=send_sems.at[peer],
            recv_sem=recv_sems.at[me],
            device_id=(peer,),
            device_id_type=mesh_id,
        )

    def receive(peer):
        return pltpu.make_async_remote_copy(
            src_ref=outgoing.at[peer],
            dst_ref=inbox.at[peer],
            send_sem=send_sems.at[peer],
            recv_sem=recv_sems.at[peer],
            device_id=(peer,),
            device_id_type=mesh_id,
        )

    def pack_batch(step, own):
        peers = [lax.rem(me + step * batch + part, devices) for part in range(batch)]
        picks = [sel[pl.ds(peer, 1), :] for peer in peers]
        hits = jnp.concatenate([(slot_ids == row).astype(F32) for row in picks], axis=0)
        turned = jnp.concatenate([(lane_ids == row).astype(F32) for row in picks], axis=0)
        rows_of = mm(hits.astype(BF), feats[...]).astype(BF)
        info = mm_nt(meta[...], turned.astype(BF)).astype(BF)
        for part, peer in enumerate(peers):
            lines = slice(part * slots, (part + 1) * slots)
            lanes = slice(part * LANES, (part + 1) * LANES)
            if own and part == 0:
                inbox[me, :slots, :] = rows_of[lines, :]
                inbox[me, slots:, :] = info[:, lanes]
            else:
                outgoing[peer, :slots, :] = rows_of[lines, :]
                outgoing[peer, slots:, :] = info[:, lanes]
                send(peer).start()

    pack_batch(0, True)

    def pack_rest(step, carry):
        pack_batch(step, False)
        return carry

    lax.fori_loop(1, devices // batch, pack_rest, 0)

    r.need("hidden_weight")
    previous = memory[...]
    for part in range(3):
        cut = slice(part * columns, (part + 1) * columns)
        hidden[:, cut] = mm(previous, r.hidden_weight[:, cut])
    idle()
    totals[...] = jnp.zeros_like(totals)
    counts[...] = jnp.zeros_like(counts)
    high, low = halves(r.time_message[...])
    weight = r.edge_weight[...]
    turn = (
        lax.broadcasted_iota(jnp.int32, (slots, LANES), 0)
        == lax.broadcasted_iota(jnp.int32, (slots, LANES), 1)
    ).astype(F32).astype(BF)
    chunk = batch * slots

    def add_batch(step, own):
        for part in range(batch):
            peer = lax.rem(me + devices - step * batch - part, devices)
            if not (own and part == 0):
                receive(peer).wait_recv()
            at = slice(part * slots, (part + 1) * slots)
            picked[at, :] = inbox[peer, :slots, :]
            picked_meta[at, :] = mm_nt(turn, inbox[peer, slots:, :])
        info = picked_meta[...]
        place, when, valid = info[:, 0:1], info[:, 1:2], info[:, 2:3]
        lanes = lax.broadcasted_iota(jnp.int32, (chunk, high.shape[0]), 1).astype(F32)
        picks = (lanes == when).astype(F32).astype(BF)
        pre = mm(picked[...], weight) + mm(picks, high) + mm(picks, low)
        message = (pre / (1.0 + jnp.exp(-pre))).astype(BF)
        node_ids = lax.broadcasted_iota(jnp.int32, (chunk, rows), 1).astype(F32)
        marks = jnp.where(node_ids == place, valid, 0.0).astype(BF)
        totals[...] += mm_tn(marks, message)
        counts[...] += mm_tn(marks, jnp.ones((chunk, LANES), BF))

    add_batch(0, True)

    def add_rest(step, carry):
        add_batch(step, False)
        return carry

    lax.fori_loop(1, devices // batch, add_rest, 0)

    r.need("input_weight")

    def prepare(part):
        size = rows // subs
        at = slice(part * size, (part + 1) * size)
        count = counts[at, 0:1]
        aggregate = (totals[at, :] / jnp.maximum(count, 1.0)).astype(BF)

        def gate(which):
            cut = slice(which * columns, (which + 1) * columns)
            bias = jnp.concatenate(
                [r.gate_bias[which * stride + p : which * stride + p + 1, :] for p in range(stride)],
                axis=1,
            )
            return mm(aggregate, r.input_weight[:, cut]) + bias, hidden[at, cut]

        from_input, from_hidden = gate(0)
        update = jax.nn.sigmoid(from_input + from_hidden)
        from_input, from_hidden = gate(1)
        resets = jax.nn.sigmoid(from_input + from_hidden)
        from_input, from_hidden = gate(2)
        candidate = jnp.tanh(from_input + resets * from_hidden)
        old = memory[at, :].astype(F32)
        fresh = (1.0 - update) * candidate + update * old
        fresh = jnp.where(count > 0, fresh, old)
        r.out_memory[at, :] = fresh.astype(BF)
        first = part * size * stride
        for p in range(stride):
            r.wide[pl.ds(first + p, size, stride=stride), :] = fresh[:, p * LANES : (p + 1) * LANES]
        at = slice(first, first + size * stride)
        r.own_table[at, :] = r.wide[at, :].astype(BF)
        if part == subs - 1:
            r.leave("out_memory")

    gather_blocks(
        line,
        side,
        subs,
        r.own_table,
        r.whole,
        r.gather_recv,
        r.gather_hop_recv,
        r.gather_line_send,
        r.gather_first_send,
        r.gather_second_send,
        r.gather_hop_send,
        r.gather_own,
        prepare,
        late_idle,
        arrived,
    )

    def drain(step, carry):
        send(lax.rem(me + step, devices)).wait_send()
        return carry

    lax.fori_loop(1, devices, drain, 0)


def keep(blocks, tall, dest, kind, values):
    upper, lower = halves(values)
    for b in range(blocks):
        rows = slice(b * GROUP, (b + 1) * GROUP)
        first = b * tall + kind * GROUP
        dest[first : first + GROUP, :] = upper[rows, :]
        first += 2 * HEADS * GROUP
        dest[first : first + GROUP, :] = lower[rows, :]


def head_cuts(columns):
    head = columns // HEADS
    return [slice(h * head, (h + 1) * head) for h in range(HEADS)]


def early_products(r):
    events, columns = r.back.shape
    blocks = events // GROUP
    tall = 4 * HEADS * GROUP
    r.need("upstream")
    r.need("out_weight")
    r.need("value_weight")
    r.back[...] = mm_nt(r.upstream[...], r.out_weight[...]).astype(BF)
    for h, cut in enumerate(head_cuts(columns)):
        keep(blocks, tall, r.pull, HEADS + h, mm_nt(r.back[:, cut], r.value_weight[:, cut]))
        keep(blocks, tall, r.pull_time, HEADS + h, jnp.zeros((events, LANES), F32))


def early_marks(r):
    fanout, events = r.buckets.shape
    blocks = events // GROUP
    wide = fanout * GROUP
    even = (
        lax.broadcasted_iota(jnp.int32, (fanout, LANES), 0)
        == lax.broadcasted_iota(jnp.int32, (fanout, LANES), 1)
    ).astype(F32).astype(BF)
    r.names[...] = mm_tn(r.buckets[...].astype(F32).astype(BF), even)
    r.logits[...] = jnp.zeros_like(r.logits)
    r.logits[:fanout, :] = r.affinity[...]
    lane_names = lax.broadcasted_iota(jnp.int32, (GROUP, LANES), 1).astype(F32)

    def mark(b, carry):
        mine = r.names[pl.ds(pl.multiple_of(b * GROUP, GROUP), GROUP), :]
        for j in range(fanout):
            at = pl.ds(pl.multiple_of(b * wide + j * GROUP, GROUP), GROUP)
            r.hot[at, :] = (lane_names == mine[:, j : j + 1]).astype(F32).astype(BF)
        return carry

    lax.fori_loop(0, blocks, mark, 0)


def event_phase(r, fetch_targets, fetch_block):
    events, columns = r.back.shape
    fanout = r.buckets.shape[0]
    head = columns // HEADS
    stride = columns // LANES
    kinds = 2 * HEADS
    blocks = events // GROUP
    wide = fanout * GROUP
    tall = 2 * kinds * GROUP
    rows_all = fanout * events
    heads = head_cuts(columns)
    (target, query, pull, pull_time) = (r.target, r.query, r.pull, r.pull_time)
    (mix, hits, scores, close, hot, logits) = (r.mix, r.hits, r.scores, r.close, r.hot, r.logits)
    high, low = halves(r.time_key[...])
    lane = lax.broadcasted_iota(jnp.int32, (GROUP, LANES), 1)

    fetch_targets()
    fetch_block(0, r.near[0])
    for part in range(stride):
        target[:, part * LANES : (part + 1) * LANES] = r.own_near[
            pl.ds(part, events, stride=stride), :
        ].astype(BF)
    r.need("query_weight")
    r.need("key_weight")
    query[...] = mm(target[...], r.query_weight[...]).astype(BF)
    for h, cut in enumerate(heads):
        keep(blocks, tall, pull, h, mm_nt(query[:, cut], r.key_weight[:, cut]))
        keep(
            blocks,
            tall,
            pull_time,
            h,
            mm_nt(query[:, cut], high[:, cut]) + mm_nt(query[:, cut], low[:, cut]),
        )

    scale = 1.0 / math.sqrt(head)
    pad = scores.shape[0] // blocks
    own = lax.rem(lane, GROUP) == lax.broadcasted_iota(jnp.int32, (GROUP, LANES), 0)
    row_ids = lax.broadcasted_iota(jnp.int32, (pad, LANES), 0)
    lane_ids = lax.broadcasted_iota(jnp.int32, (pad, LANES), 1)
    forward = lane_ids < HEADS * GROUP
    per_row = LANES // GROUP

    def close_rows(b):
        return jnp.concatenate(
            [
                close[pl.ds(pl.multiple_of(part * rows_all + b * wide, GROUP), wide), :]
                for part in range(stride)
            ],
            axis=1,
        )

    def score(b, near):
        for part in range(stride):
            at = pl.ds(pl.multiple_of(part * rows_all + b * wide, GROUP), wide)
            close[at, :] = near[pl.ds(part, wide, stride=stride), :].astype(BF)
        at = pl.ds(pl.multiple_of(b * wide, GROUP), wide)
        from_at = pl.ds(pl.multiple_of(b * tall, GROUP), tall)
        both = mm_nt(close_rows(b), pull[from_at, :]) + mm_nt(hot[at, :], pull_time[from_at, :])
        both = both[:, :LANES] + both[:, LANES:]
        raw = jnp.zeros((pad, LANES), F32)
        for j in range(fanout):
            line = jnp.where(own, both[j * GROUP : (j + 1) * GROUP, :], 0.0)
            raw = jnp.where(row_ids == j, jnp.sum(line, axis=0, keepdims=True), raw)
        chunk = pl.multiple_of(b // per_row * LANES, LANES)
        piece = logits[:, pl.ds(chunk, LANES)]
        piece = pltpu.roll(piece, lax.rem(LANES - lax.rem(b, per_row) * GROUP, LANES), axis=1)
        given = piece
        for h in range(1, HEADS):
            moved = pltpu.roll(piece, h * GROUP, axis=1)
            given = jnp.where(lane_ids >= h * GROUP, moved, given)
        scores[pl.ds(pl.multiple_of(b * pad, pad), pad), :] = jnp.where(
            forward, raw * scale + given, raw
        )

    def score_two(step, carry):
        b = step * 2
        fetch_block(b + 1, r.near[1])
        score(b, r.near[0])
        fetch_block(b + 2, r.near[0])
        score(b + 1, r.near[1])
        return carry

    lax.fori_loop(0, blocks // 2 - 1, score_two, 0)
    fetch_block(blocks - 1, r.near[1])
    score(blocks - 2, r.near[0])
    score(blocks - 1, r.near[1])

    for b in range(blocks):
        at = slice(b * pad, (b + 1) * pad)
        here = scores[at, :]
        active = row_ids < fanout
        top = jnp.max(jnp.where(active, here, -3.0e38), axis=0, keepdims=True)
        raised = jnp.where(active, jnp.exp(jnp.where(active, here - top, 0.0)), 0.0)
        probs = raised / jnp.sum(raised, axis=0, keepdims=True)
        slopes = pltpu.roll(here, HEADS * GROUP, axis=1).astype(BF).astype(F32)
        inner = jnp.sum(probs * slopes, axis=0, keepdims=True)
        slopes = probs * (slopes - inner) * scale
        scores[at, :] = jnp.where(forward, probs, pltpu.roll(slopes, HEADS * GROUP, axis=1))

    def blend(b):
        weights = scores[pl.ds(pl.multiple_of(b * pad, pad), pad), :]
        spread = jnp.concatenate(
            [
                jnp.where(own, jnp.broadcast_to(weights[j : j + 1, :], (GROUP, LANES)), 0.0)
                for j in range(fanout)
            ],
            axis=0,
        ).astype(BF)
        at = pl.ds(pl.multiple_of(b * wide, GROUP), wide)
        mixed = mm_tn(spread, close_rows(b)).astype(BF)
        times = mm_tn(spread, hot[at, :]).astype(BF)
        to = pl.ds(pl.multiple_of(b * GROUP, GROUP), GROUP)
        for k in range(kinds):
            mix[k, to, :] = mixed[k * GROUP : (k + 1) * GROUP, :]
        for h in range(HEADS):
            hits[h, to, :] = times[(HEADS + h) * GROUP : (HEADS + h + 1) * GROUP, :]

    def blend_four(step, carry):
        for place in range(4):
            blend(step * 4 + place)
        return carry

    lax.fori_loop(0, blocks // 4, blend_four, 0)


def gradient_steps(r):
    (target, query, back, mix, hits, grads) = (r.target, r.query, r.back, r.mix, r.hits, r.grads)
    events, columns = back.shape
    heads = head_cuts(columns)
    high, low = halves(r.time_key[...])

    def value_and_key():
        for h, cut in enumerate(heads):
            grads[2 * columns : 3 * columns, cut] = mm_tn(mix[h], back[:, cut]).astype(BF)
            grads[:columns, cut] = mm_tn(mix[HEADS + h], query[:, cut]).astype(BF)

    def cotangents():
        for h, cut in enumerate(heads):
            back[:, cut] = mm(mix[h], r.value_weight[:, cut]).astype(BF)
            query[:, cut] = (
                mm(mix[HEADS + h], r.key_weight[:, cut])
                + mm(hits[h], high[:, cut])
                + mm(hits[h], low[:, cut])
            ).astype(BF)

    def query_and_out():
        grads[columns : 2 * columns, :] = mm_tn(target[...], query[...]).astype(BF)
        grads[3 * columns :, :] = mm_tn(back[...], r.upstream[...]).astype(BF)

    def embed():
        r.embedding[...] = (mm(back[...], r.out_weight[...]) + target[...].astype(F32)).astype(BF)
        r.leave("embedding")

    return value_and_key, cotangents, query_and_out, embed


class Refs:
    def __init__(self, names, refs, staged):
        for name, ref in zip(names, refs, strict=True):
            setattr(self, name, ref)
        self.copies = {}
        self.leaving = []
        for place, name in enumerate(staged):
            copy = pltpu.make_async_copy(
                getattr(self, name), getattr(self, name + "_here"), self.stage_sems.at[place]
            )
            copy.start()
            self.copies[name] = copy
            setattr(self, name, getattr(self, name + "_here"))
        if hasattr(self, "near_first"):
            self.near = (self.near_first, self.near_second)
        if hasattr(self, "grads"):
            self.out_sems = [getattr(self, name) for name in OUT_SEMS]
            self.back_sems = [getattr(self, name) for name in BACK_SEMS]

    def leave(self, name):
        copy = pltpu.make_async_copy(
            getattr(self, name), getattr(self, name + "_out"), getattr(self, name + "_sem")
        )
        copy.start()
        self.leaving.append(copy)

    def finish(self):
        for copy in self.leaving:
            copy.wait()

    def need(self, name):
        copy = self.copies.pop(name, None)
        if copy is not None:
            copy.wait()


OUT_SEMS = [f"out{place}" for place in range(6)]
BACK_SEMS = [f"back{place}" for place in range(6)]
FRONT_STAGED = ("hidden_weight", "input_weight")
EVENT_STAGED = ("upstream", "out_weight", "value_weight", "query_weight", "key_weight")


def front_kernel(sizes, names, *refs):
    r = Refs(names, refs, FRONT_STAGED)
    front_phase(*sizes, r, lambda: None, lambda: None, None)
    r.finish()


def fetch_kernel(ids, own_ids, source, dest, sem):
    fanout, events = ids.shape
    stride = dest.shape[0] // ((fanout + 1) * events)
    wide = fanout * GROUP

    def request(start, row):
        pltpu.make_async_copy(
            source.at[pl.ds(pl.multiple_of(start * stride, stride), stride)],
            dest.at[pl.ds(pl.multiple_of(row * stride, stride), stride)],
            sem,
        ).start()

    def request_all(e, carry):
        for j in range(fanout):
            request(ids[j, e], e // GROUP * wide + j * GROUP + e % GROUP)
        request(own_ids[e], fanout * events + e)
        return carry

    lax.fori_loop(0, events, request_all, 0)
    pltpu.make_async_copy(source.at[pl.ds(0, dest.shape[0])], dest, sem).wait()


def event_kernel(reduce_sizes, names, *refs):
    r = Refs(names, refs, EVENT_STAGED)
    fanout, events = r.buckets.shape
    block_rows = r.near_first.shape[0]
    early_products(r)
    early_marks(r)

    def fetch_targets():
        copy = pltpu.make_async_copy(
            r.rows.at[pl.ds(events // GROUP * block_rows, r.own_near.shape[0])],
            r.own_near,
            r.fetch_sem,
        )
        copy.start()
        copy.wait()

    def fetch_block(b, near):
        first = pl.multiple_of(b * block_rows, block_rows)
        copy = pltpu.make_async_copy(r.rows.at[pl.ds(first, block_rows)], near, r.fetch_sem)
        copy.start()
        copy.wait()

    event_phase(r, fetch_targets, fetch_block)
    reduce_phase(*reduce_sizes, r, True, gradient_steps(r))
    r.finish()


def whole_kernel(front_sizes, reduce_sizes, names, *refs):
    r = Refs(names, refs, FRONT_STAGED + EVENT_STAGED)
    fanout, events = r.buckets.shape
    stride = r.own_near.shape[0] // events
    table = r.table
    r.close = r.whole

    def arrived(source, first, start, size):
        step_rows = 128

        def widen(step, carry):
            from_at = pl.ds(pl.multiple_of(first + step * step_rows, 16), step_rows)
            to_at = pl.ds((start + step * step_rows) // stride, step_rows // stride)
            rows = source[from_at, :].astype(F32)
            table[to_at] = rows.reshape(step_rows // stride, stride, LANES)
            return carry

        lax.fori_loop(0, size // step_rows, widen, 0)

    front_phase(*front_sizes, r, lambda: early_products(r), lambda: early_marks(r), arrived)

    def move(start, dest, row):
        dest[pl.ds(pl.multiple_of(row * stride, stride), stride), :] = table[start]

    def fetch_targets():
        unroll = 16

        def some(step, carry):
            for place in range(unroll):
                e = step * unroll + place
                move(r.own_ids[e], r.own_near, e)
            return carry

        lax.fori_loop(0, events // unroll, some, 0)

    def fetch_block(b, near):
        for e in range(GROUP):
            for j in range(fanout):
                move(r.ids[j, b * GROUP + e], near, j * GROUP + e)

    event_phase(r, fetch_targets, fetch_block)
    reduce_phase(*reduce_sizes, r, False, gradient_steps(r))
    r.finish()


def finish_kernel(order, total, embedding, memory, *rest):
    outs, (here, wide, *passing, read_sems, write_sems, in_sems, out_sems) = rest[:6], rest[6:]
    grads, kept = outs[:4], outs[4:]
    columns = grads[0].shape[0]
    per = read_sems.shape[0] // 4
    size = columns // per
    reads, writes, enter = [], [], []
    for place in range(4 * per):
        at = pl.ds(place * size, size)
        reads.append(pltpu.make_async_copy(total.at[at], here.at[at], read_sems.at[place]))
        reads[-1].start()
    for place, source in enumerate((embedding, memory)):
        enter.append(pltpu.make_async_copy(source, passing[place], in_sems.at[place]))
        enter[-1].start()
    for place in range(4 * per):
        at = pl.ds(place * size, size)
        reads[place].wait()
        wide[at, :] = here[at, :].astype(F32)
        to = grads[order[place // per]].at[pl.ds(place % per * size, size)]
        writes.append(pltpu.make_async_copy(wide.at[at], to, write_sems.at[place]))
        writes[-1].start()
    for place in range(2):
        enter[place].wait()
        writes.append(pltpu.make_async_copy(passing[place], kept[place], out_sems.at[place]))
        writes[-1].start()
    for copy in writes:
        copy.wait()


def shards(
    event_node,
    neighbours,
    event_bucket,
    neighbour_bucket,
    edge_features,
    affinity,
    upstream,
    node_memory,
    edge_weight,
    time_message,
    input_weight,
    hidden_weight,
    gate_bias,
    time_key,
    query_weight,
    key_weight,
    value_weight,
    out_weight,
):
    devices = lax.axis_size("node")
    node_rows, columns = node_memory.shape
    events, fanout = neighbours.shape
    features = edge_features.shape[1]
    stride = columns // LANES
    slots = -(-(3 * events // devices) // 16) * 16
    chips = devices // 2
    side = max(s for s in range(1, chips + 1) if chips % (s * s) == 0 and s**3 <= chips)
    line = chips // (side * side)
    subs = 2
    half = 2 * columns
    strands = max(1, min(4, half // (16 * chips)))
    factor = 1.0 / math.sqrt(events * devices)
    front_sizes = (devices, slots, line, side, subs)
    reduce_sizes = (line, side, strands, factor)
    table_rows = devices * node_rows * stride
    close_rows = fanout * events * stride
    resident = table_rows * LANES * 4 <= RESIDENT_LIMIT
    vmem = pl.BlockSpec(memory_space=pltpu.VMEM)
    smem = pl.BlockSpec(memory_space=pltpu.SMEM)
    hbm = pl.BlockSpec(memory_space=pl.ANY)
    dma = pltpu.SemaphoreType.DMA

    def buffer(rows, width, dtype=BF):
        return pltpu.VMEM((rows, width), dtype)

    front_in = {
        "node": (event_node.reshape(1, events), vmem),
        "bucket": (event_bucket.reshape(1, events), vmem),
        "feats": (edge_features, vmem),
        "memory": (node_memory, vmem),
        "edge_weight": (edge_weight, vmem),
        "time_message": (time_message, vmem),
        "input_weight": (input_weight, hbm),
        "hidden_weight": (hidden_weight, hbm),
        "gate_bias": (gate_bias.reshape(-1, LANES), vmem),
    }
    event_in = {
        "buckets": (neighbour_bucket.T, vmem),
        "affinity": (affinity.T, vmem),
        "upstream": (upstream, hbm),
        "time_key": (time_key, vmem),
        "query_weight": (query_weight, hbm),
        "key_weight": (key_weight, hbm),
        "value_weight": (value_weight, hbm),
        "out_weight": (out_weight, hbm),
    }
    index_in = {"ids": (neighbours.T, smem), "own_ids": (event_node, smem)}
    memory_out = {"out_memory_out": (jax.ShapeDtypeStruct((node_rows, columns), BF), hbm)}
    event_out = {
        "embedding_out": (jax.ShapeDtypeStruct((events, columns), BF), hbm),
        "result_out": (jax.ShapeDtypeStruct((2 * half, columns), BF), hbm),
    }
    front_scratch = {
        "outgoing": pltpu.VMEM((devices, slots + 16, features), BF),
        "inbox": pltpu.VMEM((devices, slots + 16, features), BF),
        "sel": buffer(devices, events, F32),
        "meta": buffer(16, events),
        "hidden": buffer(node_rows, 3 * columns, F32),
        "picked": buffer(4 * slots, features),
        "picked_meta": buffer(4 * slots, 16, F32),
        "totals": buffer(node_rows, columns, F32),
        "counts": buffer(node_rows, LANES, F32),
        "wide": buffer(node_rows * stride, LANES, F32),
        "own_table": buffer(node_rows * stride, LANES),
        "send_sems": dma((devices,)),
        "recv_sems": dma((devices,)),
        "gather_recv": dma((chips * subs,)),
        "gather_hop_recv": dma((chips * subs,)),
        "gather_line_send": dma((line * subs, 2)),
        "gather_first_send": dma((line * subs, side - 1)),
        "gather_second_send": dma((line * subs, side, side - 1)),
        "gather_hop_send": dma((chips * subs,)),
        "gather_own": dma,
        "out_memory": buffer(node_rows, columns),
        "out_memory_sem": dma,
    }
    event_scratch = {
        "target": buffer(events, columns),
        "query": buffer(events, columns),
        "back": buffer(events, columns),
        "pull": buffer(4 * HEADS * events, columns),
        "pull_time": buffer(4 * HEADS * events, LANES),
        "mix": pltpu.VMEM((2 * HEADS, events, columns), BF),
        "hits": pltpu.VMEM((HEADS, events, LANES), BF),
        "scores": buffer(events // GROUP * 16, LANES, F32),
        "hot": buffer(fanout * events, LANES),
        "names": buffer(events, LANES, F32),
        "logits": buffer(16, events, F32),
        "own_near": buffer(events * stride, LANES, F32),
        "near_first": buffer(fanout * GROUP * stride, LANES, F32),
        "near_second": buffer(fanout * GROUP * stride, LANES, F32),
        "grads": buffer(2 * half, columns),
        "swapped": buffer(half, columns),
        "pair": buffer(half, columns),
        "plane_land": buffer(half, columns),
        "plane_sum": buffer(half // (side * side), columns),
        "line_land": buffer(half // (side * side), columns),
        "embedding": buffer(events, columns),
        "embedding_sem": dma,
        "result": buffer(2 * half, columns),
        "result_sems": dma((strands, 2)),
    }
    plane = side * side
    for name, shape in zip(
        OUT_SEMS + BACK_SEMS,
        [(strands,)] * 2
        + [(strands, plane)] * 2
        + [(strands, line)] * 4
        + [(strands, plane)] * 2
        + [(strands,)] * 2,
    ):
        event_scratch[name] = dma(shape)

    def call(kernel, sizes, name, number, inputs, outputs, scratch, staged):
        scratch = dict(scratch)
        for key in staged:
            array = inputs[key][0]
            scratch[key + "_here"] = pltpu.VMEM(array.shape, array.dtype)
        scratch["stage_sems"] = dma((len(staged),))
        names = list(inputs) + list(outputs) + list(scratch)
        return pl.pallas_call(
            functools.partial(kernel, *sizes, names),
            out_shape=tuple(shape for shape, _ in outputs.values()),
            in_specs=[spec for _, spec in inputs.values()],
            out_specs=tuple(spec for _, spec in outputs.values()),
            scratch_shapes=list(scratch.values()),
            compiler_params=pltpu.CompilerParams(
                collective_id=number, has_side_effects=True, vmem_limit_bytes=VMEM_LIMIT
            ),
            name=name,
        )(*[array for array, _ in inputs.values()])

    if resident:
        new_memory, embedding, total = call(
            whole_kernel,
            (front_sizes, reduce_sizes),
            "whole_step",
            0,
            front_in | event_in | index_in,
            memory_out | event_out,
            front_scratch
            | event_scratch
            | {
                "whole": buffer(max(table_rows, close_rows), LANES),
                "table": pltpu.VMEM((table_rows // stride, stride, LANES), F32),
            },
            FRONT_STAGED + EVENT_STAGED,
        )
    else:
        new_memory, whole = call(
            front_kernel,
            (front_sizes,),
            "front_step",
            0,
            front_in,
            memory_out | {"whole": (jax.ShapeDtypeStruct((table_rows, LANES), BF), hbm)},
            front_scratch,
            FRONT_STAGED,
        )
        rows = pl.pallas_call(
            fetch_kernel,
            out_shape=jax.ShapeDtypeStruct(((fanout + 1) * events * stride, LANES), F32),
            in_specs=[smem, smem, hbm],
            out_specs=hbm,
            scratch_shapes=[dma],
            name="fetch_step",
        )(neighbours.T, event_node, whole.astype(F32))
        embedding, total = call(
            event_kernel,
            (reduce_sizes,),
            "event_step",
            1,
            event_in | {"rows": (rows, hbm)},
            event_out,
            event_scratch | {"close": buffer(close_rows, LANES), "fetch_sem": dma},
            EVENT_STAGED,
        )
    per = 2
    grad_shape = jax.ShapeDtypeStruct((columns, columns), F32)
    *grads, embedding, new_memory = pl.pallas_call(
        functools.partial(finish_kernel, (1, 0, 2, 3)),
        out_shape=(grad_shape,) * 4
        + (
            jax.ShapeDtypeStruct(embedding.shape, BF),
            jax.ShapeDtypeStruct(new_memory.shape, BF),
        ),
        in_specs=[hbm] * 3,
        out_specs=(hbm,) * 6,
        scratch_shapes=[
            buffer(4 * columns, columns),
            buffer(4 * columns, columns, F32),
            buffer(events, columns),
            buffer(node_rows, columns),
            dma((4 * per,)),
            dma((4 * per,)),
            dma((2,)),
            dma((2,)),
        ],
        compiler_params=pltpu.CompilerParams(vmem_limit_bytes=VMEM_LIMIT),
        name="finish_step",
    )(total, embedding, new_memory)
    return (embedding, new_memory) + tuple(grads)


def solution(mesh):
    placed = (
        P("node"),
        P("node", None),
        P("node"),
        P("node", None),
        P("node", None),
        P("node", None),
        P("node", None),
        P("node", None),
        P(),
        P(),
        P(),
        P(),
        P(),
        P(),
        P(),
        P(),
        P(),
        P(),
    )
    return jax.shard_map(
        shards,
        mesh=mesh,
        in_specs=placed,
        out_specs=(P("node", None), P("node", None), P(), P(), P(), P()),
        check_vma=False,
    )
```

```python
import functools
import math

import jax
import jax.numpy as jnp
from jax import lax
from jax.experimental import pallas as pl
from jax.experimental.pallas import tpu as pltpu
from jax.sharding import PartitionSpec as P

HEADS = 2
LANES = 128
GROUP = 32
BF = jnp.bfloat16
F32 = jnp.float32
VMEM_LIMIT = 60 * 1024 * 1024
RESIDENT_LIMIT = 20 * 1024 * 1024
NT = (((1,), (1,)), ((), ()))
TN = (((0,), (0,)), ((), ()))


def mm(a, b):
    return jnp.dot(a, b, preferred_element_type=F32)


def mm_nt(a, b):
    return lax.dot_general(a, b, NT, preferred_element_type=F32)


def mm_tn(a, b):
    return lax.dot_general(a, b, TN, preferred_element_type=F32)


def halves(table):
    high = table.astype(BF)
    low = (table - high.astype(F32)).astype(BF)
    return high, low


def reduce_phase(line, side, strands, factor, r, meet, steps):
    (grads, result, near, pair) = (r.grads, r.result, r.swapped, r.pair)
    (plane_land, plane_sum, line_land) = (r.plane_land, r.plane_sum, r.line_land)
    (pair_send, pair_recv, plane_send, plane_recv, line_send, line_recv) = r.out_sems
    (line_back_send, line_back_recv, plane_back_send, plane_back_recv) = r.back_sems[:4]
    hop_send, hop_recv = r.back_sems[4:]
    me = lax.axis_index("node")
    core = lax.rem(me, 2)
    chip = me // 2
    partner = me + 1 - 2 * core
    plane = side * side
    spot, far = lax.rem(chip, plane), chip // plane
    half = grads.shape[0] // 2
    rows = half // strands
    rows_p = rows // plane
    rows_z = rows_p // line
    mesh_id = pl.DeviceIdType.MESH

    def across(place, step, count):
        if count & (count - 1):
            return lax.rem(place + step, count)
        bit = 1
        out = place
        while bit <= step:
            if step & bit:
                out += bit - 2 * bit * lax.rem(place // bit, 2)
            bit *= 2
        return out

    spots = [across(spot, step, plane) for step in range(plane - 1, 0, -1)]
    fars = [across(far, step, line) for step in range(line - 1, 0, -1)]

    def spot_device(place):
        return me + (place - spot) * 2

    def far_device(place):
        return me + (place - far) * (2 * plane)

    everyone = (
        [partner]
        + [spot_device(place) for place in spots]
        + [far_device(place) for place in fars]
    )
    if meet:
        barrier = pltpu.get_barrier_semaphore()
        for device in everyone:
            pl.semaphore_signal(barrier, inc=1, device_id=(device,), device_id_type=mesh_id)
        pl.semaphore_wait(barrier, len(everyone))

    def span(start, size):
        return pl.ds(pl.multiple_of(start, 16), size)

    def remote(src, dst, send, recv, device):
        return pltpu.make_async_remote_copy(
            src_ref=src,
            dst_ref=dst,
            send_sem=send,
            recv_sem=recv,
            device_id=(device,),
            device_id_type=mesh_id,
        )

    def swap(s):
        return remote(
            grads.at[span((1 - core) * half + s * rows, rows)],
            near.at[span(s * rows, rows)],
            pair_send.at[s],
            pair_recv.at[s],
            partner,
        )

    def to_plane(s, place, source):
        return remote(
            pair.at[span(s * rows + place * rows_p, rows_p)],
            plane_land.at[span(s * rows + source * rows_p, rows_p)],
            plane_send.at[s, place],
            plane_recv.at[s, source],
            spot_device(place),
        )

    def to_far(s, place, source):
        return remote(
            plane_sum.at[span(s * rows_p + place * rows_z, rows_z)],
            line_land.at[span(s * rows_p + source * rows_z, rows_z)],
            line_send.at[s, place],
            line_recv.at[s, source],
            far_device(place),
        )

    def place_of(which, s, q, f=0):
        return which * half + s * rows + q * rows_p + f * rows_z

    def spread(at, send, recv, device):
        return remote(result.at[at], result.at[at], send, recv, device)

    def back_far(s, place, source):
        at = span(place_of(core, s, spot, source), rows_z)
        return spread(at, line_back_send.at[s, place], line_back_recv.at[s, source], far_device(place))

    def back_plane(s, place, source):
        at = span(place_of(core, s, source), rows_p)
        return spread(
            at, plane_back_send.at[s, place], plane_back_recv.at[s, source], spot_device(place)
        )

    def hop(s, which):
        at = span(place_of(which, s, 0), rows)
        return spread(at, hop_send.at[s], hop_recv.at[s], partner)

    started = []

    def start(made):
        made.start()
        started.append(made)

    def stage_pair(s):
        swap(s).wait_recv()
        at = span(s * rows, rows)
        own = grads[span(core * half + s * rows, rows), :]
        pair[at, :] = (own.astype(F32) + near[at, :].astype(F32)).astype(BF)
        for place in spots:
            start(to_plane(s, place, spot))

    def stage_plane(s):
        total = pair[span(s * rows + spot * rows_p, rows_p), :].astype(F32)
        for place in spots:
            to_plane(s, place, place).wait_recv()
            total += plane_land[span(s * rows + place * rows_p, rows_p), :].astype(F32)
        plane_sum[span(s * rows_p, rows_p), :] = total.astype(BF)
        for place in fars:
            start(to_far(s, place, far))

    def stage_line(s):
        total = plane_sum[span(s * rows_p + far * rows_z, rows_z), :].astype(F32)
        for place in fars:
            to_far(s, place, place).wait_recv()
            total += line_land[span(s * rows_p + place * rows_z, rows_z), :].astype(F32)
        result[span(place_of(core, s, spot, far), rows_z), :] = (total * factor).astype(BF)
        for place in fars:
            start(back_far(s, place, far))

    def stage_back_line(s):
        for place in fars:
            back_far(s, place, place).wait_recv()
        for place in spots:
            start(back_plane(s, place, spot))

    def stage_back_plane(s):
        for place in spots:
            back_plane(s, place, place).wait_recv()
        start(hop(s, core))

    early = strands // 2
    steps[0]()
    for s in range(early):
        start(swap(s))
    steps[1]()
    for s in range(early):
        stage_pair(s)
    steps[2]()
    for s in range(early, strands):
        start(swap(s))
    steps[3]()
    for s in range(early, strands):
        stage_pair(s)
    stages = [stage_plane, stage_line, stage_back_line, stage_back_plane]
    for step in range(strands + len(stages) - 1):
        for number, stage in enumerate(stages):
            if 0 <= step - number < strands:
                stage(step - number)
    leaving = []
    for s in range(strands):
        hop(s, 1 - core).wait_recv()
        for which in range(2):
            at = pl.ds(which * half + s * rows, rows)
            leaving.append(
                pltpu.make_async_copy(result.at[at], r.result_out.at[at], r.result_sems.at[s, which])
            )
            leaving[-1].start()
    for made in started:
        made.wait_send()
    for copy in leaving:
        copy.wait()


def gather_blocks(
    line,
    side,
    subs,
    own,
    whole,
    recv,
    hop_recv,
    line_send,
    first_send,
    second_send,
    hop_send,
    own_sem,
    prepare,
    idle,
    arrived,
):
    me = lax.axis_index("node")
    core = lax.rem(me, 2)
    chip = me // 2
    partner = me + 1 - 2 * core
    low, mid, far = lax.rem(chip, side), lax.rem(chip // side, side), chip // (side * side)
    first = (1 - core) * low + core * mid
    second = (1 - core) * mid + core * low
    first_stride = 1 + core * (side - 1)
    second_stride = side - core * (side - 1)
    plane = side * side
    rows = own.shape[0]
    size = rows // subs
    mesh_id = pl.DeviceIdType.MESH

    def chip_of(place, over, across):
        return (
            place * plane
            + lax.rem(first + over, side) * first_stride
            + lax.rem(second + across, side) * second_stride
        )

    first_peers = [2 * chip_of(far, step, 0) + core for step in range(1, side)]
    second_peers = [2 * chip_of(far, 0, step) + core for step in range(1, side)]

    def at(source, part, kind):
        return pl.ds(pl.multiple_of((2 * source + kind) * rows + part * size, 16), size)

    def piece(source, part, kind, mine):
        return own.at[pl.ds(part * size, size)] if mine else whole.at[at(source, part, kind)]

    def copy(source, part, mine, send_sem, device):
        return pltpu.make_async_remote_copy(
            src_ref=piece(source, part, core, mine),
            dst_ref=whole.at[at(source, part, core)],
            send_sem=send_sem,
            recv_sem=recv.at[source * subs + part],
            device_id=(device,),
            device_id_type=mesh_id,
        )

    def hop(source, part, mine, kind):
        return pltpu.make_async_remote_copy(
            src_ref=piece(source, part, kind, mine),
            dst_ref=whole.at[at(source, part, kind)],
            send_sem=hop_send.at[source * subs + part],
            recv_sem=hop_recv.at[source * subs + part],
            device_id=(partner,),
            device_id_type=mesh_id,
        )

    def along(place, part, mine, way):
        return copy(
            chip_of(place, 0, 0),
            part,
            mine,
            line_send.at[place * subs + part, way],
            me + (1 - 2 * way) * 2 * plane,
        )

    def over_first(place, part, mine, to):
        return copy(
            chip_of(place, 0, 0), part, mine, first_send.at[place * subs + part, to], first_peers[to]
        )

    def over_second(place, over, part, mine, to):
        return copy(
            chip_of(place, over, 0),
            part,
            mine,
            second_send.at[place * subs + part, over, to],
            second_peers[to],
        )

    def landed(source, part):
        copy(source, part, False, hop_send.at[0], partner).wait_recv()

    def settle(source, part, kind):
        if arrived is not None:
            start = pl.multiple_of((2 * source + kind) * rows + part * size, 16)
            arrived(whole, start, start, size)

    stay = None
    if arrived is None:
        mine_at = pl.ds(pl.multiple_of(me * rows, 16), rows)
        stay = pltpu.make_async_copy(own, whole.at[mine_at], own_sem)

    def arrive(place, part, mine, ways):
        source = chip_of(place, 0, 0)
        if mine:
            prepare(part)
        else:
            landed(source, part)
        for way in ways:
            open_end = far < line - 1 if way == 0 else far > 0

            @pl.when(open_end)
            def _(way=way):
                along(place, part, mine, way).start()

        for to in range(side - 1):
            over_first(place, part, mine, to).start()
        for to in range(side - 1):
            over_second(place, 0, part, mine, to).start()
        hop(source, part, mine, core).start()
        if not mine:
            settle(source, part, core)
        elif arrived is not None:
            arrived(own, part * size, pl.multiple_of(me * rows + part * size, 16), size)
        if mine and part == subs - 1:
            if stay is not None:
                stay.start()
            idle()

    def pass_on(place, part):
        for over in range(1, side):
            source = chip_of(place, over, 0)
            landed(source, part)
            for to in range(side - 1):
                over_second(place, over, part, False, to).start()
            hop(source, part, False, core).start()
            settle(source, part, core)

    def finish(place, part):
        for across in range(1, side):
            for over in range(side):
                source = chip_of(place, over, across)
                landed(source, part)
                hop(source, part, False, core).start()
                settle(source, part, core)

    def receive_hops(place, part):
        for over in range(side):
            for across in range(side):
                source = chip_of(place, over, across)
                hop(source, part, False, 1 - core).wait_recv()
                settle(source, part, 1 - core)

    units = [(0, 0)] + [(reach, way) for reach in range(1, line) for way in range(2)]
    work = [(reach, way, part) for reach, way in units for part in range(subs)]

    def run(item, stage):
        reach, way, part = item
        place = far - reach if way == 0 else far + reach

        def body():
            if stage == 0:
                arrive(place, part, reach == 0, (0, 1) if reach == 0 else (way,))
            elif stage == 1:
                pass_on(place, part)
            elif stage == 2:
                finish(place, part)
            else:
                receive_hops(place, part)

        if reach == 0:
            body()
        else:
            pl.when(place >= 0 if way == 0 else place < line)(body)

    lags = (0, 4, 8, 10)
    for step in range(len(work) + lags[-1]):
        for stage, lag in enumerate(lags):
            if 0 <= step - lag < len(work):
                run(work[step - lag], stage)
    if stay is not None:
        stay.wait()

    def drain(place, carry):
        for part in range(subs):
            for to in range(side - 1):
                over_first(place, part, False, to).wait_send()
                for over in range(side):
                    over_second(place, over, part, False, to).wait_send()

            @pl.when((place <= far) & (far < line - 1))
            def _(part=part):
                along(place, part, False, 0).wait_send()

            @pl.when((place >= far) & (far > 0))
            def _(part=part):
                along(place, part, False, 1).wait_send()

            for over in range(side):
                for across in range(side):
                    hop(chip_of(place, over, across), part, False, core).wait_send()
        return carry

    lax.fori_loop(0, line, drain, 0)


def front_phase(devices, slots, line, side, subs, r, idle, late_idle, arrived):
    me = lax.axis_index("node")
    (node, bucket, feats, memory) = (r.node, r.bucket, r.feats, r.memory)
    (outgoing, inbox, sel, meta, hidden) = (r.outgoing, r.inbox, r.sel, r.meta, r.hidden)
    (picked, picked_meta, totals, counts) = (r.picked, r.picked_meta, r.totals, r.counts)
    (send_sems, recv_sems) = (r.send_sems, r.recv_sems)
    events = feats.shape[0]
    rows, columns = memory.shape
    stride = columns // LANES
    batch = 4
    mesh_id = pl.DeviceIdType.MESH
    barrier = pltpu.get_barrier_semaphore()

    def greet(step, carry):
        pl.semaphore_signal(
            barrier, inc=1, device_id=(lax.rem(me + step, devices),), device_id_type=mesh_id
        )
        return carry

    lax.fori_loop(1, devices, greet, 0)

    ids = lax.broadcasted_iota(jnp.int32, (devices, events), 0) * rows
    names = node[...]
    theirs = (names >= ids) & (names < ids + rows)
    before = lax.broadcasted_iota(jnp.int32, (events, events), 0) < lax.broadcasted_iota(
        jnp.int32, (events, events), 1
    )
    rank = mm(theirs.astype(F32).astype(BF), before.astype(F32).astype(BF))
    sel[...] = jnp.where(theirs, rank, -1.0)
    within = jnp.sum(jnp.where(theirs, names - ids, 0).astype(F32), axis=0, keepdims=True)
    kind = lax.broadcasted_iota(jnp.int32, (16, events), 0)
    meta[...] = jnp.where(
        kind == 0,
        within,
        jnp.where(kind == 1, bucket[...].astype(F32), jnp.where(kind == 2, 1.0, 0.0)),
    ).astype(BF)
    slot_ids = lax.broadcasted_iota(jnp.int32, (slots, events), 0).astype(F32)
    lane_ids = lax.broadcasted_iota(jnp.int32, (LANES, events), 0).astype(F32)
    pl.semaphore_wait(barrier, devices - 1)

    def send(peer):
        return pltpu.make_async_remote_copy(
            src_ref=outgoing.at[peer],
            dst_ref=inbox.at[me],
            send_sem=send_sems.at[peer],
            recv_sem=recv_sems.at[me],
            device_id=(peer,),
            device_id_type=mesh_id,
        )

    def receive(peer):
        return pltpu.make_async_remote_copy(
            src_ref=outgoing.at[peer],
            dst_ref=inbox.at[peer],
            send_sem=send_sems.at[peer],
            recv_sem=recv_sems.at[peer],
            device_id=(peer,),
            device_id_type=mesh_id,
        )

    def pack_batch(step, own):
        peers = [lax.rem(me + step * batch + part, devices) for part in range(batch)]
        picks = [sel[pl.ds(peer, 1), :] for peer in peers]
        hits = jnp.concatenate([(slot_ids == row).astype(F32) for row in picks], axis=0)
        turned = jnp.concatenate([(lane_ids == row).astype(F32) for row in picks], axis=0)
        rows_of = mm(hits.astype(BF), feats[...]).astype(BF)
        info = mm_nt(meta[...], turned.astype(BF)).astype(BF)
        for part, peer in enumerate(peers):
            lines = slice(part * slots, (part + 1) * slots)
            lanes = slice(part * LANES, (part + 1) * LANES)
            if own and part == 0:
                inbox[me, :slots, :] = rows_of[lines, :]
                inbox[me, slots:, :] = info[:, lanes]
            else:
                outgoing[peer, :slots, :] = rows_of[lines, :]
                outgoing[peer, slots:, :] = info[:, lanes]
                send(peer).start()

    pack_batch(0, True)

    def pack_rest(step, carry):
        pack_batch(step, False)
        return carry

    lax.fori_loop(1, devices // batch, pack_rest, 0)

    r.need("hidden_weight")
    previous = memory[...]
    for part in range(3):
        cut = slice(part * columns, (part + 1) * columns)
        hidden[:, cut] = mm(previous, r.hidden_weight[:, cut])
    idle()
    totals[...] = jnp.zeros_like(totals)
    counts[...] = jnp.zeros_like(counts)
    high, low = halves(r.time_message[...])
    weight = r.edge_weight[...]
    turn = (
        lax.broadcasted_iota(jnp.int32, (slots, LANES), 0)
        == lax.broadcasted_iota(jnp.int32, (slots, LANES), 1)
    ).astype(F32).astype(BF)
    chunk = batch * slots

    def add_batch(step, own):
        for part in range(batch):
            peer = lax.rem(me + devices - step * batch - part, devices)
            if not (own and part == 0):
                receive(peer).wait_recv()
            at = slice(part * slots, (part + 1) * slots)
            picked[at, :] = inbox[peer, :slots, :]
            picked_meta[at, :] = mm_nt(turn, inbox[peer, slots:, :])
        info = picked_meta[...]
        place, when, valid = info[:, 0:1], info[:, 1:2], info[:, 2:3]
        lanes = lax.broadcasted_iota(jnp.int32, (chunk, high.shape[0]), 1).astype(F32)
        picks = (lanes == when).astype(F32).astype(BF)
        pre = mm(picked[...], weight) + mm(picks, high) + mm(picks, low)
        message = (pre / (1.0 + jnp.exp(-pre))).astype(BF)
        node_ids = lax.broadcasted_iota(jnp.int32, (chunk, rows), 1).astype(F32)
        marks = jnp.where(node_ids == place, valid, 0.0).astype(BF)
        totals[...] += mm_tn(marks, message)
        counts[...] += mm_tn(marks, jnp.ones((chunk, LANES), BF))

    add_batch(0, True)

    def add_rest(step, carry):
        add_batch(step, False)
        return carry

    lax.fori_loop(1, devices // batch, add_rest, 0)

    r.need("input_weight")

    def prepare(part):
        size = rows // subs
        at = slice(part * size, (part + 1) * size)
        count = counts[at, 0:1]
        aggregate = (totals[at, :] / jnp.maximum(count, 1.0)).astype(BF)

        def gate(which):
            cut = slice(which * columns, (which + 1) * columns)
            bias = jnp.concatenate(
                [r.gate_bias[which * stride + p : which * stride + p + 1, :] for p in range(stride)],
                axis=1,
            )
            return mm(aggregate, r.input_weight[:, cut]) + bias, hidden[at, cut]

        from_input, from_hidden = gate(0)
        update = jax.nn.sigmoid(from_input + from_hidden)
        from_input, from_hidden = gate(1)
        resets = jax.nn.sigmoid(from_input + from_hidden)
        from_input, from_hidden = gate(2)
        candidate = jnp.tanh(from_input + resets * from_hidden)
        old = memory[at, :].astype(F32)
        fresh = (1.0 - update) * candidate + update * old
        fresh = jnp.where(count > 0, fresh, old)
        r.out_memory[at, :] = fresh.astype(BF)
        first = part * size * stride
        for p in range(stride):
            r.wide[pl.ds(first + p, size, stride=stride), :] = fresh[:, p * LANES : (p + 1) * LANES]
        at = slice(first, first + size * stride)
        r.own_table[at, :] = r.wide[at, :].astype(BF)
        if part == subs - 1:
            r.leave("out_memory")

    gather_blocks(
        line,
        side,
        subs,
        r.own_table,
        r.whole,
        r.gather_recv,
        r.gather_hop_recv,
        r.gather_line_send,
        r.gather_first_send,
        r.gather_second_send,
        r.gather_hop_send,
        r.gather_own,
        prepare,
        late_idle,
        arrived,
    )

    def drain(step, carry):
        send(lax.rem(me + step, devices)).wait_send()
        return carry

    lax.fori_loop(1, devices, drain, 0)


def keep(blocks, tall, dest, kind, values):
    upper, lower = halves(values)
    for b in range(blocks):
        rows = slice(b * GROUP, (b + 1) * GROUP)
        first = b * tall + kind * GROUP
        dest[first : first + GROUP, :] = upper[rows, :]
        first += 2 * HEADS * GROUP
        dest[first : first + GROUP, :] = lower[rows, :]


def head_cuts(columns):
    head = columns // HEADS
    return [slice(h * head, (h + 1) * head) for h in range(HEADS)]


def early_products(r):
    events, columns = r.back.shape
    blocks = events // GROUP
    tall = 4 * HEADS * GROUP
    r.need("upstream")
    r.need("out_weight")
    r.need("value_weight")
    r.back[...] = mm_nt(r.upstream[...], r.out_weight[...]).astype(BF)
    for h, cut in enumerate(head_cuts(columns)):
        keep(blocks, tall, r.pull, HEADS + h, mm_nt(r.back[:, cut], r.value_weight[:, cut]))
        keep(blocks, tall, r.pull_time, HEADS + h, jnp.zeros((events, LANES), F32))


def early_marks(r):
    fanout, events = r.buckets.shape
    blocks = events // GROUP
    wide = fanout * GROUP
    even = (
        lax.broadcasted_iota(jnp.int32, (fanout, LANES), 0)
        == lax.broadcasted_iota(jnp.int32, (fanout, LANES), 1)
    ).astype(F32).astype(BF)
    r.names[...] = mm_tn(r.buckets[...].astype(F32).astype(BF), even)
    r.logits[...] = jnp.zeros_like(r.logits)
    r.logits[:fanout, :] = r.affinity[...]
    lane_names = lax.broadcasted_iota(jnp.int32, (GROUP, LANES), 1).astype(F32)

    def mark(b, carry):
        mine = r.names[pl.ds(pl.multiple_of(b * GROUP, GROUP), GROUP), :]
        for j in range(fanout):
            at = pl.ds(pl.multiple_of(b * wide + j * GROUP, GROUP), GROUP)
            r.hot[at, :] = (lane_names == mine[:, j : j + 1]).astype(F32).astype(BF)
        return carry

    lax.fori_loop(0, blocks, mark, 0)


def event_phase(r, fetch_targets, fetch_block):
    events, columns = r.back.shape
    fanout = r.buckets.shape[0]
    head = columns // HEADS
    stride = columns // LANES
    kinds = 2 * HEADS
    blocks = events // GROUP
    wide = fanout * GROUP
    tall = 2 * kinds * GROUP
    rows_all = fanout * events
    heads = head_cuts(columns)
    (target, query, pull, pull_time) = (r.target, r.query, r.pull, r.pull_time)
    (mix, hits, scores, close, hot, logits) = (r.mix, r.hits, r.scores, r.close, r.hot, r.logits)
    high, low = halves(r.time_key[...])
    lane = lax.broadcasted_iota(jnp.int32, (GROUP, LANES), 1)

    fetch_targets()
    fetch_block(0, r.near[0])
    for part in range(stride):
        target[:, part * LANES : (part + 1) * LANES] = r.own_near[
            pl.ds(part, events, stride=stride), :
        ].astype(BF)
    r.need("query_weight")
    r.need("key_weight")
    query[...] = mm(target[...], r.query_weight[...]).astype(BF)
    for h, cut in enumerate(heads):
        keep(blocks, tall, pull, h, mm_nt(query[:, cut], r.key_weight[:, cut]))
        keep(
            blocks,
            tall,
            pull_time,
            h,
            mm_nt(query[:, cut], high[:, cut]) + mm_nt(query[:, cut], low[:, cut]),
        )

    scale = 1.0 / math.sqrt(head)
    pad = scores.shape[0] // blocks
    own = lax.rem(lane, GROUP) == lax.broadcasted_iota(jnp.int32, (GROUP, LANES), 0)
    row_ids = lax.broadcasted_iota(jnp.int32, (pad, LANES), 0)
    lane_ids = lax.broadcasted_iota(jnp.int32, (pad, LANES), 1)
    forward = lane_ids < HEADS * GROUP
    per_row = LANES // GROUP

    def close_rows(b):
        return jnp.concatenate(
            [
                close[pl.ds(pl.multiple_of(part * rows_all + b * wide, GROUP), wide), :]
                for part in range(stride)
            ],
            axis=1,
        )

    def score(b, near):
        for part in range(stride):
            at = pl.ds(pl.multiple_of(part * rows_all + b * wide, GROUP), wide)
            close[at, :] = near[pl.ds(part, wide, stride=stride), :].astype(BF)
        at = pl.ds(pl.multiple_of(b * wide, GROUP), wide)
        from_at = pl.ds(pl.multiple_of(b * tall, GROUP), tall)
        both = mm_nt(close_rows(b), pull[from_at, :]) + mm_nt(hot[at, :], pull_time[from_at, :])
        both = both[:, :LANES] + both[:, LANES:]
        raw = jnp.zeros((pad, LANES), F32)
        for j in range(fanout):
            line = jnp.where(own, both[j * GROUP : (j + 1) * GROUP, :], 0.0)
            raw = jnp.where(row_ids == j, jnp.sum(line, axis=0, keepdims=True), raw)
        chunk = pl.multiple_of(b // per_row * LANES, LANES)
        piece = logits[:, pl.ds(chunk, LANES)]
        piece = pltpu.roll(piece, lax.rem(LANES - lax.rem(b, per_row) * GROUP, LANES), axis=1)
        given = piece
        for h in range(1, HEADS):
            moved = pltpu.roll(piece, h * GROUP, axis=1)
            given = jnp.where(lane_ids >= h * GROUP, moved, given)
        scores[pl.ds(pl.multiple_of(b * pad, pad), pad), :] = jnp.where(
            forward, raw * scale + given, raw
        )

    def score_four(b, more):
        for place in range(4):
            if more or place < 3:
                fetch_block(b + place + 1, r.near[(place + 1) % 2])
            score(b + place, r.near[place % 2])

    def score_step(step, carry):
        score_four(step * 4, True)
        return carry

    lax.fori_loop(0, blocks // 4 - 1, score_step, 0)
    score_four(blocks - 4, False)

    for b in range(blocks):
        at = slice(b * pad, (b + 1) * pad)
        here = scores[at, :]
        active = row_ids < fanout
        top = jnp.max(jnp.where(active, here, -3.0e38), axis=0, keepdims=True)
        raised = jnp.where(active, jnp.exp(jnp.where(active, here - top, 0.0)), 0.0)
        probs = raised / jnp.sum(raised, axis=0, keepdims=True)
        slopes = pltpu.roll(here, HEADS * GROUP, axis=1).astype(BF).astype(F32)
        inner = jnp.sum(probs * slopes, axis=0, keepdims=True)
        slopes = probs * (slopes - inner) * scale
        scores[at, :] = jnp.where(forward, probs, pltpu.roll(slopes, HEADS * GROUP, axis=1))

    def blend(b):
        weights = scores[pl.ds(pl.multiple_of(b * pad, pad), pad), :]
        spread = jnp.concatenate(
            [
                jnp.where(own, jnp.broadcast_to(weights[j : j + 1, :], (GROUP, LANES)), 0.0)
                for j in range(fanout)
            ],
            axis=0,
        ).astype(BF)
        at = pl.ds(pl.multiple_of(b * wide, GROUP), wide)
        mixed = mm_tn(spread, close_rows(b)).astype(BF)
        times = mm_tn(spread, hot[at, :]).astype(BF)
        to = pl.ds(pl.multiple_of(b * GROUP, GROUP), GROUP)
        for k in range(kinds):
            mix[k, to, :] = mixed[k * GROUP : (k + 1) * GROUP, :]
        for h in range(HEADS):
            hits[h, to, :] = times[(HEADS + h) * GROUP : (HEADS + h + 1) * GROUP, :]

    def blend_four(step, carry):
        for place in range(4):
            blend(step * 4 + place)
        return carry

    lax.fori_loop(0, blocks // 4, blend_four, 0)


def gradient_steps(r):
    (target, query, back, mix, hits, grads) = (r.target, r.query, r.back, r.mix, r.hits, r.grads)
    events, columns = back.shape
    heads = head_cuts(columns)
    high, low = halves(r.time_key[...])

    def value_and_key():
        for h, cut in enumerate(heads):
            grads[2 * columns : 3 * columns, cut] = mm_tn(mix[h], back[:, cut]).astype(BF)
            grads[:columns, cut] = mm_tn(mix[HEADS + h], query[:, cut]).astype(BF)

    def cotangents():
        for h, cut in enumerate(heads):
            back[:, cut] = mm(mix[h], r.value_weight[:, cut]).astype(BF)
            query[:, cut] = (
                mm(mix[HEADS + h], r.key_weight[:, cut])
                + mm(hits[h], high[:, cut])
                + mm(hits[h], low[:, cut])
            ).astype(BF)

    def query_and_out():
        grads[columns : 2 * columns, :] = mm_tn(target[...], query[...]).astype(BF)
        grads[3 * columns :, :] = mm_tn(back[...], r.upstream[...]).astype(BF)

    def embed():
        r.embedding[...] = (mm(back[...], r.out_weight[...]) + target[...].astype(F32)).astype(BF)
        r.leave("embedding")

    return value_and_key, cotangents, query_and_out, embed


class Refs:
    def __init__(self, names, refs, staged):
        for name, ref in zip(names, refs, strict=True):
            setattr(self, name, ref)
        self.copies = {}
        self.leaving = []
        for place, name in enumerate(staged):
            copy = pltpu.make_async_copy(
                getattr(self, name), getattr(self, name + "_here"), self.stage_sems.at[place]
            )
            copy.start()
            self.copies[name] = copy
            setattr(self, name, getattr(self, name + "_here"))
        if hasattr(self, "near_first"):
            self.near = (self.near_first, self.near_second)
        if hasattr(self, "grads"):
            self.out_sems = [getattr(self, name) for name in OUT_SEMS]
            self.back_sems = [getattr(self, name) for name in BACK_SEMS]

    def leave(self, name):
        copy = pltpu.make_async_copy(
            getattr(self, name), getattr(self, name + "_out"), getattr(self, name + "_sem")
        )
        copy.start()
        self.leaving.append(copy)

    def finish(self):
        for copy in self.leaving:
            copy.wait()

    def need(self, name):
        copy = self.copies.pop(name, None)
        if copy is not None:
            copy.wait()


OUT_SEMS = [f"out{place}" for place in range(6)]
BACK_SEMS = [f"back{place}" for place in range(6)]
FRONT_STAGED = ("hidden_weight", "input_weight")
EVENT_STAGED = ("upstream", "out_weight", "value_weight", "query_weight", "key_weight")


def front_kernel(sizes, names, *refs):
    r = Refs(names, refs, FRONT_STAGED)
    front_phase(*sizes, r, lambda: None, lambda: None, None)
    r.finish()


def fetch_kernel(ids, own_ids, source, dest, sem):
    fanout, events = ids.shape
    stride = dest.shape[0] // ((fanout + 1) * events)
    wide = fanout * GROUP

    def request(start, row):
        pltpu.make_async_copy(
            source.at[pl.ds(pl.multiple_of(start * stride, stride), stride)],
            dest.at[pl.ds(pl.multiple_of(row * stride, stride), stride)],
            sem,
        ).start()

    def request_all(e, carry):
        for j in range(fanout):
            request(ids[j, e], e // GROUP * wide + j * GROUP + e % GROUP)
        request(own_ids[e], fanout * events + e)
        return carry

    lax.fori_loop(0, events, request_all, 0)
    pltpu.make_async_copy(source.at[pl.ds(0, dest.shape[0])], dest, sem).wait()


def event_kernel(reduce_sizes, names, *refs):
    r = Refs(names, refs, EVENT_STAGED)
    fanout, events = r.buckets.shape
    block_rows = r.near_first.shape[0]
    early_products(r)
    early_marks(r)

    def fetch_targets():
        copy = pltpu.make_async_copy(
            r.rows.at[pl.ds(events // GROUP * block_rows, r.own_near.shape[0])],
            r.own_near,
            r.fetch_sem,
        )
        copy.start()
        copy.wait()

    def fetch_block(b, near):
        first = pl.multiple_of(b * block_rows, block_rows)
        copy = pltpu.make_async_copy(r.rows.at[pl.ds(first, block_rows)], near, r.fetch_sem)
        copy.start()
        copy.wait()

    event_phase(r, fetch_targets, fetch_block)
    reduce_phase(*reduce_sizes, r, True, gradient_steps(r))
    r.finish()


def whole_kernel(front_sizes, reduce_sizes, names, *refs):
    r = Refs(names, refs, FRONT_STAGED + EVENT_STAGED)
    fanout, events = r.buckets.shape
    stride = r.own_near.shape[0] // events
    table = r.table
    r.close = r.whole

    def arrived(source, first, start, size):
        step_rows = 128

        def widen(step, carry):
            from_at = pl.ds(pl.multiple_of(first + step * step_rows, 16), step_rows)
            to_at = pl.ds((start + step * step_rows) // stride, step_rows // stride)
            rows = source[from_at, :].astype(F32)
            table[to_at] = rows.reshape(step_rows // stride, stride, LANES)
            return carry

        lax.fori_loop(0, size // step_rows, widen, 0)

    front_phase(*front_sizes, r, lambda: early_products(r), lambda: early_marks(r), arrived)

    def move(start, dest, row):
        dest[pl.ds(pl.multiple_of(row * stride, stride), stride), :] = table[start]

    def fetch_targets():
        unroll = 16

        def some(step, carry):
            for place in range(unroll):
                e = step * unroll + place
                move(r.own_ids[e], r.own_near, e)
            return carry

        lax.fori_loop(0, events // unroll, some, 0)

    def fetch_block(b, near):
        for e in range(GROUP):
            for j in range(fanout):
                move(r.ids[j, b * GROUP + e], near, j * GROUP + e)

    event_phase(r, fetch_targets, fetch_block)
    reduce_phase(*reduce_sizes, r, False, gradient_steps(r))
    r.finish()


def finish_kernel(order, total, embedding, memory, *rest):
    outs, (here, wide, *passing, read_sems, write_sems, in_sems, out_sems) = rest[:6], rest[6:]
    grads, kept = outs[:4], outs[4:]
    columns = grads[0].shape[0]
    per = read_sems.shape[0] // 4
    size = columns // per
    reads, writes, enter = [], [], []
    for place in range(4 * per):
        at = pl.ds(place * size, size)
        reads.append(pltpu.make_async_copy(total.at[at], here.at[at], read_sems.at[place]))
        reads[-1].start()
    for place, source in enumerate((embedding, memory)):
        enter.append(pltpu.make_async_copy(source, passing[place], in_sems.at[place]))
        enter[-1].start()
    for place in range(4 * per):
        at = pl.ds(place * size, size)
        reads[place].wait()
        wide[at, :] = here[at, :].astype(F32)
        to = grads[order[place // per]].at[pl.ds(place % per * size, size)]
        writes.append(pltpu.make_async_copy(wide.at[at], to, write_sems.at[place]))
        writes[-1].start()
    for place in range(2):
        enter[place].wait()
        writes.append(pltpu.make_async_copy(passing[place], kept[place], out_sems.at[place]))
        writes[-1].start()
    for copy in writes:
        copy.wait()


def shards(
    event_node,
    neighbours,
    event_bucket,
    neighbour_bucket,
    edge_features,
    affinity,
    upstream,
    node_memory,
    edge_weight,
    time_message,
    input_weight,
    hidden_weight,
    gate_bias,
    time_key,
    query_weight,
    key_weight,
    value_weight,
    out_weight,
):
    devices = lax.axis_size("node")
    node_rows, columns = node_memory.shape
    events, fanout = neighbours.shape
    features = edge_features.shape[1]
    stride = columns // LANES
    slots = -(-(3 * events // devices) // 16) * 16
    chips = devices // 2
    side = max(s for s in range(1, chips + 1) if chips % (s * s) == 0 and s**3 <= chips)
    line = chips // (side * side)
    subs = 2
    half = 2 * columns
    strands = max(1, min(4, half // (16 * chips)))
    factor = 1.0 / math.sqrt(events * devices)
    front_sizes = (devices, slots, line, side, subs)
    reduce_sizes = (line, side, strands, factor)
    table_rows = devices * node_rows * stride
    close_rows = fanout * events * stride
    resident = table_rows * LANES * 4 <= RESIDENT_LIMIT
    vmem = pl.BlockSpec(memory_space=pltpu.VMEM)
    smem = pl.BlockSpec(memory_space=pltpu.SMEM)
    hbm = pl.BlockSpec(memory_space=pl.ANY)
    dma = pltpu.SemaphoreType.DMA

    def buffer(rows, width, dtype=BF):
        return pltpu.VMEM((rows, width), dtype)

    front_in = {
        "node": (event_node.reshape(1, events), vmem),
        "bucket": (event_bucket.reshape(1, events), vmem),
        "feats": (edge_features, vmem),
        "memory": (node_memory, vmem),
        "edge_weight": (edge_weight, vmem),
        "time_message": (time_message, vmem),
        "input_weight": (input_weight, hbm),
        "hidden_weight": (hidden_weight, hbm),
        "gate_bias": (gate_bias.reshape(-1, LANES), vmem),
    }
    event_in = {
        "buckets": (neighbour_bucket.T, vmem),
        "affinity": (affinity.T, vmem),
        "upstream": (upstream, hbm),
        "time_key": (time_key, vmem),
        "query_weight": (query_weight, hbm),
        "key_weight": (key_weight, hbm),
        "value_weight": (value_weight, hbm),
        "out_weight": (out_weight, hbm),
    }
    index_in = {"ids": (neighbours.T, smem), "own_ids": (event_node, smem)}
    memory_out = {"out_memory_out": (jax.ShapeDtypeStruct((node_rows, columns), BF), hbm)}
    event_out = {
        "embedding_out": (jax.ShapeDtypeStruct((events, columns), BF), hbm),
        "result_out": (jax.ShapeDtypeStruct((2 * half, columns), BF), hbm),
    }
    front_scratch = {
        "outgoing": pltpu.VMEM((devices, slots + 16, features), BF),
        "inbox": pltpu.VMEM((devices, slots + 16, features), BF),
        "sel": buffer(devices, events, F32),
        "meta": buffer(16, events),
        "hidden": buffer(node_rows, 3 * columns, F32),
        "picked": buffer(4 * slots, features),
        "picked_meta": buffer(4 * slots, 16, F32),
        "totals": buffer(node_rows, columns, F32),
        "counts": buffer(node_rows, LANES, F32),
        "wide": buffer(node_rows * stride, LANES, F32),
        "own_table": buffer(node_rows * stride, LANES),
        "send_sems": dma((devices,)),
        "recv_sems": dma((devices,)),
        "gather_recv": dma((chips * subs,)),
        "gather_hop_recv": dma((chips * subs,)),
        "gather_line_send": dma((line * subs, 2)),
        "gather_first_send": dma((line * subs, side - 1)),
        "gather_second_send": dma((line * subs, side, side - 1)),
        "gather_hop_send": dma((chips * subs,)),
        "gather_own": dma,
        "out_memory": buffer(node_rows, columns),
        "out_memory_sem": dma,
    }
    event_scratch = {
        "target": buffer(events, columns),
        "query": buffer(events, columns),
        "back": buffer(events, columns),
        "pull": buffer(4 * HEADS * events, columns),
        "pull_time": buffer(4 * HEADS * events, LANES),
        "mix": pltpu.VMEM((2 * HEADS, events, columns), BF),
        "hits": pltpu.VMEM((HEADS, events, LANES), BF),
        "scores": buffer(events // GROUP * 16, LANES, F32),
        "hot": buffer(fanout * events, LANES),
        "names": buffer(events, LANES, F32),
        "logits": buffer(16, events, F32),
        "own_near": buffer(events * stride, LANES, F32),
        "near_first": buffer(fanout * GROUP * stride, LANES, F32),
        "near_second": buffer(fanout * GROUP * stride, LANES, F32),
        "grads": buffer(2 * half, columns),
        "swapped": buffer(half, columns),
        "pair": buffer(half, columns),
        "plane_land": buffer(half, columns),
        "plane_sum": buffer(half // (side * side), columns),
        "line_land": buffer(half // (side * side), columns),
        "embedding": buffer(events, columns),
        "embedding_sem": dma,
        "result": buffer(2 * half, columns),
        "result_sems": dma((strands, 2)),
    }
    plane = side * side
    for name, shape in zip(
        OUT_SEMS + BACK_SEMS,
        [(strands,)] * 2
        + [(strands, plane)] * 2
        + [(strands, line)] * 4
        + [(strands, plane)] * 2
        + [(strands,)] * 2,
    ):
        event_scratch[name] = dma(shape)

    def call(kernel, sizes, name, number, inputs, outputs, scratch, staged):
        scratch = dict(scratch)
        for key in staged:
            array = inputs[key][0]
            scratch[key + "_here"] = pltpu.VMEM(array.shape, array.dtype)
        scratch["stage_sems"] = dma((len(staged),))
        names = list(inputs) + list(outputs) + list(scratch)
        return pl.pallas_call(
            functools.partial(kernel, *sizes, names),
            out_shape=tuple(shape for shape, _ in outputs.values()),
            in_specs=[spec for _, spec in inputs.values()],
            out_specs=tuple(spec for _, spec in outputs.values()),
            scratch_shapes=list(scratch.values()),
            compiler_params=pltpu.CompilerParams(
                collective_id=number, has_side_effects=True, vmem_limit_bytes=VMEM_LIMIT
            ),
            name=name,
        )(*[array for array, _ in inputs.values()])

    if resident:
        new_memory, embedding, total = call(
            whole_kernel,
            (front_sizes, reduce_sizes),
            "whole_step",
            0,
            front_in | event_in | index_in,
            memory_out | event_out,
            front_scratch
            | event_scratch
            | {
                "whole": buffer(max(table_rows, close_rows), LANES),
                "table": pltpu.VMEM((table_rows // stride, stride, LANES), F32),
            },
            FRONT_STAGED + EVENT_STAGED,
        )
    else:
        new_memory, whole = call(
            front_kernel,
            (front_sizes,),
            "front_step",
            0,
            front_in,
            memory_out | {"whole": (jax.ShapeDtypeStruct((table_rows, LANES), BF), hbm)},
            front_scratch,
            FRONT_STAGED,
        )
        rows = pl.pallas_call(
            fetch_kernel,
            out_shape=jax.ShapeDtypeStruct(((fanout + 1) * events * stride, LANES), F32),
            in_specs=[smem, smem, hbm],
            out_specs=hbm,
            scratch_shapes=[dma],
            name="fetch_step",
        )(neighbours.T, event_node, whole.astype(F32))
        embedding, total = call(
            event_kernel,
            (reduce_sizes,),
            "event_step",
            1,
            event_in | {"rows": (rows, hbm)},
            event_out,
            event_scratch | {"close": buffer(close_rows, LANES), "fetch_sem": dma},
            EVENT_STAGED,
        )
    per = 2
    grad_shape = jax.ShapeDtypeStruct((columns, columns), F32)
    *grads, embedding, new_memory = pl.pallas_call(
        functools.partial(finish_kernel, (1, 0, 2, 3)),
        out_shape=(grad_shape,) * 4
        + (
            jax.ShapeDtypeStruct(embedding.shape, BF),
            jax.ShapeDtypeStruct(new_memory.shape, BF),
        ),
        in_specs=[hbm] * 3,
        out_specs=(hbm,) * 6,
        scratch_shapes=[
            buffer(4 * columns, columns),
            buffer(4 * columns, columns, F32),
            buffer(events, columns),
            buffer(node_rows, columns),
            dma((4 * per,)),
            dma((4 * per,)),
            dma((2,)),
            dma((2,)),
        ],
        compiler_params=pltpu.CompilerParams(vmem_limit_bytes=VMEM_LIMIT),
        name="finish_step",
    )(total, embedding, new_memory)
    return (embedding, new_memory) + tuple(grads)


def solution(mesh):
    placed = (
        P("node"),
        P("node", None),
        P("node"),
        P("node", None),
        P("node", None),
        P("node", None),
        P("node", None),
        P("node", None),
        P(),
        P(),
        P(),
        P(),
        P(),
        P(),
        P(),
        P(),
        P(),
        P(),
    )
    return jax.shard_map(
        shards,
        mesh=mesh,
        in_specs=placed,
        out_specs=(P("node", None), P("node", None), P(), P(), P(), P()),
        check_vma=False,
    )
```

```python
import functools
import math

import jax
import jax.numpy as jnp
from jax import lax
from jax.experimental import pallas as pl
from jax.experimental.pallas import tpu as pltpu
from jax.sharding import PartitionSpec as P

HEADS = 2
LANES = 128
GROUP = 32
BF = jnp.bfloat16
F32 = jnp.float32
VMEM_LIMIT = 60 * 1024 * 1024
RESIDENT_LIMIT = 20 * 1024 * 1024
NT = (((1,), (1,)), ((), ()))
TN = (((0,), (0,)), ((), ()))


def mm(a, b):
    return jnp.dot(a, b, preferred_element_type=F32)


def mm_nt(a, b):
    return lax.dot_general(a, b, NT, preferred_element_type=F32)


def mm_tn(a, b):
    return lax.dot_general(a, b, TN, preferred_element_type=F32)


def halves(table):
    high = table.astype(BF)
    low = (table - high.astype(F32)).astype(BF)
    return high, low


def reduce_phase(line, side, strands, factor, r, meet, steps):
    (grads, result, near, pair) = (r.grads, r.result, r.swapped, r.pair)
    (plane_land, plane_sum, line_land) = (r.plane_land, r.plane_sum, r.line_land)
    (pair_send, pair_recv, plane_send, plane_recv, line_send, line_recv) = r.out_sems
    (line_back_send, line_back_recv, plane_back_send, plane_back_recv) = r.back_sems[:4]
    hop_send, hop_recv = r.back_sems[4:]
    me = lax.axis_index("node")
    core = lax.rem(me, 2)
    chip = me // 2
    partner = me + 1 - 2 * core
    plane = side * side
    spot, far = lax.rem(chip, plane), chip // plane
    half = grads.shape[0] // 2
    rows = half // strands
    rows_p = rows // plane
    rows_z = rows_p // line
    mesh_id = pl.DeviceIdType.MESH

    def across(place, step, count):
        if count & (count - 1):
            return lax.rem(place + step, count)
        bit = 1
        out = place
        while bit <= step:
            if step & bit:
                out += bit - 2 * bit * lax.rem(place // bit, 2)
            bit *= 2
        return out

    spots = [across(spot, step, plane) for step in range(plane - 1, 0, -1)]
    fars = [across(far, step, line) for step in range(line - 1, 0, -1)]

    def spot_device(place):
        return me + (place - spot) * 2

    def far_device(place):
        return me + (place - far) * (2 * plane)

    everyone = (
        [partner]
        + [spot_device(place) for place in spots]
        + [far_device(place) for place in fars]
    )
    if meet:
        barrier = pltpu.get_barrier_semaphore()
        for device in everyone:
            pl.semaphore_signal(barrier, inc=1, device_id=(device,), device_id_type=mesh_id)
        pl.semaphore_wait(barrier, len(everyone))

    def span(start, size):
        return pl.ds(pl.multiple_of(start, 16), size)

    def remote(src, dst, send, recv, device):
        return pltpu.make_async_remote_copy(
            src_ref=src,
            dst_ref=dst,
            send_sem=send,
            recv_sem=recv,
            device_id=(device,),
            device_id_type=mesh_id,
        )

    def swap(s):
        return remote(
            grads.at[span((1 - core) * half + s * rows, rows)],
            near.at[span(s * rows, rows)],
            pair_send.at[s],
            pair_recv.at[s],
            partner,
        )

    def to_plane(s, place, source):
        return remote(
            pair.at[span(s * rows + place * rows_p, rows_p)],
            plane_land.at[span(s * rows + source * rows_p, rows_p)],
            plane_send.at[s, place],
            plane_recv.at[s, source],
            spot_device(place),
        )

    def to_far(s, place, source):
        return remote(
            plane_sum.at[span(s * rows_p + place * rows_z, rows_z)],
            line_land.at[span(s * rows_p + source * rows_z, rows_z)],
            line_send.at[s, place],
            line_recv.at[s, source],
            far_device(place),
        )

    def place_of(which, s, q, f=0):
        return which * half + s * rows + q * rows_p + f * rows_z

    def spread(at, send, recv, device):
        return remote(result.at[at], result.at[at], send, recv, device)

    def back_far(s, place, source):
        at = span(place_of(core, s, spot, source), rows_z)
        return spread(at, line_back_send.at[s, place], line_back_recv.at[s, source], far_device(place))

    def back_plane(s, place, source):
        at = span(place_of(core, s, source), rows_p)
        return spread(
            at, plane_back_send.at[s, place], plane_back_recv.at[s, source], spot_device(place)
        )

    def hop(s, which):
        at = span(place_of(which, s, 0), rows)
        return spread(at, hop_send.at[s], hop_recv.at[s], partner)

    started = []

    def start(made):
        made.start()
        started.append(made)

    def stage_pair(s):
        swap(s).wait_recv()
        at = span(s * rows, rows)
        own = grads[span(core * half + s * rows, rows), :]
        pair[at, :] = (own.astype(F32) + near[at, :].astype(F32)).astype(BF)
        for place in spots:
            start(to_plane(s, place, spot))

    def stage_plane(s):
        total = pair[span(s * rows + spot * rows_p, rows_p), :].astype(F32)
        for place in spots:
            to_plane(s, place, place).wait_recv()
            total += plane_land[span(s * rows + place * rows_p, rows_p), :].astype(F32)
        plane_sum[span(s * rows_p, rows_p), :] = total.astype(BF)
        for place in fars:
            start(to_far(s, place, far))

    def stage_line(s):
        total = plane_sum[span(s * rows_p + far * rows_z, rows_z), :].astype(F32)
        for place in fars:
            to_far(s, place, place).wait_recv()
            total += line_land[span(s * rows_p + place * rows_z, rows_z), :].astype(F32)
        result[span(place_of(core, s, spot, far), rows_z), :] = (total * factor).astype(BF)
        for place in fars:
            start(back_far(s, place, far))

    def stage_back_line(s):
        for place in fars:
            back_far(s, place, place).wait_recv()
        for place in spots:
            start(back_plane(s, place, spot))

    def stage_back_plane(s):
        for place in spots:
            back_plane(s, place, place).wait_recv()
        start(hop(s, core))

    early = strands // 2
    steps[0]()
    for s in range(early):
        start(swap(s))
    steps[1]()
    for s in range(early):
        stage_pair(s)
    steps[2]()
    for s in range(early, strands):
        start(swap(s))
    steps[3]()
    for s in range(early, strands):
        stage_pair(s)
    stages = [stage_plane, stage_line, stage_back_line, stage_back_plane]
    for step in range(strands + len(stages) - 1):
        for number, stage in enumerate(stages):
            if 0 <= step - number < strands:
                stage(step - number)
    leaving = []
    for s in range(strands):
        hop(s, 1 - core).wait_recv()
        for which in range(2):
            at = pl.ds(which * half + s * rows, rows)
            leaving.append(
                pltpu.make_async_copy(result.at[at], r.result_out.at[at], r.result_sems.at[s, which])
            )
            leaving[-1].start()
    for made in started:
        made.wait_send()
    for copy in leaving:
        copy.wait()


def gather_blocks(
    line,
    side,
    subs,
    own,
    whole,
    recv,
    hop_recv,
    line_send,
    first_send,
    second_send,
    hop_send,
    own_sem,
    prepare,
    idle,
    arrived,
):
    me = lax.axis_index("node")
    core = lax.rem(me, 2)
    chip = me // 2
    partner = me + 1 - 2 * core
    low, mid, far = lax.rem(chip, side), lax.rem(chip // side, side), chip // (side * side)
    first = (1 - core) * low + core * mid
    second = (1 - core) * mid + core * low
    first_stride = 1 + core * (side - 1)
    second_stride = side - core * (side - 1)
    plane = side * side
    rows = own.shape[0]
    size = rows // subs
    mesh_id = pl.DeviceIdType.MESH

    def chip_of(place, over, across):
        return (
            place * plane
            + lax.rem(first + over, side) * first_stride
            + lax.rem(second + across, side) * second_stride
        )

    first_peers = [2 * chip_of(far, step, 0) + core for step in range(1, side)]
    second_peers = [2 * chip_of(far, 0, step) + core for step in range(1, side)]

    def at(source, part, kind):
        return pl.ds(pl.multiple_of((2 * source + kind) * rows + part * size, 16), size)

    def piece(source, part, kind, mine):
        return own.at[pl.ds(part * size, size)] if mine else whole.at[at(source, part, kind)]

    def copy(source, part, mine, send_sem, device):
        return pltpu.make_async_remote_copy(
            src_ref=piece(source, part, core, mine),
            dst_ref=whole.at[at(source, part, core)],
            send_sem=send_sem,
            recv_sem=recv.at[source * subs + part],
            device_id=(device,),
            device_id_type=mesh_id,
        )

    def hop(source, part, mine, kind):
        return pltpu.make_async_remote_copy(
            src_ref=piece(source, part, kind, mine),
            dst_ref=whole.at[at(source, part, kind)],
            send_sem=hop_send.at[source * subs + part],
            recv_sem=hop_recv.at[source * subs + part],
            device_id=(partner,),
            device_id_type=mesh_id,
        )

    def along(place, part, mine, way):
        return copy(
            chip_of(place, 0, 0),
            part,
            mine,
            line_send.at[place * subs + part, way],
            me + (1 - 2 * way) * 2 * plane,
        )

    def over_first(place, part, mine, to):
        return copy(
            chip_of(place, 0, 0), part, mine, first_send.at[place * subs + part, to], first_peers[to]
        )

    def over_second(place, over, part, mine, to):
        return copy(
            chip_of(place, over, 0),
            part,
            mine,
            second_send.at[place * subs + part, over, to],
            second_peers[to],
        )

    def landed(source, part):
        copy(source, part, False, hop_send.at[0], partner).wait_recv()

    def settle(source, part, kind):
        if arrived is not None:
            start = pl.multiple_of((2 * source + kind) * rows + part * size, 16)
            arrived(whole, start, start, size)

    stay = None
    if arrived is None:
        mine_at = pl.ds(pl.multiple_of(me * rows, 16), rows)
        stay = pltpu.make_async_copy(own, whole.at[mine_at], own_sem)

    def arrive(place, part, mine, ways):
        source = chip_of(place, 0, 0)
        if mine:
            prepare(part)
        else:
            landed(source, part)
        for way in ways:
            open_end = far < line - 1 if way == 0 else far > 0

            @pl.when(open_end)
            def _(way=way):
                along(place, part, mine, way).start()

        for to in range(side - 1):
            over_first(place, part, mine, to).start()
        for to in range(side - 1):
            over_second(place, 0, part, mine, to).start()
        hop(source, part, mine, core).start()
        if not mine:
            settle(source, part, core)
        elif arrived is not None:
            arrived(own, part * size, pl.multiple_of(me * rows + part * size, 16), size)
        if mine and part == subs - 1:
            if stay is not None:
                stay.start()
            idle()

    def pass_on(place, part):
        for over in range(1, side):
            source = chip_of(place, over, 0)
            landed(source, part)
            for to in range(side - 1):
                over_second(place, over, part, False, to).start()
            hop(source, part, False, core).start()
            settle(source, part, core)

    def finish(place, part):
        for across in range(1, side):
            for over in range(side):
                source = chip_of(place, over, across)
                landed(source, part)
                hop(source, part, False, core).start()
                settle(source, part, core)

    def receive_hops(place, part):
        for over in range(side):
            for across in range(side):
                source = chip_of(place, over, across)
                hop(source, part, False, 1 - core).wait_recv()
                settle(source, part, 1 - core)

    units = [(0, 0)] + [(reach, way) for reach in range(1, line) for way in range(2)]
    work = [(reach, way, part) for reach, way in units for part in range(subs)]

    def run(item, stage):
        reach, way, part = item
        place = far - reach if way == 0 else far + reach

        def body():
            if stage == 0:
                arrive(place, part, reach == 0, (0, 1) if reach == 0 else (way,))
            elif stage == 1:
                pass_on(place, part)
            elif stage == 2:
                finish(place, part)
            else:
                receive_hops(place, part)

        if reach == 0:
            body()
        else:
            pl.when(place >= 0 if way == 0 else place < line)(body)

    lags = (0, 4, 8, 10)
    for step in range(len(work) + lags[-1]):
        for stage, lag in enumerate(lags):
            if 0 <= step - lag < len(work):
                run(work[step - lag], stage)
    if stay is not None:
        stay.wait()

    def drain(place, carry):
        for part in range(subs):
            for to in range(side - 1):
                over_first(place, part, False, to).wait_send()
                for over in range(side):
                    over_second(place, over, part, False, to).wait_send()

            @pl.when((place <= far) & (far < line - 1))
            def _(part=part):
                along(place, part, False, 0).wait_send()

            @pl.when((place >= far) & (far > 0))
            def _(part=part):
                along(place, part, False, 1).wait_send()

            for over in range(side):
                for across in range(side):
                    hop(chip_of(place, over, across), part, False, core).wait_send()
        return carry

    lax.fori_loop(0, line, drain, 0)


def front_phase(devices, slots, line, side, subs, r, idle, late_idle, arrived):
    me = lax.axis_index("node")
    (node, bucket, feats, memory) = (r.node, r.bucket, r.feats, r.memory)
    (outgoing, inbox, sel, meta, hidden) = (r.outgoing, r.inbox, r.sel, r.meta, r.hidden)
    (picked, picked_meta, totals, counts) = (r.picked, r.picked_meta, r.totals, r.counts)
    (send_sems, recv_sems) = (r.send_sems, r.recv_sems)
    events = feats.shape[0]
    rows, columns = memory.shape
    stride = columns // LANES
    batch = 4
    mesh_id = pl.DeviceIdType.MESH
    barrier = pltpu.get_barrier_semaphore()

    def greet(step, carry):
        pl.semaphore_signal(
            barrier, inc=1, device_id=(lax.rem(me + step, devices),), device_id_type=mesh_id
        )
        return carry

    lax.fori_loop(1, devices, greet, 0)

    ids = lax.broadcasted_iota(jnp.int32, (devices, events), 0) * rows
    names = node[...]
    theirs = (names >= ids) & (names < ids + rows)
    before = lax.broadcasted_iota(jnp.int32, (events, events), 0) < lax.broadcasted_iota(
        jnp.int32, (events, events), 1
    )
    rank = mm(theirs.astype(F32).astype(BF), before.astype(F32).astype(BF))
    sel[...] = jnp.where(theirs, rank, -1.0)
    within = jnp.sum(jnp.where(theirs, names - ids, 0).astype(F32), axis=0, keepdims=True)
    kind = lax.broadcasted_iota(jnp.int32, (16, events), 0)
    meta[...] = jnp.where(
        kind == 0,
        within,
        jnp.where(kind == 1, bucket[...].astype(F32), jnp.where(kind == 2, 1.0, 0.0)),
    ).astype(BF)
    slot_ids = lax.broadcasted_iota(jnp.int32, (slots, events), 0).astype(F32)
    lane_ids = lax.broadcasted_iota(jnp.int32, (LANES, events), 0).astype(F32)
    pl.semaphore_wait(barrier, devices - 1)

    def send(peer):
        return pltpu.make_async_remote_copy(
            src_ref=outgoing.at[peer],
            dst_ref=inbox.at[me],
            send_sem=send_sems.at[peer],
            recv_sem=recv_sems.at[me],
            device_id=(peer,),
            device_id_type=mesh_id,
        )

    def receive(peer):
        return pltpu.make_async_remote_copy(
            src_ref=outgoing.at[peer],
            dst_ref=inbox.at[peer],
            send_sem=send_sems.at[peer],
            recv_sem=recv_sems.at[peer],
            device_id=(peer,),
            device_id_type=mesh_id,
        )

    def pack_batch(step, own):
        peers = [lax.rem(me + step * batch + part, devices) for part in range(batch)]
        picks = [sel[pl.ds(peer, 1), :] for peer in peers]
        hits = jnp.concatenate([(slot_ids == row).astype(F32) for row in picks], axis=0)
        turned = jnp.concatenate([(lane_ids == row).astype(F32) for row in picks], axis=0)
        rows_of = mm(hits.astype(BF), feats[...]).astype(BF)
        info = mm_nt(meta[...], turned.astype(BF)).astype(BF)
        for part, peer in enumerate(peers):
            lines = slice(part * slots, (part + 1) * slots)
            lanes = slice(part * LANES, (part + 1) * LANES)
            if own and part == 0:
                inbox[me, :slots, :] = rows_of[lines, :]
                inbox[me, slots:, :] = info[:, lanes]
            else:
                outgoing[peer, :slots, :] = rows_of[lines, :]
                outgoing[peer, slots:, :] = info[:, lanes]
                send(peer).start()

    pack_batch(0, True)

    def pack_rest(step, carry):
        pack_batch(step, False)
        return carry

    lax.fori_loop(1, devices // batch, pack_rest, 0)

    r.need("hidden_weight")
    previous = memory[...]
    for part in range(3):
        cut = slice(part * columns, (part + 1) * columns)
        hidden[:, cut] = mm(previous, r.hidden_weight[:, cut])
    idle()
    totals[...] = jnp.zeros_like(totals)
    counts[...] = jnp.zeros_like(counts)
    high, low = halves(r.time_message[...])
    weight = r.edge_weight[...]
    turn = (
        lax.broadcasted_iota(jnp.int32, (slots, LANES), 0)
        == lax.broadcasted_iota(jnp.int32, (slots, LANES), 1)
    ).astype(F32).astype(BF)
    chunk = batch * slots

    def add_batch(step, own):
        for part in range(batch):
            peer = lax.rem(me + devices - step * batch - part, devices)
            if not (own and part == 0):
                receive(peer).wait_recv()
            at = slice(part * slots, (part + 1) * slots)
            picked[at, :] = inbox[peer, :slots, :]
            picked_meta[at, :] = mm_nt(turn, inbox[peer, slots:, :])
        info = picked_meta[...]
        place, when, valid = info[:, 0:1], info[:, 1:2], info[:, 2:3]
        lanes = lax.broadcasted_iota(jnp.int32, (chunk, high.shape[0]), 1).astype(F32)
        picks = (lanes == when).astype(F32).astype(BF)
        pre = mm(picked[...], weight) + mm(picks, high) + mm(picks, low)
        message = (pre / (1.0 + jnp.exp(-pre))).astype(BF)
        node_ids = lax.broadcasted_iota(jnp.int32, (chunk, rows), 1).astype(F32)
        marks = jnp.where(node_ids == place, valid, 0.0).astype(BF)
        totals[...] += mm_tn(marks, message)
        counts[...] += mm_tn(marks, jnp.ones((chunk, LANES), BF))

    add_batch(0, True)

    def add_rest(step, carry):
        add_batch(step, False)
        return carry

    lax.fori_loop(1, devices // batch, add_rest, 0)

    r.need("input_weight")

    def prepare(part):
        size = rows // subs
        at = slice(part * size, (part + 1) * size)
        count = counts[at, 0:1]
        aggregate = (totals[at, :] / jnp.maximum(count, 1.0)).astype(BF)

        def gate(which):
            cut = slice(which * columns, (which + 1) * columns)
            bias = jnp.concatenate(
                [r.gate_bias[which * stride + p : which * stride + p + 1, :] for p in range(stride)],
                axis=1,
            )
            return mm(aggregate, r.input_weight[:, cut]) + bias, hidden[at, cut]

        from_input, from_hidden = gate(0)
        update = jax.nn.sigmoid(from_input + from_hidden)
        from_input, from_hidden = gate(1)
        resets = jax.nn.sigmoid(from_input + from_hidden)
        from_input, from_hidden = gate(2)
        candidate = jnp.tanh(from_input + resets * from_hidden)
        old = memory[at, :].astype(F32)
        fresh = (1.0 - update) * candidate + update * old
        fresh = jnp.where(count > 0, fresh, old)
        r.out_memory[at, :] = fresh.astype(BF)
        first = part * size * stride
        for p in range(stride):
            r.wide[pl.ds(first + p, size, stride=stride), :] = fresh[:, p * LANES : (p + 1) * LANES]
        at = slice(first, first + size * stride)
        r.own_table[at, :] = r.wide[at, :].astype(BF)
        if part == subs - 1:
            r.leave("out_memory")

    gather_blocks(
        line,
        side,
        subs,
        r.own_table,
        r.whole,
        r.gather_recv,
        r.gather_hop_recv,
        r.gather_line_send,
        r.gather_first_send,
        r.gather_second_send,
        r.gather_hop_send,
        r.gather_own,
        prepare,
        late_idle,
        arrived,
    )

    def drain(step, carry):
        send(lax.rem(me + step, devices)).wait_send()
        return carry

    lax.fori_loop(1, devices, drain, 0)


def keep(blocks, tall, dest, kind, values):
    upper, lower = halves(values)
    for b in range(blocks):
        rows = slice(b * GROUP, (b + 1) * GROUP)
        first = b * tall + kind * GROUP
        dest[first : first + GROUP, :] = upper[rows, :]
        first += 2 * HEADS * GROUP
        dest[first : first + GROUP, :] = lower[rows, :]


def head_cuts(columns):
    head = columns // HEADS
    return [slice(h * head, (h + 1) * head) for h in range(HEADS)]


def early_products(r):
    events, columns = r.back.shape
    blocks = events // GROUP
    tall = 4 * HEADS * GROUP
    r.need("upstream")
    r.need("out_weight")
    r.need("value_weight")
    r.back[...] = mm_nt(r.upstream[...], r.out_weight[...]).astype(BF)
    for h, cut in enumerate(head_cuts(columns)):
        keep(blocks, tall, r.pull, HEADS + h, mm_nt(r.back[:, cut], r.value_weight[:, cut]))
        keep(blocks, tall, r.pull_time, HEADS + h, jnp.zeros((events, LANES), F32))


def early_marks(r):
    fanout, events = r.buckets.shape
    blocks = events // GROUP
    wide = fanout * GROUP
    even = (
        lax.broadcasted_iota(jnp.int32, (fanout, LANES), 0)
        == lax.broadcasted_iota(jnp.int32, (fanout, LANES), 1)
    ).astype(F32).astype(BF)
    r.names[...] = mm_tn(r.buckets[...].astype(F32).astype(BF), even)
    r.logits[...] = jnp.zeros_like(r.logits)
    r.logits[:fanout, :] = r.affinity[...]
    lane_names = lax.broadcasted_iota(jnp.int32, (GROUP, LANES), 1).astype(F32)

    def mark(b, carry):
        mine = r.names[pl.ds(pl.multiple_of(b * GROUP, GROUP), GROUP), :]
        for j in range(fanout):
            at = pl.ds(pl.multiple_of(b * wide + j * GROUP, GROUP), GROUP)
            r.hot[at, :] = (lane_names == mine[:, j : j + 1]).astype(F32).astype(BF)
        return carry

    lax.fori_loop(0, blocks, mark, 0)


def event_phase(r, fetch_targets, fetch_block):
    events, columns = r.back.shape
    fanout = r.buckets.shape[0]
    head = columns // HEADS
    stride = columns // LANES
    kinds = 2 * HEADS
    blocks = events // GROUP
    wide = fanout * GROUP
    tall = 2 * kinds * GROUP
    rows_all = fanout * events
    heads = head_cuts(columns)
    (target, query, pull, pull_time) = (r.target, r.query, r.pull, r.pull_time)
    (mix, hits, scores, close, hot, logits) = (r.mix, r.hits, r.scores, r.close, r.hot, r.logits)
    high, low = halves(r.time_key[...])
    lane = lax.broadcasted_iota(jnp.int32, (GROUP, LANES), 1)

    fetch_targets()
    fetch_block(0, r.near[0])
    for part in range(stride):
        target[:, part * LANES : (part + 1) * LANES] = r.own_near[
            pl.ds(part, events, stride=stride), :
        ].astype(BF)
    r.need("query_weight")
    r.need("key_weight")
    query[...] = mm(target[...], r.query_weight[...]).astype(BF)
    for h, cut in enumerate(heads):
        keep(blocks, tall, pull, h, mm_nt(query[:, cut], r.key_weight[:, cut]))
        keep(
            blocks,
            tall,
            pull_time,
            h,
            mm_nt(query[:, cut], high[:, cut]) + mm_nt(query[:, cut], low[:, cut]),
        )

    scale = 1.0 / math.sqrt(head)
    pad = scores.shape[0] // blocks
    own = lax.rem(lane, GROUP) == lax.broadcasted_iota(jnp.int32, (GROUP, LANES), 0)
    row_ids = lax.broadcasted_iota(jnp.int32, (pad, LANES), 0)
    lane_ids = lax.broadcasted_iota(jnp.int32, (pad, LANES), 1)
    forward = lane_ids < HEADS * GROUP
    per_row = LANES // GROUP

    def close_rows(b):
        return jnp.concatenate(
            [
                close[pl.ds(pl.multiple_of(part * rows_all + b * wide, GROUP), wide), :]
                for part in range(stride)
            ],
            axis=1,
        )

    def score(b, near):
        for part in range(stride):
            at = pl.ds(pl.multiple_of(part * rows_all + b * wide, GROUP), wide)
            close[at, :] = near[pl.ds(part, wide, stride=stride), :].astype(BF)
        at = pl.ds(pl.multiple_of(b * wide, GROUP), wide)
        from_at = pl.ds(pl.multiple_of(b * tall, GROUP), tall)
        both = mm_nt(close_rows(b), pull[from_at, :]) + mm_nt(hot[at, :], pull_time[from_at, :])
        both = both[:, :LANES] + both[:, LANES:]
        raw = jnp.zeros((pad, LANES), F32)
        for j in range(fanout):
            line = jnp.where(own, both[j * GROUP : (j + 1) * GROUP, :], 0.0)
            raw = jnp.where(row_ids == j, jnp.sum(line, axis=0, keepdims=True), raw)
        chunk = pl.multiple_of(b // per_row * LANES, LANES)
        piece = logits[:, pl.ds(chunk, LANES)]
        piece = pltpu.roll(piece, lax.rem(LANES - lax.rem(b, per_row) * GROUP, LANES), axis=1)
        given = piece
        for h in range(1, HEADS):
            moved = pltpu.roll(piece, h * GROUP, axis=1)
            given = jnp.where(lane_ids >= h * GROUP, moved, given)
        scores[pl.ds(pl.multiple_of(b * pad, pad), pad), :] = jnp.where(
            forward, raw * scale + given, raw
        )

    def score_four(b, more):
        for place in range(4):
            if more or place < 3:
                fetch_block(b + place + 1, r.near[(place + 1) % 2])
            score(b + place, r.near[place % 2])

    def score_step(step, carry):
        score_four(step * 4, True)
        return carry

    lax.fori_loop(0, blocks // 4 - 1, score_step, 0)
    score_four(blocks - 4, False)

    for b in range(blocks):
        at = slice(b * pad, (b + 1) * pad)
        here = scores[at, :]
        active = row_ids < fanout
        top = jnp.max(jnp.where(active, here, -3.0e38), axis=0, keepdims=True)
        raised = jnp.where(active, jnp.exp(jnp.where(active, here - top, 0.0)), 0.0)
        probs = raised / jnp.sum(raised, axis=0, keepdims=True)
        slopes = pltpu.roll(here, HEADS * GROUP, axis=1).astype(BF).astype(F32)
        inner = jnp.sum(probs * slopes, axis=0, keepdims=True)
        slopes = probs * (slopes - inner) * scale
        scores[at, :] = jnp.where(forward, probs, pltpu.roll(slopes, HEADS * GROUP, axis=1))

    def blend(b):
        weights = scores[pl.ds(pl.multiple_of(b * pad, pad), pad), :]
        spread = jnp.concatenate(
            [
                jnp.where(own, jnp.broadcast_to(weights[j : j + 1, :], (GROUP, LANES)), 0.0)
                for j in range(fanout)
            ],
            axis=0,
        ).astype(BF)
        at = pl.ds(pl.multiple_of(b * wide, GROUP), wide)
        mixed = mm_tn(spread, close_rows(b)).astype(BF)
        times = mm_tn(spread, hot[at, :]).astype(BF)
        to = pl.ds(pl.multiple_of(b * GROUP, GROUP), GROUP)
        for k in range(kinds):
            mix[k, to, :] = mixed[k * GROUP : (k + 1) * GROUP, :]
        for h in range(HEADS):
            hits[h, to, :] = times[(HEADS + h) * GROUP : (HEADS + h + 1) * GROUP, :]

    def blend_eight(step, carry):
        for place in range(8):
            blend(step * 8 + place)
        return carry

    lax.fori_loop(0, blocks // 8, blend_eight, 0)


def gradient_steps(r):
    (target, query, back, mix, hits, grads) = (r.target, r.query, r.back, r.mix, r.hits, r.grads)
    events, columns = back.shape
    heads = head_cuts(columns)
    high, low = halves(r.time_key[...])

    def value_and_key():
        for h, cut in enumerate(heads):
            grads[2 * columns : 3 * columns, cut] = mm_tn(mix[h], back[:, cut]).astype(BF)
            grads[:columns, cut] = mm_tn(mix[HEADS + h], query[:, cut]).astype(BF)

    def cotangents():
        for h, cut in enumerate(heads):
            back[:, cut] = mm(mix[h], r.value_weight[:, cut]).astype(BF)
            query[:, cut] = (
                mm(mix[HEADS + h], r.key_weight[:, cut])
                + mm(hits[h], high[:, cut])
                + mm(hits[h], low[:, cut])
            ).astype(BF)

    def query_and_out():
        grads[columns : 2 * columns, :] = mm_tn(target[...], query[...]).astype(BF)
        grads[3 * columns :, :] = mm_tn(back[...], r.upstream[...]).astype(BF)

    def embed():
        r.embedding[...] = (mm(back[...], r.out_weight[...]) + target[...].astype(F32)).astype(BF)
        r.leave("embedding")

    return value_and_key, cotangents, query_and_out, embed


class Refs:
    def __init__(self, names, refs, staged):
        for name, ref in zip(names, refs, strict=True):
            setattr(self, name, ref)
        self.copies = {}
        self.leaving = []
        for place, name in enumerate(staged):
            copy = pltpu.make_async_copy(
                getattr(self, name), getattr(self, name + "_here"), self.stage_sems.at[place]
            )
            copy.start()
            self.copies[name] = copy
            setattr(self, name, getattr(self, name + "_here"))
        if hasattr(self, "near_first"):
            self.near = (self.near_first, self.near_second)
        if hasattr(self, "grads"):
            self.out_sems = [getattr(self, name) for name in OUT_SEMS]
            self.back_sems = [getattr(self, name) for name in BACK_SEMS]

    def leave(self, name):
        copy = pltpu.make_async_copy(
            getattr(self, name), getattr(self, name + "_out"), getattr(self, name + "_sem")
        )
        copy.start()
        self.leaving.append(copy)

    def finish(self):
        for copy in self.leaving:
            copy.wait()

    def need(self, name):
        copy = self.copies.pop(name, None)
        if copy is not None:
            copy.wait()


OUT_SEMS = [f"out{place}" for place in range(6)]
BACK_SEMS = [f"back{place}" for place in range(6)]
FRONT_STAGED = ("hidden_weight", "input_weight")
EVENT_STAGED = ("upstream", "out_weight", "value_weight", "query_weight", "key_weight")


def front_kernel(sizes, names, *refs):
    r = Refs(names, refs, FRONT_STAGED)
    front_phase(*sizes, r, lambda: None, lambda: None, None)
    r.finish()


def fetch_kernel(ids, own_ids, source, dest, sem):
    fanout, events = ids.shape
    stride = dest.shape[0] // ((fanout + 1) * events)
    wide = fanout * GROUP

    def request(start, row):
        pltpu.make_async_copy(
            source.at[pl.ds(pl.multiple_of(start * stride, stride), stride)],
            dest.at[pl.ds(pl.multiple_of(row * stride, stride), stride)],
            sem,
        ).start()

    def request_all(e, carry):
        for j in range(fanout):
            request(ids[j, e], e // GROUP * wide + j * GROUP + e % GROUP)
        request(own_ids[e], fanout * events + e)
        return carry

    lax.fori_loop(0, events, request_all, 0)
    pltpu.make_async_copy(source.at[pl.ds(0, dest.shape[0])], dest, sem).wait()


def event_kernel(reduce_sizes, names, *refs):
    r = Refs(names, refs, EVENT_STAGED)
    fanout, events = r.buckets.shape
    block_rows = r.near_first.shape[0]
    early_products(r)
    early_marks(r)

    def fetch_targets():
        copy = pltpu.make_async_copy(
            r.rows.at[pl.ds(events // GROUP * block_rows, r.own_near.shape[0])],
            r.own_near,
            r.fetch_sem,
        )
        copy.start()
        copy.wait()

    def fetch_block(b, near):
        first = pl.multiple_of(b * block_rows, block_rows)
        copy = pltpu.make_async_copy(r.rows.at[pl.ds(first, block_rows)], near, r.fetch_sem)
        copy.start()
        copy.wait()

    event_phase(r, fetch_targets, fetch_block)
    reduce_phase(*reduce_sizes, r, True, gradient_steps(r))
    r.finish()


def whole_kernel(front_sizes, reduce_sizes, names, *refs):
    r = Refs(names, refs, FRONT_STAGED + EVENT_STAGED)
    fanout, events = r.buckets.shape
    stride = r.own_near.shape[0] // events
    table = r.table
    r.close = r.whole

    def arrived(source, first, start, size):
        step_rows = 128

        def widen(step, carry):
            from_at = pl.ds(pl.multiple_of(first + step * step_rows, 16), step_rows)
            to_at = pl.ds((start + step * step_rows) // stride, step_rows // stride)
            rows = source[from_at, :].astype(F32)
            table[to_at] = rows.reshape(step_rows // stride, stride, LANES)
            return carry

        lax.fori_loop(0, size // step_rows, widen, 0)

    front_phase(*front_sizes, r, lambda: early_products(r), lambda: early_marks(r), arrived)

    def move(start, dest, row):
        dest[pl.ds(pl.multiple_of(row * stride, stride), stride), :] = table[start]

    def fetch_targets():
        unroll = 16

        def some(step, carry):
            for place in range(unroll):
                e = step * unroll + place
                move(r.own_ids[e], r.own_near, e)
            return carry

        lax.fori_loop(0, events // unroll, some, 0)

    def fetch_block(b, near):
        for e in range(GROUP):
            for j in range(fanout):
                move(r.ids[j, b * GROUP + e], near, j * GROUP + e)

    event_phase(r, fetch_targets, fetch_block)
    reduce_phase(*reduce_sizes, r, False, gradient_steps(r))
    r.finish()


def finish_kernel(order, total, embedding, memory, *rest):
    outs, (here, wide, *passing, read_sems, write_sems, in_sems, out_sems) = rest[:6], rest[6:]
    grads, kept = outs[:4], outs[4:]
    columns = grads[0].shape[0]
    per = read_sems.shape[0] // 4
    size = columns // per
    reads, writes, enter = [], [], []
    for place in range(4 * per):
        at = pl.ds(place * size, size)
        reads.append(pltpu.make_async_copy(total.at[at], here.at[at], read_sems.at[place]))
        reads[-1].start()
    for place, source in enumerate((embedding, memory)):
        enter.append(pltpu.make_async_copy(source, passing[place], in_sems.at[place]))
        enter[-1].start()
    for place in range(4 * per):
        at = pl.ds(place * size, size)
        reads[place].wait()
        wide[at, :] = here[at, :].astype(F32)
        to = grads[order[place // per]].at[pl.ds(place % per * size, size)]
        writes.append(pltpu.make_async_copy(wide.at[at], to, write_sems.at[place]))
        writes[-1].start()
    for place in range(2):
        enter[place].wait()
        writes.append(pltpu.make_async_copy(passing[place], kept[place], out_sems.at[place]))
        writes[-1].start()
    for copy in writes:
        copy.wait()


def shards(
    event_node,
    neighbours,
    event_bucket,
    neighbour_bucket,
    edge_features,
    affinity,
    upstream,
    node_memory,
    edge_weight,
    time_message,
    input_weight,
    hidden_weight,
    gate_bias,
    time_key,
    query_weight,
    key_weight,
    value_weight,
    out_weight,
):
    devices = lax.axis_size("node")
    node_rows, columns = node_memory.shape
    events, fanout = neighbours.shape
    features = edge_features.shape[1]
    stride = columns // LANES
    slots = -(-(3 * events // devices) // 16) * 16
    chips = devices // 2
    side = max(s for s in range(1, chips + 1) if chips % (s * s) == 0 and s**3 <= chips)
    line = chips // (side * side)
    subs = 2
    half = 2 * columns
    strands = max(1, min(4, half // (16 * chips)))
    factor = 1.0 / math.sqrt(events * devices)
    front_sizes = (devices, slots, line, side, subs)
    reduce_sizes = (line, side, strands, factor)
    table_rows = devices * node_rows * stride
    close_rows = fanout * events * stride
    resident = table_rows * LANES * 4 <= RESIDENT_LIMIT
    vmem = pl.BlockSpec(memory_space=pltpu.VMEM)
    smem = pl.BlockSpec(memory_space=pltpu.SMEM)
    hbm = pl.BlockSpec(memory_space=pl.ANY)
    dma = pltpu.SemaphoreType.DMA

    def buffer(rows, width, dtype=BF):
        return pltpu.VMEM((rows, width), dtype)

    front_in = {
        "node": (event_node.reshape(1, events), vmem),
        "bucket": (event_bucket.reshape(1, events), vmem),
        "feats": (edge_features, vmem),
        "memory": (node_memory, vmem),
        "edge_weight": (edge_weight, vmem),
        "time_message": (time_message, vmem),
        "input_weight": (input_weight, hbm),
        "hidden_weight": (hidden_weight, hbm),
        "gate_bias": (gate_bias.reshape(-1, LANES), vmem),
    }
    event_in = {
        "buckets": (neighbour_bucket.T, vmem),
        "affinity": (affinity.T, vmem),
        "upstream": (upstream, hbm),
        "time_key": (time_key, vmem),
        "query_weight": (query_weight, hbm),
        "key_weight": (key_weight, hbm),
        "value_weight": (value_weight, hbm),
        "out_weight": (out_weight, hbm),
    }
    index_in = {"ids": (neighbours.T, smem), "own_ids": (event_node, smem)}
    memory_out = {"out_memory_out": (jax.ShapeDtypeStruct((node_rows, columns), BF), hbm)}
    event_out = {
        "embedding_out": (jax.ShapeDtypeStruct((events, columns), BF), hbm),
        "result_out": (jax.ShapeDtypeStruct((2 * half, columns), BF), hbm),
    }
    front_scratch = {
        "outgoing": pltpu.VMEM((devices, slots + 16, features), BF),
        "inbox": pltpu.VMEM((devices, slots + 16, features), BF),
        "sel": buffer(devices, events, F32),
        "meta": buffer(16, events),
        "hidden": buffer(node_rows, 3 * columns, F32),
        "picked": buffer(4 * slots, features),
        "picked_meta": buffer(4 * slots, 16, F32),
        "totals": buffer(node_rows, columns, F32),
        "counts": buffer(node_rows, LANES, F32),
        "wide": buffer(node_rows * stride, LANES, F32),
        "own_table": buffer(node_rows * stride, LANES),
        "send_sems": dma((devices,)),
        "recv_sems": dma((devices,)),
        "gather_recv": dma((chips * subs,)),
        "gather_hop_recv": dma((chips * subs,)),
        "gather_line_send": dma((line * subs, 2)),
        "gather_first_send": dma((line * subs, side - 1)),
        "gather_second_send": dma((line * subs, side, side - 1)),
        "gather_hop_send": dma((chips * subs,)),
        "gather_own": dma,
        "out_memory": buffer(node_rows, columns),
        "out_memory_sem": dma,
    }
    event_scratch = {
        "target": buffer(events, columns),
        "query": buffer(events, columns),
        "back": buffer(events, columns),
        "pull": buffer(4 * HEADS * events, columns),
        "pull_time": buffer(4 * HEADS * events, LANES),
        "mix": pltpu.VMEM((2 * HEADS, events, columns), BF),
        "hits": pltpu.VMEM((HEADS, events, LANES), BF),
        "scores": buffer(events // GROUP * 16, LANES, F32),
        "hot": buffer(fanout * events, LANES),
        "names": buffer(events, LANES, F32),
        "logits": buffer(16, events, F32),
        "own_near": buffer(events * stride, LANES, F32),
        "near_first": buffer(fanout * GROUP * stride, LANES, F32),
        "near_second": buffer(fanout * GROUP * stride, LANES, F32),
        "grads": buffer(2 * half, columns),
        "swapped": buffer(half, columns),
        "pair": buffer(half, columns),
        "plane_land": buffer(half, columns),
        "plane_sum": buffer(half // (side * side), columns),
        "line_land": buffer(half // (side * side), columns),
        "embedding": buffer(events, columns),
        "embedding_sem": dma,
        "result": buffer(2 * half, columns),
        "result_sems": dma((strands, 2)),
    }
    plane = side * side
    for name, shape in zip(
        OUT_SEMS + BACK_SEMS,
        [(strands,)] * 2
        + [(strands, plane)] * 2
        + [(strands, line)] * 4
        + [(strands, plane)] * 2
        + [(strands,)] * 2,
    ):
        event_scratch[name] = dma(shape)

    def call(kernel, sizes, name, number, inputs, outputs, scratch, staged):
        scratch = dict(scratch)
        for key in staged:
            array = inputs[key][0]
            scratch[key + "_here"] = pltpu.VMEM(array.shape, array.dtype)
        scratch["stage_sems"] = dma((len(staged),))
        names = list(inputs) + list(outputs) + list(scratch)
        return pl.pallas_call(
            functools.partial(kernel, *sizes, names),
            out_shape=tuple(shape for shape, _ in outputs.values()),
            in_specs=[spec for _, spec in inputs.values()],
            out_specs=tuple(spec for _, spec in outputs.values()),
            scratch_shapes=list(scratch.values()),
            compiler_params=pltpu.CompilerParams(
                collective_id=number, has_side_effects=True, vmem_limit_bytes=VMEM_LIMIT
            ),
            name=name,
        )(*[array for array, _ in inputs.values()])

    if resident:
        new_memory, embedding, total = call(
            whole_kernel,
            (front_sizes, reduce_sizes),
            "whole_step",
            0,
            front_in | event_in | index_in,
            memory_out | event_out,
            front_scratch
            | event_scratch
            | {
                "whole": buffer(max(table_rows, close_rows), LANES),
                "table": pltpu.VMEM((table_rows // stride, stride, LANES), F32),
            },
            FRONT_STAGED + EVENT_STAGED,
        )
    else:
        new_memory, whole = call(
            front_kernel,
            (front_sizes,),
            "front_step",
            0,
            front_in,
            memory_out | {"whole": (jax.ShapeDtypeStruct((table_rows, LANES), BF), hbm)},
            front_scratch,
            FRONT_STAGED,
        )
        rows = pl.pallas_call(
            fetch_kernel,
            out_shape=jax.ShapeDtypeStruct(((fanout + 1) * events * stride, LANES), F32),
            in_specs=[smem, smem, hbm],
            out_specs=hbm,
            scratch_shapes=[dma],
            name="fetch_step",
        )(neighbours.T, event_node, whole.astype(F32))
        embedding, total = call(
            event_kernel,
            (reduce_sizes,),
            "event_step",
            1,
            event_in | {"rows": (rows, hbm)},
            event_out,
            event_scratch | {"close": buffer(close_rows, LANES), "fetch_sem": dma},
            EVENT_STAGED,
        )
    per = 2
    grad_shape = jax.ShapeDtypeStruct((columns, columns), F32)
    *grads, embedding, new_memory = pl.pallas_call(
        functools.partial(finish_kernel, (1, 0, 2, 3)),
        out_shape=(grad_shape,) * 4
        + (
            jax.ShapeDtypeStruct(embedding.shape, BF),
            jax.ShapeDtypeStruct(new_memory.shape, BF),
        ),
        in_specs=[hbm] * 3,
        out_specs=(hbm,) * 6,
        scratch_shapes=[
            buffer(4 * columns, columns),
            buffer(4 * columns, columns, F32),
            buffer(events, columns),
            buffer(node_rows, columns),
            dma((4 * per,)),
            dma((4 * per,)),
            dma((2,)),
            dma((2,)),
        ],
        compiler_params=pltpu.CompilerParams(vmem_limit_bytes=VMEM_LIMIT),
        name="finish_step",
    )(total, embedding, new_memory)
    return (embedding, new_memory) + tuple(grads)


def solution(mesh):
    placed = (
        P("node"),
        P("node", None),
        P("node"),
        P("node", None),
        P("node", None),
        P("node", None),
        P("node", None),
        P("node", None),
        P(),
        P(),
        P(),
        P(),
        P(),
        P(),
        P(),
        P(),
        P(),
        P(),
    )
    return jax.shard_map(
        shards,
        mesh=mesh,
        in_specs=placed,
        out_specs=(P("node", None), P("node", None), P(), P(), P(), P()),
        check_vma=False,
    )
```
